256 devices in a mesh: seq: 16 (over z, core), fsdp: 16 (over x, y).
Axes of the slice: x: 4, y: 4, z: 8, core: 2. Of those that a mesh axis runs over, the one named last changes fastest.
Arguments:
- inputs: bfloat16 [16, 2048, 2304], P('fsdp', 'seq'), may hold values from -6 to 6
- queries: bfloat16 [16, 2048, 2048], P('fsdp', 'seq'), may hold values from -96 to 96
- w_kv: bfloat16 [2304, 2048], P('fsdp'), may hold values from -0.125 to 0.125
- doc_lengths: int32 [16, 8], P('fsdp'), may hold values from 1 to 1536, 2048 in all within a row
- grad_out: bfloat16 [16, 2048, 2048], P('fsdp', 'seq'), may hold values from -6 to 6
Outputs:
- attn_out: bfloat16 [16, 2048, 2048], P('fsdp', 'seq')
- grad_inputs: bfloat16 [16, 2048, 2304], P('fsdp', 'seq')
- grad_weights: float32 [2304, 2048], P('fsdp', 'seq')
The draws below stay inside these ranges and needn't reach their ends.
Inputs may be any that keep to these rules, and one draw needn't show every extreme that they name: `doc_lengths`: each row lists the lengths of the 8 documents packed in order into one sequence; a row sums to 2048 and its longest document has 1536 tokens.
All inputs are finite; a program needn't handle non-finite values.
Results may differ from the reference program's by a relative error of at most 0.03.
Values may be sent and summed in bfloat16 or wider, within the bound.
A program may use at most 128 MiB of HBM per device.

```python
import math
import jax
import jax.numpy as jnp
import numpy as np
from jax import lax

D = 2304
QH = 16
KVH = 8
HD = 128
WIN = 1024
NDOC = 8
TOK_DEV = 128
G = 2
KW = 2048
SEQLEN = 2048
SEQS = 16
MOST = 1536
N_SEQ = 16


def raised(result, stream_key, source, target, shards_of, factor):
    def block_of(axis_at):
        return (jnp.arange(result.shape[axis_at]) // (result.shape[axis_at] // shards_of)).reshape((-1,) + (1,) * (result.ndim - 1 - axis_at))

    first = jax.random.permutation(stream_key, shards_of)[block_of(target)]
    second = (block_of(target) + shards_of // 2) % shards_of
    return jnp.where((block_of(source) == first) | (block_of(source) == second), factor * result, result)


def shard_levels(stream_key, shape, cuts, low, high):
    loudness = 1.0
    for axis_at, parts in cuts:
        draws = jax.random.uniform(jax.random.fold_in(jax.random.fold_in(stream_key, 6), axis_at), (parts,), jnp.float32, low / len(cuts), high / len(cuts))
        loudness = loudness * jnp.repeat(jnp.exp(draws), shape[axis_at] // parts).reshape((-1,) + (1,) * (len(shape) - 1 - axis_at))
    return loudness


def profile(amount, total, limit, skew):
    loads = [(1 << 20) // math.isqrt(grade ** skew) + 1 for grade in range(2, amount + 1)]
    spare, holding = total - limit - (amount - 1), [1] * (amount - 1)
    while spare > 0:
        candidates = [i for i in range(amount - 1) if holding[i] < limit]
        whole, budget = sum([loads[i] for i in candidates]), spare
        for i in candidates:
            addition = min(limit - holding[i], max(1, budget * loads[i] // whole), spare)
            holding[i] = holding[i] + addition
            spare = spare - addition
    return np.array([limit] + holding)


def ragged_sizes(key, number_of, total, bound, lean):
    if number_of == 2:
        one = jax.random.randint(key, (), max(1, total - bound), min(bound, total - 1) + 1)
        return jnp.stack([one, total - one])
    sizes = jnp.asarray(profile(number_of, total, bound, lean), jnp.int32)
    twos = (number_of - 1) // 2
    donor, taker = sizes[1:1 + 2 * twos:2], sizes[2:2 + 2 * twos:2]
    slack = jnp.minimum(donor - 1, bound - taker)
    passed = jax.random.randint(jax.random.fold_in(key, 1), (twos,), 0, 1 << 20) % (slack + 1)
    sizes = sizes.at[1:1 + 2 * twos:2].set(donor - passed).at[2:2 + 2 * twos:2].set(taker + passed)
    return sizes[jax.random.permutation(jax.random.fold_in(key, 2), number_of)]


def scatter_about(stream_key, dims, spread, limit, split=(), kind=jnp.bfloat16):
    level = shard_levels(stream_key, dims, split, -0.22, 0.18) if split else 1.0
    entries = jax.random.normal(stream_key, dims, jnp.float32) * spread * level
    return jnp.minimum(jnp.maximum(entries, -limit), limit).astype(kind)


def gaussian_with(own_key, dims, deviation, bound, shards, heavy, kind=jnp.bfloat16):
    array = deviation * jax.random.normal(own_key, dims, jnp.float32)
    if shards:
        array = array * shard_levels(own_key, dims, shards, -0.22, 0.18)
    return jnp.clip(raised(array, jax.random.fold_in(own_key, 3), *heavy), -bound, bound).astype(kind)


def setup_inputs(seed: int = 0) -> dict:
    keys = jax.random.split(jax.random.key(seed), 6)
    return {
        "inputs": gaussian_with(keys[0], (SEQS, SEQLEN, D), 1.0, 6.0, ((0, 16), (1, 16)), (0, 2, 16, 2.0)),
        "queries": scatter_about(keys[1], (SEQS, SEQLEN, QH * HD), 16.0, 96.0, ((0, 16), (1, 16))),
        "w_kv": scatter_about(keys[2], (D, KW), D ** -0.5, 0.125, ((0, 16),)),
        "doc_lengths": jax.vmap(lambda own: ragged_sizes(own, NDOC, SEQLEN, MOST, 2))(jax.random.split(keys[3], SEQS)).reshape((SEQS, NDOC)).astype(jnp.int32),
        "grad_out": scatter_about(keys[4], (SEQS, SEQLEN, QH * HD), 1.0, 6.0, ((0, 16), (1, 16))),
    }


SOFT_CAP = 50.0
QUERY_SCALE = 1.0 / 12.0
ROPE_BASE = 10000.0


def doc_layout(lengths, places):
    lengths = lengths.astype(jnp.int32)
    doc_ends = jnp.cumsum(lengths).astype(jnp.int32)
    doc_ended = doc_ends[None, :] <= places[:, None]
    doc_index = jnp.sum(doc_ended.astype(jnp.int32), axis=1).astype(jnp.int32)
    before = jnp.sum(jnp.where(doc_ended, lengths[None, :], 0), axis=1).astype(jnp.int32)
    return doc_index, (places - before).astype(jnp.int32)


def rotate(values, places, direction):
    half_dim = values.shape[-1] // 2
    exponent = jnp.arange(half_dim, dtype=jnp.float32) * (2.0 / values.shape[-1])
    inverse_rate = jnp.power(ROPE_BASE, -exponent)
    angles = places.astype(jnp.float32)[:, None] * inverse_rate[None, :]
    cosine = jnp.cos(angles)[:, None, :]
    sine_part = direction * jnp.sin(angles)[:, None, :]
    first_half = values[..., :half_dim]
    second_half = values[..., half_dim:]
    return jnp.concatenate([first_half * cosine - second_half * sine_part, second_half * cosine + first_half * sine_part], axis=-1)


def rounded_copy(values):
    return lax.optimization_barrier(values.astype(jnp.bfloat16)).astype(jnp.float32)


def one_sequence(tokens, query_rows, lengths, cotangent, w_kv):
    half_kv = KVH * HD
    places = jnp.arange(SEQLEN, dtype=jnp.int32)
    doc_index, within = doc_layout(lengths, places)
    projected = jnp.dot(tokens, w_kv, preferred_element_type=jnp.float32)
    key_rows = rotate(projected[:, :half_kv].reshape(SEQLEN, KVH, HD), within, 1.0).reshape(SEQLEN, half_kv).astype(jnp.bfloat16)
    value_rows = projected[:, half_kv:].astype(jnp.bfloat16)
    distance = places[:, None] - places[None, :]
    allowed = (doc_index[:, None] == doc_index[None, :]) & (distance >= 0) & (distance <= WIN - 1)
    owner = (places // TOK_DEV).astype(jnp.int32)
    own_term = jnp.arange(N_SEQ, dtype=jnp.int32)[:, None] == owner[None, :]

    def one_head(head_index):
        q_part = lax.dynamic_slice_in_dim(query_rows, head_index * G * HD, G * HD, 1).reshape(SEQLEN, G, HD).astype(jnp.float32)
        d_part = lax.dynamic_slice_in_dim(cotangent, head_index * G * HD, G * HD, 1).reshape(SEQLEN, G, HD).astype(jnp.float32)
        k_part = lax.dynamic_slice_in_dim(key_rows, head_index * HD, HD, 1).astype(jnp.float32)
        v_part = lax.dynamic_slice_in_dim(value_rows, head_index * HD, HD, 1).astype(jnp.float32)
        scores = jnp.einsum('tgd,nd->gtn', q_part, k_part) * QUERY_SCALE
        squashed = jnp.tanh(scores / SOFT_CAP)
        weights = jnp.where(allowed[None], jnp.exp(SOFT_CAP * squashed), 0.0)
        probs = weights / jnp.sum(weights, axis=-1, keepdims=True)
        rounded = rounded_copy(probs)
        attended = rounded_copy(jnp.einsum('gtn,nd->tgd', rounded, v_part))
        delta_row = jnp.einsum('tgd,tgd->gt', d_part, attended)
        dprob = jnp.einsum('tgd,nd->gtn', d_part, v_part)
        dscore = rounded_copy(probs * (dprob - delta_row[:, :, None]) * (1.0 - squashed * squashed))
        q_shards = q_part.reshape(N_SEQ, TOK_DEV, G, HD)
        d_shards = d_part.reshape(N_SEQ, TOK_DEV, G, HD)
        key_terms = jnp.einsum('gstn,stgd->snd', dscore.reshape(G, N_SEQ, TOK_DEV, SEQLEN), q_shards) * QUERY_SCALE
        value_terms = jnp.einsum('gstn,stgd->snd', rounded.reshape(G, N_SEQ, TOK_DEV, SEQLEN), d_shards)
        key_grad = jnp.sum(jnp.where(own_term[:, :, None], key_terms, rounded_copy(key_terms)), axis=0)
        value_grad = jnp.sum(jnp.where(own_term[:, :, None], value_terms, rounded_copy(value_terms)), axis=0)
        return attended.astype(jnp.bfloat16), key_grad, value_grad

    attended, key_grad, value_grad = lax.map(one_head, jnp.arange(KVH, dtype=jnp.int32))
    out_rows = jnp.transpose(attended, (1, 0, 2, 3)).reshape(SEQLEN, QH * HD)
    key_total = rotate(jnp.transpose(key_grad, (1, 0, 2)), within, -1.0).reshape(SEQLEN, half_kv)
    value_total = jnp.transpose(value_grad, (1, 0, 2)).reshape(SEQLEN, half_kv)
    grad_kv = jnp.concatenate([key_total, value_total], axis=1).astype(jnp.bfloat16)
    grad_rows = jnp.dot(grad_kv, w_kv.T, preferred_element_type=jnp.float32).astype(jnp.bfloat16)
    return out_rows, grad_rows, grad_kv


def reference(inputs, queries, w_kv, doc_lengths, grad_out):
    def per_sequence(operands):
        return one_sequence(operands[0], operands[1], operands[2], operands[3], w_kv)

    attn_out, grad_inputs, grad_kv = lax.map(per_sequence, (inputs, queries, doc_lengths, grad_out))
    token_blocks = inputs.reshape(SEQS * N_SEQ, TOK_DEV, D)
    grad_blocks = grad_kv.reshape(SEQS * N_SEQ, TOK_DEV, KW)

    def accumulate(running, pieces):
        device_term = jnp.dot(pieces[0].T, pieces[1], preferred_element_type=jnp.float32)
        return running + rounded_copy(device_term), None

    grad_weights, ignored = lax.scan(accumulate, jnp.zeros((D, KW), jnp.float32), (token_blocks, grad_blocks))
    return attn_out, grad_inputs, grad_weights
```

```python
import functools

import jax
import jax.numpy as jnp
from jax import lax
from jax.experimental import pallas as pl
from jax.experimental.pallas import tpu as pltpu
from jax.sharding import PartitionSpec as P

D = 2304
HD = 128
WIN = 1024
SEQLEN = 2048
NDOC = 8
NZ = 8
NX = 4
NY = 4
ROWS = D // (NX * NY)
HALF = 1024
PART = 512
TOK = 128
CTOK = 256
CAP = 50.0
SCALE = 1.0 / 12.0
ROPE_BASE = 10000.0
MESH = pl.DeviceIdType.MESH
ANY = pl.BlockSpec(memory_space=pl.ANY)
VM = pl.BlockSpec(memory_space=pltpu.VMEM)
BF = jnp.bfloat16
F32 = jnp.float32


def where_am_i():
    s = lax.axis_index("seq")
    f = lax.axis_index("fsdp")
    z = s // 2
    c = s - 2 * z
    x = f // NY
    y = f - NY * x
    return s, f, z, c, x, y


def ring(v, n):
    return lax.rem(v + n, n)


def remote(src, dst, send, recv, s, f):
    return pltpu.make_async_remote_copy(
        src_ref=src,
        dst_ref=dst,
        send_sem=send,
        recv_sem=recv,
        device_id={"seq": s, "fsdp": f},
        device_id_type=MESH,
    )


def enter(s, f, x, y):
    barrier = pltpu.get_barrier_semaphore()
    for step in range(1, 2 * NZ):
        pl.semaphore_signal(
            barrier,
            inc=1,
            device_id={"seq": ring(s + step, 2 * NZ), "fsdp": f},
            device_id_type=MESH,
        )
    for dx, dy in ((1, 0), (-1, 0), (0, 1), (0, -1)):
        pl.semaphore_signal(
            barrier,
            inc=1,
            device_id={"seq": s, "fsdp": ring(x + dx, NX) * NY + ring(y + dy, NY)},
            device_id_type=MESH,
        )
    pl.semaphore_wait(barrier, 2 * NZ - 1 + 4)


def rotated(values, cosine, sine):
    return values * cosine + pltpu.roll(values, HD // 2, 1) * sine


def k1_kernel(
    x_ref,
    q_ref,
    w_ref,
    g_ref,
    cos_ref,
    sin_ref,
    qh_ref,
    gh_ref,
    kv_ref,
    xt_ref,
    wh_ref,
    wg,
    xs,
    proj,
    wl_sem,
    xl_sem,
    xr_sem,
    ws_sem,
    wr_sem,
    ql_sem,
    qs_sem,
    qr_sem,
    ks_sem,
    kr_sem,
    fs_sem,
    fr_sem,
    o_sem,
):
    s, f, z, c, x, y = where_am_i()
    sib = s + 1 - 2 * c
    own_rows = pl.ds(pl.multiple_of(f * ROWS, 16), ROWS)
    load_w = []
    for k in range(8):
        cols = pl.ds(pl.multiple_of((2 * k + c) * HD, HD), HD)
        load_w.append(
            pltpu.make_async_copy(
                w_ref.at[:, cols], wg.at[own_rows, pl.ds(k * HD, HD)], wl_sem.at[k]
            )
        )
    for copy in load_w:
        copy.start()
    own_tok = pl.ds(pl.multiple_of(c * TOK, TOK), TOK)
    load_x = pltpu.make_async_copy(x_ref, xs.at[own_tok], xl_sem)
    load_x.start()
    enter(s, f, x, y)

    def piece(part, off, half=None):
        origin = ring(x + off[0], NX) * NY + ring(y + off[1], NY)
        rows = pl.ds(pl.multiple_of(origin * ROWS, 16), ROWS)
        if half is None:
            return wg.at[rows, pl.ds(part * PART, PART)]
        return wg.at[rows, pl.ds(part * PART + half * (PART // 2), PART // 2)]

    sends = []

    def pass_on(part, off, step, half=None):
        there = tuple((o - d) % 4 for o, d in zip(off, step))
        there = tuple(-1 if t == 3 else t for t in there)
        ref = piece(part, off, half)
        copy = remote(
            ref,
            ref,
            ws_sem.at[len(sends)],
            wr_sem.at[part, there[0] + 1, there[1] + 1, half or 0],
            s,
            ring(x + step[0], NX) * NY + ring(y + step[1], NY),
        )
        copy.start()
        sends.append(copy)

    def arrived(part, off, half=None):
        ref = piece(part, off, half)
        remote(
            ref, ref, ws_sem.at[0], wr_sem.at[part, off[0] + 1, off[1] + 1, half or 0], s, f
        ).wait_recv()

    def at(part, a, b):
        return (a, b) if part == 0 else (b, a)

    for copy in load_w:
        copy.wait()
    for part in range(2):
        for d in (1, -1):
            pass_on(part, (0, 0), at(part, d, 0))
    for part in range(2):
        for d in (1, -1):
            pass_on(part, (0, 0), at(part, 0, d))
    load_x.wait()
    give_x = remote(xs.at[own_tok], xs.at[own_tok], xr_sem.at[0], xr_sem.at[1], sib, f)
    give_x.start()

    own_seq = pl.ds(pl.multiple_of(s * TOK, TOK), TOK)
    own_head = pl.ds(pl.multiple_of(s * HD, HD), HD)
    keep = []
    for i, (src, dst) in enumerate(((q_ref, qh_ref), (g_ref, gh_ref))):
        keep.append(pltpu.make_async_copy(src.at[:, own_head], dst.at[own_seq], ql_sem.at[i]))
        keep[-1].start()
    for step in range(1, 2 * NZ):
        to = ring(s + step, 2 * NZ)
        head = pl.ds(pl.multiple_of(to * HD, HD), HD)
        for i, (src, dst) in enumerate(((q_ref, qh_ref), (g_ref, gh_ref))):
            remote(src.at[:, head], dst.at[own_seq], qs_sem.at[i], qr_sem.at[i], to, f).start()

    for d in (-1, 1):
        for part in range(2):
            arrived(part, at(part, d, 0))
            pass_on(part, at(part, d, 0), at(part, -d, 0), 0 if d < 0 else 1)
            for e in (1, -1):
                pass_on(part, at(part, d, 0), at(part, 0, e))
    for d in (-1, 1):
        for part in range(2):
            arrived(part, at(part, 0, d))
            pass_on(part, at(part, 0, d), at(part, 0, -d), 0 if d < 0 else 1)
    for part in range(2):
        arrived(part, at(part, 2, 0), 0)
        arrived(part, at(part, 2, 0), 1)
        for e in (1, -1):
            pass_on(part, at(part, 2, 0), at(part, 0, e))
    remote(xs.at[own_tok], xs.at[own_tok], xr_sem.at[0], xr_sem.at[1], sib, f).wait_recv()

    def turn(i, carry):
        cols = pl.ds(pl.multiple_of(i * 256, 256), 256)
        xt_ref[cols, :] = xs[:, cols].T
        return carry

    lax.fori_loop(0, D // 256, turn, 0)
    for a in (-1, 1, 2):
        for d in (-1, 1):
            for part in range(2):
                arrived(part, at(part, a, d))
                pass_on(part, at(part, a, d), at(part, 0, -d), 0 if d < 0 else 1)
    for a in (0, -1, 1, 2):
        for part in range(2):
            arrived(part, at(part, a, 2), 0)
            arrived(part, at(part, a, 2), 1)
    save_w = pltpu.make_async_copy(wg, wh_ref, o_sem)
    save_w.start()

    def kv_copy(k):
        kind = k // 4
        head = 2 * (k % 4) + c
        to = 2 * head + kind
        rows = pl.ds(pl.multiple_of(z * CTOK, CTOK), CTOK)
        local = pltpu.make_async_copy(proj.at[k], kv_ref.at[kind, rows], kr_sem)
        away = remote(proj.at[k], kv_ref.at[kind, rows], ks_sem.at[k], kr_sem, to, f)
        return to == s, local, away

    for t in range(4):
        res = jnp.dot(xs[...], wg[:, t * 256 : (t + 1) * 256], preferred_element_type=F32)
        for j in range(2):
            k = 2 * t + j
            block = res[:, j * HD : (j + 1) * HD]
            if k < 4:
                block = rotated(block, cos_ref[...], sin_ref[...])
            proj[k] = block.astype(BF)
            mine, local, away = kv_copy(k)

            @pl.when(mine)
            def _():
                local.start()

            @pl.when(jnp.logical_not(mine))
            def _():
                away.start()

    for copy in sends:
        copy.wait_send()
    give_x.wait_send()
    for copy in keep:
        copy.wait()
    for i, (src, dst) in enumerate(((q_ref, qh_ref), (g_ref, gh_ref))):
        others = dst.at[pl.ds(0, SEQLEN - TOK)]
        whole = remote(others, others, qs_sem.at[i], qr_sem.at[i], sib, f)
        whole.wait_send()
        whole.wait_recv()
    got = kv_ref.at[c]
    pltpu.make_async_copy(got, got, kr_sem).wait()
    share = remote(got, got, fs_sem, fr_sem, sib, f)
    share.start()
    for k in range(8):
        mine, local, away = kv_copy(k)

        @pl.when(jnp.logical_not(mine))
        def _():
            away.wait_send()

    share.wait()
    save_w.wait()


def k1(x, q, w, g, cosine, sine):
    dma = pltpu.SemaphoreType.DMA
    seq_block = jax.ShapeDtypeStruct((SEQLEN, HD), BF)
    return pl.pallas_call(
        k1_kernel,
        out_shape=(
            seq_block,
            seq_block,
            jax.ShapeDtypeStruct((2, SEQLEN, HD), BF),
            jax.ShapeDtypeStruct((D, CTOK), BF),
            jax.ShapeDtypeStruct((D, HALF), BF),
        ),
        in_specs=[ANY, ANY, ANY, ANY, VM, VM],
        out_specs=(ANY, ANY, ANY, VM, ANY),
        scratch_shapes=[
            pltpu.VMEM((D, HALF), BF),
            pltpu.VMEM((CTOK, D), BF),
            pltpu.VMEM((8, CTOK, HD), BF),
            dma((8,)),
            dma(()),
            dma((2,)),
            dma((40,)),
            dma((2, 4, 4, 2)),
            dma((2,)),
            dma((2,)),
            dma((2,)),
            dma((8,)),
            dma(()),
            dma(()),
            dma(()),
            dma(()),
        ],
        compiler_params=pltpu.CompilerParams(
            collective_id=0, has_side_effects=True, vmem_limit_bytes=40 << 20
        ),
        name="gather_project",
    )(x, q, w, g, cosine, sine)


QT = 256
KT = 256
NT = (((1,), (1,)), ((), ()))


def k2_kernel(len_ref, q_ref, g_ref, kv_ref, o_ref, dkv_ref, vt, wbuf, tbuf, dk, dv):
    ends = []
    total = 0
    for i in range(NDOC):
        total = total + len_ref[i]
        ends.append(total)
    dk[...] = jnp.zeros_like(dk)
    dv[...] = jnp.zeros_like(dv)

    def flip(i, carry):
        rows = pl.ds(pl.multiple_of(i * KT, KT), KT)
        vt[:, rows] = kv_ref[1, rows, :].T
        return carry

    lax.fori_loop(0, SEQLEN // KT, flip, 0)

    def one_tile(i, carry):
        base = i * QT
        rows = pl.ds(pl.multiple_of(base, QT), QT)
        qt = q_ref[rows, :]
        gt = g_ref[rows, :]
        pos = base + lax.broadcasted_iota(jnp.int32, (1, QT), 1)
        start = jnp.zeros((1, QT), jnp.int32)
        first = jnp.int32(0)
        for end in ends:
            start = jnp.where(pos >= end, end, start)
            first = jnp.where(base >= end, end, first)
        low = jnp.maximum(start, pos - (WIN - 1))
        first = jnp.maximum(first, base - (WIN - 1)) // KT

        def forward(t, state):
            acc, norm = state
            krows = pl.ds(pl.multiple_of(t * KT, KT), KT)
            st = lax.dot_general(kv_ref[0, krows, :], qt, NT, preferred_element_type=F32)
            squashed = jnp.tanh(st * (SCALE / CAP))
            key = t * KT + lax.broadcasted_iota(jnp.int32, (KT, QT), 0)
            allowed = (key <= pos) & (key >= low)
            weight = jnp.where(allowed, jnp.exp(CAP * squashed), 0.0)
            slot = t - first
            wbuf[slot] = weight
            tbuf[slot] = squashed
            norm = norm + jnp.sum(weight, axis=0, keepdims=True)
            acc = acc + jnp.dot(vt[:, krows], weight.astype(BF), preferred_element_type=F32)
            return acc, norm

        acc, norm = lax.fori_loop(
            first, i + 1, forward, (jnp.zeros((HD, QT), F32), jnp.zeros((1, QT), F32))
        )
        inverse = 1.0 / norm
        out_t = (acc * inverse).astype(BF)
        out = out_t.astype(F32).T
        o_ref[rows, :] = out.astype(BF)
        delta = jnp.sum(gt.astype(F32).T * out_t.astype(F32), axis=0, keepdims=True)

        def backward(t, carry2):
            krows = pl.ds(pl.multiple_of(t * KT, KT), KT)
            slot = t - first
            probs = wbuf[slot] * inverse
            squashed = tbuf[slot]
            dprob = lax.dot_general(kv_ref[1, krows, :], gt, NT, preferred_element_type=F32)
            dscore = probs * (dprob - delta) * (1.0 - squashed * squashed)
            dk[krows, :] += jnp.dot(dscore.astype(BF), qt, preferred_element_type=F32)
            dv[krows, :] += jnp.dot(probs.astype(BF), gt, preferred_element_type=F32)
            return carry2

        lax.fori_loop(first, i + 1, backward, 0)
        return carry

    lax.fori_loop(0, SEQLEN // QT, one_tile, 0)
    dkv_ref[0] = (dk[...] * SCALE).astype(BF)
    dkv_ref[1] = dv[...].astype(BF)


def k2(lengths, qh, gh, kv):
    return pl.pallas_call(
        k2_kernel,
        out_shape=(
            jax.ShapeDtypeStruct((SEQLEN, HD), BF),
            jax.ShapeDtypeStruct((2, SEQLEN, HD), BF),
        ),
        in_specs=[pl.BlockSpec(memory_space=pltpu.SMEM), VM, VM, VM],
        out_specs=(VM, VM),
        scratch_shapes=[
            pltpu.VMEM((HD, SEQLEN), BF),
            pltpu.VMEM((5, KT, QT), F32),
            pltpu.VMEM((5, KT, QT), F32),
            pltpu.VMEM((SEQLEN, HD), F32),
            pltpu.VMEM((SEQLEN, HD), F32),
        ],
        compiler_params=pltpu.CompilerParams(vmem_limit_bytes=40 << 20),
        name="attend",
    )(lengths, qh, gh, kv)


def k3_kernel(
    o_ref,
    dkv_ref,
    xt_ref,
    wh_ref,
    cos_ref,
    sin_ref,
    out_ref,
    gin_ref,
    gw_ref,
    wv,
    mine,
    theirs,
    total,
    got,
    dd,
    gi,
    gsend,
    grecv,
    part_sum,
    r1,
    r2,
    second,
    r3,
    r4,
    third,
    zr,
    l_sem,
    sib_sem,
    ds_sem,
    dr_sem,
    ol_sem,
    os_sem,
    or_sem,
    g_sem,
    s1_sem,
    r1_sem,
    s2_sem,
    r2_sem,
    s3_sem,
    r3_sem,
    s4_sem,
    r4_sem,
    zs_sem,
    zr_sem,
):
    s, f, z, c, x, y = where_am_i()
    sib = s + 1 - 2 * c
    load_w = pltpu.make_async_copy(wh_ref, wv, l_sem.at[0])
    load_d = pltpu.make_async_copy(dkv_ref.at[c], mine, l_sem.at[1])
    load_d.start()
    load_w.start()
    enter(s, f, x, y)
    swap = remote(dkv_ref.at[1 - c], theirs, sib_sem.at[0], sib_sem.at[1], sib, f)
    swap.start()
    load_d.wait()
    swap.wait_recv()
    slot = 4 * c + z // 2
    target = 2 * ring(z, NZ) + lax.rem(z, 2)

    def d_copy(step):
        chip = ring(z + step, NZ)
        rows = pl.ds(pl.multiple_of(chip * CTOK, CTOK), CTOK)
        to = 2 * chip + lax.rem(z, 2)
        return rows, remote(total.at[rows], got.at[slot], ds_sem.at[step], dr_sem, to, f)

    for step in (4, 3, 5, 2, 6, 1, 7):
        rows, copy = d_copy(step)
        total[rows, :] = (mine[rows, :].astype(F32) + theirs[rows, :].astype(F32)).astype(BF)
        copy.start()
    rows, copy = d_copy(0)
    total[rows, :] = (mine[rows, :].astype(F32) + theirs[rows, :].astype(F32)).astype(BF)
    local = pltpu.make_async_copy(total.at[rows], got.at[slot], dr_sem)

    @pl.when(target == s)
    def _():
        local.start()

    @pl.when(target != s)
    def _():
        copy.start()

    own_head = pl.ds(pl.multiple_of(s * HD, HD), HD)
    own_seq = pl.ds(pl.multiple_of(s * TOK, TOK), TOK)
    keep_o = pltpu.make_async_copy(o_ref.at[own_seq], out_ref.at[:, own_head], ol_sem)
    keep_o.start()
    for step in range(1, 2 * NZ):
        to = ring(s + step, 2 * NZ)
        theirs_tok = pl.ds(pl.multiple_of(to * TOK, TOK), TOK)
        remote(
            o_ref.at[theirs_tok], out_ref.at[:, own_head], os_sem, or_sem, to, f
        ).start()

    pltpu.make_async_copy(got, got, dr_sem).wait()
    for k in range(8):
        block = got[k]
        if k < 4:
            block = rotated(block.astype(F32), cos_ref[...], -sin_ref[...]).astype(BF)
        dd[:, k * HD : (k + 1) * HD] = block

    def term(part, cx, cy):
        rows = pl.ds(pl.multiple_of((cx * NY + cy) * ROWS, 16), ROWS)
        cols = pl.ds(part * PART, PART)
        part_sum[part, cx, cy] = jnp.dot(
            xt_ref[rows, :], dd[:, cols], preferred_element_type=F32
        ).astype(BF)

    def chunk(part, a):
        for j in range(4):
            if part == 0:
                term(part, a, j)
            else:
                term(part, j, a)

    def chunk_ref(part, a, cols):
        if part == 0:
            return part_sum.at[part, a, :, :, cols]
        return part_sum.at[part, :, a, :, cols]

    first_axis = (x, y)
    second_axis = (y, x)

    def neighbour(part, level, d):
        along_x = (part == 0) == (level == 0)
        if along_x:
            return ring(x + d, NX) * NY + y
        return x * NY + ring(y + d, NY)

    halves = (pl.ds(0, PART // 2), pl.ds(PART // 2, PART // 2))
    full = pl.ds(0, PART)
    dirs = (1, -1)
    sent = []
    for part in range(2):
        far = ring(first_axis[part] + 2, 4)
        chunk(part, far)
        for h, d in enumerate(dirs):
            copy = remote(
                chunk_ref(part, far, halves[h]),
                r1.at[part, h],
                s1_sem.at[part, h],
                r1_sem.at[part, h],
                s,
                neighbour(part, 0, d),
            )
            copy.start()
            sent.append(copy)
    for part in range(2):
        for d in (1, -1, 0):
            chunk(part, ring(first_axis[part] + d, 4))
    for part in range(2):
        for h, d in enumerate(dirs):
            near = ring(first_axis[part] + d, 4)
            remote(
                r1.at[part, h], r1.at[part, h], s1_sem.at[part, h], r1_sem.at[part, h], s, f
            ).wait_recv()
            cols = slice(h * (PART // 2), (h + 1) * (PART // 2))
            for j in range(4):
                idx = (part, near, j) if part == 0 else (part, j, near)
                part_sum[idx + (slice(None), cols)] = (
                    part_sum[idx + (slice(None), cols)].astype(F32)
                    + r1[part, h, j].astype(F32)
                ).astype(BF)
            copy = remote(
                chunk_ref(part, near, full),
                r2.at[part, h],
                s2_sem.at[part, h],
                r2_sem.at[part, h],
                s,
                neighbour(part, 0, d),
            )
            copy.start()
            sent.append(copy)

    load_w.wait()

    def input_tile(i, carry):
        rows = pl.ds(pl.multiple_of(i * 256, 256), 256)
        gi[:, rows] = lax.dot_general(dd[...], wv[rows, :], NT, preferred_element_type=F32)
        return carry

    lax.fori_loop(0, D // 256, input_tile, 0)
    other_tok = pl.ds(pl.multiple_of((1 - c) * TOK, TOK), TOK)
    own_tok = pl.ds(pl.multiple_of(c * TOK, TOK), TOK)
    gsend[...] = gi[other_tok, :].astype(BF)
    give = remote(gsend, grecv, g_sem.at[0], g_sem.at[1], sib, f)
    give.start()

    for part in range(2):
        for h in range(2):
            remote(
                r2.at[part, h], r2.at[part, h], s2_sem.at[part, h], r2_sem.at[part, h], s, f
            ).wait_recv()
        for j in range(4):
            idx = (part, x, j) if part == 0 else (part, j, y)
            second[part, j] = (
                part_sum[idx].astype(F32)
                + r2[part, 0, j].astype(F32)
                + r2[part, 1, j].astype(F32)
            ).astype(BF)
        far = ring(second_axis[part] + 2, 4)
        for h, d in enumerate(dirs):
            copy = remote(
                second.at[part, far, :, halves[h]],
                r3.at[part, h],
                s3_sem.at[part, h],
                r3_sem.at[part, h],
                s,
                neighbour(part, 1, d),
            )
            copy.start()
            sent.append(copy)
    for part in range(2):
        for h, d in enumerate(dirs):
            near = ring(second_axis[part] + d, 4)
            remote(
                r3.at[part, h], r3.at[part, h], s3_sem.at[part, h], r3_sem.at[part, h], s, f
            ).wait_recv()
            cols = slice(h * (PART // 2), (h + 1) * (PART // 2))
            second[part, near, :, cols] = (
                second[part, near, :, cols].astype(F32) + r3[part, h].astype(F32)
            ).astype(BF)
            copy = remote(
                second.at[part, near],
                r4.at[part, h],
                s4_sem.at[part, h],
                r4_sem.at[part, h],
                s,
                neighbour(part, 1, d),
            )
            copy.start()
            sent.append(copy)
    give.wait()
    gin_ref[...] = (gi[own_tok, :] + grecv[...].astype(F32)).astype(BF)
    for part in range(2):
        for h in range(2):
            remote(
                r4.at[part, h], r4.at[part, h], s4_sem.at[part, h], r4_sem.at[part, h], s, f
            ).wait_recv()
        summed = (
            second[part, second_axis[part]].astype(F32)
            + r4[part, 0].astype(F32)
            + r4[part, 1].astype(F32)
        ).astype(BF)
        for k in range(4):
            third[4 * part + k] = summed[:, k * HD : (k + 1) * HD]
    for step in range(1, NZ):
        chip = ring(z + step, NZ)
        copy = remote(
            third.at[chip], zr.at[step], zs_sem.at[step], zr_sem, 2 * chip + c, f
        )
        copy.start()
        sent.append(copy)
    for copy in sent:
        copy.wait_send()
    swap.wait_send()
    for step in range(1, NZ):
        d_copy(step)[1].wait_send()

    @pl.when(target != s)
    def _():
        copy0 = d_copy(0)[1]
        copy0.wait_send()

    keep_o.wait()
    others = o_ref.at[pl.ds(0, SEQLEN - TOK)]
    whole = remote(others, others, os_sem, or_sem, sib, f)
    whole.wait_send()
    whole.wait_recv()
    rest = zr.at[pl.ds(1, NZ - 1)]
    pltpu.make_async_copy(rest, rest, zr_sem).wait()
    acc = third[z].astype(F32)
    for step in range(1, NZ):
        acc = acc + zr[step].astype(F32)
    gw_ref[...] = acc


def k3(o, dkv, xt, wh, cosine, sine):
    dma = pltpu.SemaphoreType.DMA
    return pl.pallas_call(
        k3_kernel,
        out_shape=(
            jax.ShapeDtypeStruct((TOK, 2048), BF),
            jax.ShapeDtypeStruct((TOK, D), BF),
            jax.ShapeDtypeStruct((ROWS, HD), F32),
        ),
        in_specs=[ANY, ANY, VM, ANY, VM, VM],
        out_specs=(ANY, VM, VM),
        scratch_shapes=[
            pltpu.VMEM((D, HALF), BF),
            pltpu.VMEM((SEQLEN, HD), BF),
            pltpu.VMEM((SEQLEN, HD), BF),
            pltpu.VMEM((SEQLEN, HD), BF),
            pltpu.VMEM((8, CTOK, HD), BF),
            pltpu.VMEM((CTOK, HALF), BF),
            pltpu.VMEM((CTOK, D), F32),
            pltpu.VMEM((TOK, D), BF),
            pltpu.VMEM((TOK, D), BF),
            pltpu.VMEM((2, 4, 4, ROWS, PART), BF),
            pltpu.VMEM((2, 2, 4, ROWS, PART // 2), BF),
            pltpu.VMEM((2, 2, 4, ROWS, PART), BF),
            pltpu.VMEM((2, 4, ROWS, PART), BF),
            pltpu.VMEM((2, 2, ROWS, PART // 2), BF),
            pltpu.VMEM((2, 2, ROWS, PART), BF),
            pltpu.VMEM((8, ROWS, HD), BF),
            pltpu.VMEM((8, ROWS, HD), BF),
            dma((2,)),
            dma((2,)),
            dma((8,)),
            dma(()),
            dma(()),
            dma(()),
            dma(()),
            dma((2,)),
            dma((2, 2)),
            dma((2, 2)),
            dma((2, 2)),
            dma((2, 2)),
            dma((2, 2)),
            dma((2, 2)),
            dma((2, 2)),
            dma((2, 2)),
            dma((8,)),
            dma(()),
        ],
        compiler_params=pltpu.CompilerParams(
            collective_id=1, has_side_effects=True, vmem_limit_bytes=48 << 20
        ),
        name="gradients",
    )(o, dkv, xt, wh, cosine, sine)


def tables(lengths):
    z = lax.axis_index("seq") // 2
    places = z * CTOK + jnp.arange(CTOK, dtype=jnp.int32)
    order = jnp.arange(NDOC)
    doc_ends = jnp.sum(jnp.where(order[:, None] <= order[None, :], lengths[:, None], 0), axis=0)
    ended = doc_ends[None, :] <= places[:, None]
    within = places - jnp.sum(jnp.where(ended, lengths[None, :], 0), axis=1)
    exponent = jnp.arange(HD // 2, dtype=F32) * (2.0 / HD)
    rate = jnp.power(ROPE_BASE, -exponent)
    angles = within.astype(F32)[:, None] * rate[None, :]
    cosine, sine = jnp.cos(angles), jnp.sin(angles)
    return (
        jnp.concatenate([cosine, cosine], axis=1),
        jnp.concatenate([-sine, sine], axis=1),
    )


def on_device(inputs, queries, w_kv, doc_lengths, grad_out):
    cosine, sine = tables(doc_lengths[0])
    qh, gh, kv, xt, wh = k1(inputs[0], queries[0], w_kv, grad_out[0], cosine, sine)
    o, dkv = k2(doc_lengths[0], qh, gh, kv)
    out, gin, gw = k3(o, dkv, xt, wh, cosine, sine)
    return out[None], gin[None], gw


def solution(mesh):
    in_specs = (
        P("fsdp", "seq", None),
        P("fsdp", "seq", None),
        P("fsdp", None),
        P("fsdp", None),
        P("fsdp", "seq", None),
    )
    out_specs = (P("fsdp", "seq", None), P("fsdp", "seq", None), P("fsdp", "seq"))
    return jax.shard_map(
        on_device, mesh=mesh, in_specs=in_specs, out_specs=out_specs, check_vma=False
    )
```

```python
import functools

import jax
import jax.numpy as jnp
from jax import lax
from jax.experimental import pallas as pl
from jax.experimental.pallas import tpu as pltpu
from jax.sharding import PartitionSpec as P

D = 2304
HD = 128
WIN = 1024
SEQLEN = 2048
NDOC = 8
NZ = 8
NX = 4
NY = 4
ROWS = D // (NX * NY)
HALF = 1024
PART = 512
TOK = 128
CTOK = 256
CAP = 50.0
SCALE = 1.0 / 12.0
ROPE_BASE = 10000.0
MESH = pl.DeviceIdType.MESH
HBM = pl.BlockSpec(memory_space=pltpu.HBM)
VM = pl.BlockSpec(memory_space=pltpu.VMEM)
BF = jnp.bfloat16
F32 = jnp.float32


def where_am_i():
    s = lax.axis_index("seq")
    f = lax.axis_index("fsdp")
    z = s // 2
    c = s - 2 * z
    x = f // NY
    y = f - NY * x
    return s, f, z, c, x, y


def ring(v, n):
    return lax.rem(v + n, n)


def remote(src, dst, send, recv, s, f):
    return pltpu.make_async_remote_copy(
        src_ref=src,
        dst_ref=dst,
        send_sem=send,
        recv_sem=recv,
        device_id={"seq": s, "fsdp": f},
        device_id_type=MESH,
    )


def enter(s, f, x, y):
    barrier = pltpu.get_barrier_semaphore()
    for step in range(1, 2 * NZ):
        pl.semaphore_signal(
            barrier,
            inc=1,
            device_id={"seq": ring(s + step, 2 * NZ), "fsdp": f},
            device_id_type=MESH,
        )
    for dx, dy in ((1, 0), (-1, 0), (0, 1), (0, -1)):
        pl.semaphore_signal(
            barrier,
            inc=1,
            device_id={"seq": s, "fsdp": ring(x + dx, NX) * NY + ring(y + dy, NY)},
            device_id_type=MESH,
        )
    pl.semaphore_wait(barrier, 2 * NZ - 1 + 4)


def rotated(values, cosine, sine):
    return values * cosine + pltpu.roll(values, HD // 2, 1) * sine


def k1_kernel(
    x_ref,
    q_ref,
    w_ref,
    g_ref,
    cos_ref,
    sin_ref,
    qh_ref,
    gh_ref,
    kv_ref,
    xs,
    wg,
    proj,
    wl_sem,
    xl_sem,
    xr_sem,
    ws_sem,
    wr_sem,
    ql_sem,
    qs_sem,
    qr_sem,
    ks_sem,
    kr_sem,
    fs_sem,
    fr_sem,
):
    s, f, z, c, x, y = where_am_i()
    sib = s + 1 - 2 * c
    own_rows = pl.ds(pl.multiple_of(f * ROWS, 16), ROWS)
    load_w = []
    for k in range(8):
        cols = pl.ds(pl.multiple_of((2 * k + c) * HD, HD), HD)
        load_w.append(
            pltpu.make_async_copy(
                w_ref.at[:, cols], wg.at[own_rows, pl.ds(k * HD, HD)], wl_sem.at[k]
            )
        )
    for copy in load_w:
        copy.start()
    own_tok = pl.ds(pl.multiple_of(c * TOK, TOK), TOK)
    load_x = pltpu.make_async_copy(x_ref, xs.at[own_tok], xl_sem)
    load_x.start()
    enter(s, f, x, y)

    wide = PART // 2

    def piece(phase, part, off, half):
        origin = ring(x + off[0], NX) * NY + ring(y + off[1], NY)
        rows = pl.ds(pl.multiple_of(origin * ROWS, 16), ROWS)
        base = phase * PART + part * wide
        if half is None:
            return wg.at[rows, pl.ds(base, wide)]
        return wg.at[rows, pl.ds(base + half * (wide // 2), wide // 2)]

    sends = []

    def pass_on(phase, part, off, step, half=None):
        there = tuple((o - d) % 4 for o, d in zip(off, step))
        there = tuple(-1 if t == 3 else t for t in there)
        ref = piece(phase, part, off, half)
        copy = remote(
            ref,
            ref,
            ws_sem.at[len(sends)],
            wr_sem.at[phase, part, there[0] + 1, there[1] + 1, half or 0],
            s,
            ring(x + step[0], NX) * NY + ring(y + step[1], NY),
        )
        copy.start()
        sends.append(copy)

    def arrived(phase, part, off, half=None):
        ref = piece(phase, part, off, half)
        sem = wr_sem.at[phase, part, off[0] + 1, off[1] + 1, half or 0]
        pltpu.make_async_copy(ref, ref, sem).wait()

    def at(part, a, b):
        return (a, b) if part == 0 else (b, a)

    def begin(p):
        for d in (1, -1):
            for part in range(2):
                pass_on(p, part, (0, 0), at(part, d, 0))
        for d in (1, -1):
            for part in range(2):
                pass_on(p, part, (0, 0), at(part, 0, d))

    def near_first(p):
        for d in (-1, 1):
            for part in range(2):
                arrived(p, part, at(part, d, 0))
                pass_on(p, part, at(part, d, 0), at(part, -d, 0), 0 if d < 0 else 1)
                for e in (1, -1):
                    pass_on(p, part, at(part, d, 0), at(part, 0, e))

    def near_second(p):
        for d in (-1, 1):
            for part in range(2):
                arrived(p, part, at(part, 0, d))
                pass_on(p, part, at(part, 0, d), at(part, 0, -d), 0 if d < 0 else 1)

    def far_first(p):
        for part in range(2):
            arrived(p, part, at(part, 2, 0), 0)
            arrived(p, part, at(part, 2, 0), 1)
            for e in (1, -1):
                pass_on(p, part, at(part, 2, 0), at(part, 0, e))

    def rest_second(p):
        for a in (-1, 1, 2):
            for d in (-1, 1):
                for part in range(2):
                    arrived(p, part, at(part, a, d))
                    pass_on(p, part, at(part, a, d), at(part, 0, -d), 0 if d < 0 else 1)

    def finish(p):
        for a in (0, -1, 1, 2):
            for part in range(2):
                arrived(p, part, at(part, a, 2), 0)
                arrived(p, part, at(part, a, 2), 1)

    def kv_copy(k):
        kind = k // 4
        to = 2 * (2 * (k % 4) + c) + z // 4
        rows = pl.ds(pl.multiple_of(z * CTOK, CTOK), CTOK)
        local = pltpu.make_async_copy(proj.at[k], kv_ref.at[kind, rows], kr_sem.at[kind])
        away = remote(proj.at[k], kv_ref.at[kind, rows], ks_sem.at[k], kr_sem.at[kind], to, f)
        return to == s, local, away

    def project(p):
        for t in (2 * p, 2 * p + 1):
            res = jnp.dot(xs[...], wg[:, t * 256 : (t + 1) * 256], preferred_element_type=F32)
            for j in range(2):
                k = 2 * t + j
                block = res[:, j * HD : (j + 1) * HD]
                if k < 4:
                    block = rotated(block, cos_ref[...], sin_ref[...])
                proj[k] = block.astype(BF)
                mine, local, away = kv_copy(k)

                @pl.when(mine)
                def _():
                    local.start()

                @pl.when(jnp.logical_not(mine))
                def _():
                    away.start()

    shares = []

    def share(p):
        half = kv_ref.at[p, pl.ds(pl.multiple_of(c * (SEQLEN // 2), SEQLEN // 2), SEQLEN // 2)]
        pltpu.make_async_copy(half, half, kr_sem.at[p]).wait()
        copy = remote(half, half, fs_sem.at[p], fr_sem.at[p], sib, f)
        copy.start()
        shares.append(copy)

    for copy in load_w:
        copy.wait()
    begin(0)
    load_x.wait()
    give_x = remote(xs.at[own_tok], xs.at[own_tok], xr_sem.at[0], xr_sem.at[1], sib, f)
    give_x.start()

    own_seq = pl.ds(pl.multiple_of(s * TOK, TOK), TOK)
    own_head = pl.ds(pl.multiple_of(s * HD, HD), HD)
    keep = []
    for i, (src, dst) in enumerate(((q_ref, qh_ref), (g_ref, gh_ref))):
        keep.append(pltpu.make_async_copy(src.at[:, own_head], dst.at[own_seq], ql_sem.at[i]))
        keep[-1].start()
    for step in range(1, 2 * NZ):
        to = ring(s + step, 2 * NZ)
        head = pl.ds(pl.multiple_of(to * HD, HD), HD)
        for i, (src, dst) in enumerate(((q_ref, qh_ref), (g_ref, gh_ref))):
            remote(src.at[:, head], dst.at[own_seq], qs_sem.at[i], qr_sem.at[i], to, f).start()

    near_first(0)
    near_second(0)
    far_first(0)
    rest_second(0)
    begin(1)
    finish(0)
    give_x.wait_recv()
    project(0)
    near_first(1)
    near_second(1)
    far_first(1)
    rest_second(1)
    finish(1)
    project(1)
    share(0)
    for copy in sends:
        copy.wait_send()
    give_x.wait_send()
    for copy in keep:
        copy.wait()
    for i, dst in enumerate((qh_ref, gh_ref)):
        others = dst.at[pl.ds(0, SEQLEN - TOK)]
        pltpu.make_async_copy(others, others, qs_sem.at[i]).wait()
        pltpu.make_async_copy(others, others, qr_sem.at[i]).wait()
    share(1)
    for k in range(8):
        mine, _, away = kv_copy(k)

        @pl.when(jnp.logical_not(mine))
        def _():
            away.wait_send()

    for copy in shares:
        copy.wait()


def k1(x, q, w, g, cosine, sine):
    dma = pltpu.SemaphoreType.DMA
    seq_block = jax.ShapeDtypeStruct((SEQLEN, HD), BF)
    return pl.pallas_call(
        k1_kernel,
        out_shape=(
            seq_block,
            seq_block,
            jax.ShapeDtypeStruct((2, SEQLEN, HD), BF),
            jax.ShapeDtypeStruct((CTOK, D), BF),
            jax.ShapeDtypeStruct((D, HALF), BF),
        ),
        in_specs=[HBM, HBM, HBM, HBM, VM, VM],
        out_specs=(VM, VM, VM, VM, VM),
        scratch_shapes=[
            pltpu.VMEM((8, CTOK, HD), BF),
            dma((8,)),
            dma(()),
            dma((2,)),
            dma((80,)),
            dma((2, 2, 4, 4, 2)),
            dma((2,)),
            dma((2,)),
            dma((2,)),
            dma((8,)),
            dma((2,)),
            dma((2,)),
            dma((2,)),
        ],
        compiler_params=pltpu.CompilerParams(
            collective_id=0, has_side_effects=True, vmem_limit_bytes=16 << 20
        ),
        name="gather_project",
    )(x, q, w, g, cosine, sine)


QT = 256
KT = 256
NT = (((1,), (1,)), ((), ()))


def k2_kernel(len_ref, q_ref, g_ref, kv_ref, o_ref, dkv_ref, vt, wbuf, tbuf, dk, dv):
    ends = []
    total = 0
    for i in range(NDOC):
        total = total + len_ref[i]
        ends.append(total)
    dk[...] = jnp.zeros_like(dk)
    dv[...] = jnp.zeros_like(dv)

    def flip(i, carry):
        rows = pl.ds(pl.multiple_of(i * KT, KT), KT)
        vt[:, rows] = kv_ref[1, rows, :].T
        return carry

    lax.fori_loop(0, SEQLEN // KT, flip, 0)

    def one_tile(i, carry):
        base = i * QT
        rows = pl.ds(pl.multiple_of(base, QT), QT)
        qt = q_ref[rows, :]
        gt = g_ref[rows, :]
        pos = base + lax.broadcasted_iota(jnp.int32, (1, QT), 1)
        start = jnp.zeros((1, QT), jnp.int32)
        first = jnp.int32(0)
        for end in ends:
            start = jnp.where(pos >= end, end, start)
            first = jnp.where(base >= end, end, first)
        low = jnp.maximum(start, pos - (WIN - 1))
        first = jnp.maximum(first, base - (WIN - 1)) // KT

        def forward(t, state):
            acc, norm = state
            krows = pl.ds(pl.multiple_of(t * KT, KT), KT)
            st = lax.dot_general(kv_ref[0, krows, :], qt, NT, preferred_element_type=F32)
            squashed = jnp.tanh(st * (SCALE / CAP))
            key = t * KT + lax.broadcasted_iota(jnp.int32, (KT, QT), 0)
            allowed = (key <= pos) & (key >= low)
            weight = jnp.where(allowed, jnp.exp(CAP * squashed), 0.0)
            slot = t - first
            wbuf[slot] = weight
            tbuf[slot] = squashed
            norm = norm + jnp.sum(weight, axis=0, keepdims=True)
            acc = acc + jnp.dot(vt[:, krows], weight.astype(BF), preferred_element_type=F32)
            return acc, norm

        acc, norm = lax.fori_loop(
            first, i + 1, forward, (jnp.zeros((HD, QT), F32), jnp.zeros((1, QT), F32))
        )
        inverse = 1.0 / norm
        out_t = (acc * inverse).astype(BF)
        out = out_t.astype(F32).T
        o_ref[rows, :] = out.astype(BF)
        delta = jnp.sum(gt.astype(F32).T * out_t.astype(F32), axis=0, keepdims=True)

        def backward(t, carry2):
            krows = pl.ds(pl.multiple_of(t * KT, KT), KT)
            slot = t - first
            probs = wbuf[slot] * inverse
            squashed = tbuf[slot]
            dprob = lax.dot_general(kv_ref[1, krows, :], gt, NT, preferred_element_type=F32)
            dscore = probs * (dprob - delta) * (1.0 - squashed * squashed)
            dk[krows, :] += jnp.dot(dscore.astype(BF), qt, preferred_element_type=F32)
            dv[krows, :] += jnp.dot(probs.astype(BF), gt, preferred_element_type=F32)
            return carry2

        lax.fori_loop(first, i + 1, backward, 0)
        return carry

    lax.fori_loop(0, SEQLEN // QT, one_tile, 0)
    dkv_ref[0] = (dk[...] * SCALE).astype(BF)
    dkv_ref[1] = dv[...].astype(BF)


def k2(lengths, qh, gh, kv):
    return pl.pallas_call(
        k2_kernel,
        out_shape=(
            jax.ShapeDtypeStruct((SEQLEN, HD), BF),
            jax.ShapeDtypeStruct((2, SEQLEN, HD), BF),
        ),
        in_specs=[pl.BlockSpec(memory_space=pltpu.SMEM), VM, VM, VM],
        out_specs=(VM, VM),
        scratch_shapes=[
            pltpu.VMEM((HD, SEQLEN), BF),
            pltpu.VMEM((5, KT, QT), F32),
            pltpu.VMEM((5, KT, QT), F32),
            pltpu.VMEM((SEQLEN, HD), F32),
            pltpu.VMEM((SEQLEN, HD), F32),
        ],
        compiler_params=pltpu.CompilerParams(vmem_limit_bytes=16 << 20),
        name="attend",
    )(lengths, qh, gh, kv)


def k3_kernel(
    o_ref,
    dkv_ref,
    xs_ref,
    wv,
    cos_ref,
    sin_ref,
    out_ref,
    gin_ref,
    gw_ref,
    xt,
    theirs,
    total,
    got,
    dd,
    gi,
    gsend,
    grecv,
    part_sum,
    r1,
    r2,
    second,
    r3,
    third,
    zr,
    sib_sem,
    ds_sem,
    dr_sem,
    ol_sem,
    os_sem,
    or_sem,
    g_sem,
    s1_sem,
    r1_sem,
    s2_sem,
    r2_sem,
    s3_sem,
    r3_sem,
    zs_sem,
    zr_sem,
):
    s, f, z, c, x, y = where_am_i()
    sib = s + 1 - 2 * c
    enter(s, f, x, y)
    part_seq = SEQLEN // 2
    swap = remote(
        dkv_ref.at[:, pl.ds(pl.multiple_of((1 - c) * part_seq, part_seq), part_seq)],
        theirs,
        sib_sem.at[0],
        sib_sem.at[1],
        sib,
        f,
    )
    swap.start()

    def turn(i, carry):
        cols = pl.ds(pl.multiple_of(i * 256, 256), 256)
        xt[cols, :] = xs_ref[:, cols].T
        return carry

    lax.fori_loop(0, D // 256, turn, 0)
    swap.wait_recv()

    def d_copy(kind, j):
        chip = 4 * c + j
        rows = pl.ds(j * CTOK, CTOK)
        to = 2 * chip + lax.rem(z, 2)
        slot = 4 * kind + z // 2
        src = total.at[kind, rows]
        local = pltpu.make_async_copy(src, got.at[slot], dr_sem.at[kind])
        away = remote(src, got.at[slot], ds_sem.at[kind, j], dr_sem.at[kind], to, f)
        return to == s, local, away

    def add_up(kind):
        for j in range(4):
            there = pl.ds(pl.multiple_of((4 * c + j) * CTOK, CTOK), CTOK)
            rows = pl.ds(j * CTOK, CTOK)
            total[kind, rows, :] = (
                dkv_ref[kind, there, :].astype(F32) + theirs[kind, rows, :].astype(F32)
            ).astype(BF)

    def send_out(kind):
        for j in range(4):
            mine, local, away = d_copy(kind, j)

            @pl.when(mine)
            def _():
                local.start()

            @pl.when(jnp.logical_not(mine))
            def _():
                away.start()

    def take_in(kind):
        blocks = got.at[pl.ds(4 * kind, 4)]
        pltpu.make_async_copy(blocks, blocks, dr_sem.at[kind]).wait()
        for k in range(4 * kind, 4 * kind + 4):
            block = got[k]
            if kind == 0:
                block = rotated(block.astype(F32), cos_ref[...], -sin_ref[...]).astype(BF)
            dd[:, k * HD : (k + 1) * HD] = block

    wide = PART // 2

    def chunk(p, part, a):
        cols = pl.ds(p * PART + part * wide, wide)
        for j in range(4):
            cx, cy = (a, j) if part == 0 else (j, a)
            rows = pl.ds(pl.multiple_of((cx * NY + cy) * ROWS, 16), ROWS)
            part_sum[p, part, cx, cy] = jnp.dot(
                xt[rows, :], dd[:, cols], preferred_element_type=F32
            ).astype(BF)

    def chunk_ref(p, part, a, cols):
        if part == 0:
            return part_sum.at[p, part, a, :, :, cols]
        return part_sum.at[p, part, :, a, :, cols]

    first_axis = (x, y)
    second_axis = (y, x)

    def neighbour(part, level, d):
        if (part == 0) == (level == 0):
            return ring(x + d, NX) * NY + y
        return x * NY + ring(y + d, NY)

    halves = (pl.ds(0, wide // 2), pl.ds(wide // 2, wide // 2))
    full = pl.ds(0, wide)
    dirs = (1, -1)
    sent = []

    def landed(ref, sem):
        pltpu.make_async_copy(ref, ref, sem).wait()

    def go(src, dst, send, recv, to_f):
        copy = remote(src, dst, send, recv, s, to_f)
        copy.start()
        sent.append(copy)

    def far(p):
        for part in range(2):
            a = ring(first_axis[part] + 2, 4)
            chunk(p, part, a)
            for h, d in enumerate(dirs):
                go(
                    chunk_ref(p, part, a, halves[h]),
                    r1.at[p, part, h],
                    s1_sem.at[p, part, h],
                    r1_sem.at[p, part, h],
                    neighbour(part, 0, d),
                )

    def near(p):
        for part in range(2):
            for d in (1, -1, 0):
                chunk(p, part, ring(first_axis[part] + d, 4))

    def hop(p):
        for h, d in enumerate(dirs):
            for part in range(2):
                a = ring(first_axis[part] + d, 4)
                landed(r1.at[p, part, h], r1_sem.at[p, part, h])
                cols = slice(h * (wide // 2), (h + 1) * (wide // 2))
                for j in range(4):
                    idx = (p, part, a, j) if part == 0 else (p, part, j, a)
                    idx = idx + (slice(None), cols)
                    part_sum[idx] = (
                        part_sum[idx].astype(F32) + r1[p, part, h, j].astype(F32)
                    ).astype(BF)
                go(
                    chunk_ref(p, part, a, full),
                    r2.at[p, part, h],
                    s2_sem.at[p, part, h],
                    r2_sem.at[p, part, h],
                    neighbour(part, 0, d),
                )

    def across(p):
        for part in range(2):
            for h in range(2):
                landed(r2.at[p, part, h], r2_sem.at[p, part, h])
            for j in range(4):
                idx = (p, part, x, j) if part == 0 else (p, part, j, y)
                second[p, part, j] = (
                    part_sum[idx].astype(F32)
                    + r2[p, part, 0, j].astype(F32)
                    + r2[p, part, 1, j].astype(F32)
                ).astype(BF)
            for i, d in enumerate((2, 1, -1)):
                go(
                    second.at[p, part, ring(second_axis[part] + d, 4)],
                    r3.at[p, part, i],
                    s3_sem.at[p, part, i],
                    r3_sem.at[p, part, i],
                    neighbour(part, 1, d),
                )

    def z_copy(p, j):
        chip = 4 * p + j
        return chip != z, remote(
            third.at[chip], zr.at[z], zs_sem.at[chip], zr_sem, 2 * chip + c, f
        )

    def along(p):
        for part in range(2):
            acc = second[p, part, second_axis[part]].astype(F32)
            for i in range(3):
                landed(r3.at[p, part, i], r3_sem.at[p, part, i])
                acc = acc + r3[p, part, i].astype(F32)
            for k in range(2):
                j = 2 * part + k
                third[4 * p + j] = acc[:, k * HD : (k + 1) * HD].astype(BF)
                away, copy = z_copy(p, j)

                @pl.when(away)
                def _():
                    copy.start()

    add_up(0)
    send_out(0)
    add_up(1)
    take_in(0)
    send_out(1)
    far(0)
    near(0)
    hop(0)
    take_in(1)
    own_head = pl.ds(pl.multiple_of(s * HD, HD), HD)
    own_seq = pl.ds(pl.multiple_of(s * TOK, TOK), TOK)
    keep_o = pltpu.make_async_copy(o_ref.at[own_seq], out_ref.at[:, own_head], ol_sem)
    far(1)
    keep_o.start()
    for step in range(1, 2 * NZ):
        to = ring(s + step, 2 * NZ)
        theirs_tok = pl.ds(pl.multiple_of(to * TOK, TOK), TOK)
        remote(
            o_ref.at[theirs_tok], out_ref.at[:, own_head], os_sem, or_sem, to, f
        ).start()
    near(1)
    across(0)
    hop(1)

    def input_tile(i, carry):
        rows = pl.ds(pl.multiple_of(i * 256, 256), 256)
        gi[:, rows] = lax.dot_general(dd[...], wv[rows, :], NT, preferred_element_type=F32)
        return carry

    lax.fori_loop(0, D // 256, input_tile, 0)
    other_tok = pl.ds(pl.multiple_of((1 - c) * TOK, TOK), TOK)
    own_tok = pl.ds(pl.multiple_of(c * TOK, TOK), TOK)
    gsend[...] = gi[other_tok, :].astype(BF)
    give = remote(gsend, grecv, g_sem.at[0], g_sem.at[1], sib, f)
    give.start()
    along(0)
    give.wait()
    gin_ref[...] = (gi[own_tok, :] + grecv[...].astype(F32)).astype(BF)
    across(1)
    along(1)
    for copy in sent:
        copy.wait_send()
    swap.wait_send()
    for kind in range(2):
        for j in range(4):
            mine, _, away = d_copy(kind, j)

            @pl.when(jnp.logical_not(mine))
            def _():
                away.wait_send()

    keep_o.wait()
    others = o_ref.at[pl.ds(0, SEQLEN - TOK)]
    landed(others, os_sem)
    landed(others, or_sem)
    for p in range(2):
        for j in range(4):
            away, copy = z_copy(p, j)

            @pl.when(away)
            def _():
                copy.wait_send()

    rest = zr.at[pl.ds(1, NZ - 1)]
    landed(rest, zr_sem)
    acc = third[z].astype(F32)
    for step in range(1, NZ):
        acc = acc + zr[ring(z + step, NZ)].astype(F32)
    gw_ref[...] = acc


def k3(o, dkv, xs, wh, cosine, sine):
    dma = pltpu.SemaphoreType.DMA
    wide = PART // 2
    return pl.pallas_call(
        k3_kernel,
        out_shape=(
            jax.ShapeDtypeStruct((TOK, 2048), BF),
            jax.ShapeDtypeStruct((TOK, D), BF),
            jax.ShapeDtypeStruct((ROWS, HD), F32),
        ),
        in_specs=[VM, VM, VM, VM, VM, VM],
        out_specs=(VM, VM, VM),
        scratch_shapes=[
            pltpu.VMEM((D, CTOK), BF),
            pltpu.VMEM((2, SEQLEN // 2, HD), BF),
            pltpu.VMEM((2, SEQLEN // 2, HD), BF),
            pltpu.VMEM((8, CTOK, HD), BF),
            pltpu.VMEM((CTOK, HALF), BF),
            pltpu.VMEM((CTOK, D), F32),
            pltpu.VMEM((TOK, D), BF),
            pltpu.VMEM((TOK, D), BF),
            pltpu.VMEM((2, 2, 4, 4, ROWS, wide), BF),
            pltpu.VMEM((2, 2, 2, 4, ROWS, wide // 2), BF),
            pltpu.VMEM((2, 2, 2, 4, ROWS, wide), BF),
            pltpu.VMEM((2, 2, 4, ROWS, wide), BF),
            pltpu.VMEM((2, 2, 3, ROWS, wide), BF),
            pltpu.VMEM((8, ROWS, HD), BF),
            pltpu.VMEM((8, ROWS, HD), BF),
            dma((2,)),
            dma((2, 4)),
            dma((2,)),
            dma(()),
            dma(()),
            dma(()),
            dma((2,)),
            dma((2, 2, 2)),
            dma((2, 2, 2)),
            dma((2, 2, 2)),
            dma((2, 2, 2)),
            dma((2, 2, 3)),
            dma((2, 2, 3)),
            dma((8,)),
            dma(()),
        ],
        compiler_params=pltpu.CompilerParams(
            collective_id=1, has_side_effects=True, vmem_limit_bytes=28 << 20
        ),
        name="gradients",
    )(o, dkv, xs, wh, cosine, sine)


def tables(lengths):
    z = lax.axis_index("seq") // 2
    places = z * CTOK + jnp.arange(CTOK, dtype=jnp.int32)
    order = jnp.arange(NDOC)
    doc_ends = jnp.sum(jnp.where(order[:, None] <= order[None, :], lengths[:, None], 0), axis=0)
    ended = doc_ends[None, :] <= places[:, None]
    within = places - jnp.sum(jnp.where(ended, lengths[None, :], 0), axis=1)
    exponent = jnp.arange(HD // 2, dtype=F32) * (2.0 / HD)
    rate = jnp.power(ROPE_BASE, -exponent)
    angles = within.astype(F32)[:, None] * rate[None, :]
    cosine, sine = jnp.cos(angles), jnp.sin(angles)
    return (
        jnp.concatenate([cosine, cosine], axis=1),
        jnp.concatenate([-sine, sine], axis=1),
    )


def on_device(inputs, queries, w_kv, doc_lengths, grad_out):
    cosine, sine = tables(doc_lengths[0])
    held = [
        pltpu.with_memory_space_constraint(a, pltpu.HBM)
        for a in (inputs[0], queries[0], w_kv, grad_out[0])
    ]
    qh, gh, kv, xs, wh = k1(*held, cosine, sine)
    o, dkv = k2(doc_lengths[0], qh, gh, kv)
    out, gin, gw = k3(o, dkv, xs, wh, cosine, sine)
    return out[None], gin[None], gw


def solution(mesh):
    in_specs = (
        P("fsdp", "seq", None),
        P("fsdp", "seq", None),
        P("fsdp", None),
        P("fsdp", None),
        P("fsdp", "seq", None),
    )
    out_specs = (P("fsdp", "seq", None), P("fsdp", "seq", None), P("fsdp", "seq"))
    return jax.shard_map(
        on_device, mesh=mesh, in_specs=in_specs, out_specs=out_specs, check_vma=False
    )
```

```python
import functools

import jax
import jax.numpy as jnp
from jax import lax
from jax.experimental import pallas as pl
from jax.experimental.pallas import tpu as pltpu
from jax.sharding import PartitionSpec as P

D = 2304
HD = 128
WIN = 1024
SEQLEN = 2048
NDOC = 8
NZ = 8
NX = 4
NY = 4
ROWS = D // (NX * NY)
HALF = 1024
PART = 512
TOK = 128
CTOK = 256
CAP = 50.0
SCALE = 1.0 / 12.0
ROPE_BASE = 10000.0
MESH = pl.DeviceIdType.MESH
HBM = pl.BlockSpec(memory_space=pltpu.HBM)
VM = pl.BlockSpec(memory_space=pltpu.VMEM)
BF = jnp.bfloat16
F32 = jnp.float32


def where_am_i():
    s = lax.axis_index("seq")
    f = lax.axis_index("fsdp")
    z = s // 2
    c = s - 2 * z
    x = f // NY
    y = f - NY * x
    return s, f, z, c, x, y


def ring(v, n):
    return lax.rem(v + n, n)


def remote(src, dst, send, recv, s, f):
    return pltpu.make_async_remote_copy(
        src_ref=src,
        dst_ref=dst,
        send_sem=send,
        recv_sem=recv,
        device_id={"seq": s, "fsdp": f},
        device_id_type=MESH,
    )


def enter(s, f, x, y):
    barrier = pltpu.get_barrier_semaphore()
    for step in range(1, 2 * NZ):
        pl.semaphore_signal(
            barrier,
            inc=1,
            device_id={"seq": ring(s + step, 2 * NZ), "fsdp": f},
            device_id_type=MESH,
        )
    for dx, dy in ((1, 0), (-1, 0), (0, 1), (0, -1)):
        pl.semaphore_signal(
            barrier,
            inc=1,
            device_id={"seq": s, "fsdp": ring(x + dx, NX) * NY + ring(y + dy, NY)},
            device_id_type=MESH,
        )
    pl.semaphore_wait(barrier, 2 * NZ - 1 + 4)


def rotated(values, cosine, sine):
    return values * cosine + pltpu.roll(values, HD // 2, 1) * sine


def k1_kernel(
    x_ref,
    q_ref,
    w_ref,
    g_ref,
    cos_ref,
    sin_ref,
    qh_ref,
    gh_ref,
    kv_ref,
    xs,
    wg,
    proj,
    wl_sem,
    xl_sem,
    xr_sem,
    ws_sem,
    wr_sem,
    ql_sem,
    qs_sem,
    qr_sem,
    ks_sem,
    kr_sem,
    fs_sem,
    fr_sem,
):
    s, f, z, c, x, y = where_am_i()
    sib = s + 1 - 2 * c
    own_rows = pl.ds(pl.multiple_of(f * ROWS, 16), ROWS)
    load_w = []
    for k in range(8):
        cols = pl.ds(pl.multiple_of((2 * k + c) * HD, HD), HD)
        load_w.append(
            pltpu.make_async_copy(
                w_ref.at[:, cols], wg.at[own_rows, pl.ds(k * HD, HD)], wl_sem.at[k]
            )
        )
    for copy in load_w:
        copy.start()
    own_tok = pl.ds(pl.multiple_of(c * TOK, TOK), TOK)
    load_x = pltpu.make_async_copy(x_ref, xs.at[own_tok], xl_sem)
    load_x.start()
    enter(s, f, x, y)

    wide = PART // 2

    def piece(phase, part, off, half):
        origin = ring(x + off[0], NX) * NY + ring(y + off[1], NY)
        rows = pl.ds(pl.multiple_of(origin * ROWS, 16), ROWS)
        base = phase * PART + part * wide
        if half is None:
            return wg.at[rows, pl.ds(base, wide)]
        return wg.at[rows, pl.ds(base + half * (wide // 2), wide // 2)]

    sends = []

    def pass_on(phase, part, off, step, half=None):
        there = tuple((o - d) % 4 for o, d in zip(off, step))
        there = tuple(-1 if t == 3 else t for t in there)
        ref = piece(phase, part, off, half)
        copy = remote(
            ref,
            ref,
            ws_sem.at[len(sends)],
            wr_sem.at[phase, part, there[0] + 1, there[1] + 1, half or 0],
            s,
            ring(x + step[0], NX) * NY + ring(y + step[1], NY),
        )
        copy.start()
        sends.append(copy)

    def arrived(phase, part, off, half=None):
        ref = piece(phase, part, off, half)
        sem = wr_sem.at[phase, part, off[0] + 1, off[1] + 1, half or 0]
        pltpu.make_async_copy(ref, ref, sem).wait()

    def at(part, a, b):
        return (a, b) if part == 0 else (b, a)

    def begin(p):
        for d in (1, -1):
            for part in range(2):
                pass_on(p, part, (0, 0), at(part, d, 0))
        for d in (1, -1):
            for part in range(2):
                pass_on(p, part, (0, 0), at(part, 0, d))

    def near_first(p):
        for d in (-1, 1):
            for part in range(2):
                arrived(p, part, at(part, d, 0))
                pass_on(p, part, at(part, d, 0), at(part, -d, 0), 0 if d < 0 else 1)
                for e in (1, -1):
                    pass_on(p, part, at(part, d, 0), at(part, 0, e))

    def near_second(p):
        for d in (-1, 1):
            for part in range(2):
                arrived(p, part, at(part, 0, d))
                pass_on(p, part, at(part, 0, d), at(part, 0, -d), 0 if d < 0 else 1)

    def far_first(p):
        for part in range(2):
            arrived(p, part, at(part, 2, 0), 0)
            arrived(p, part, at(part, 2, 0), 1)
            for e in (1, -1):
                pass_on(p, part, at(part, 2, 0), at(part, 0, e))

    def rest_second(p):
        for a in (-1, 1, 2):
            for d in (-1, 1):
                for part in range(2):
                    arrived(p, part, at(part, a, d))
                    pass_on(p, part, at(part, a, d), at(part, 0, -d), 0 if d < 0 else 1)

    def finish(p):
        for a in (0, -1, 1, 2):
            for part in range(2):
                arrived(p, part, at(part, a, 2), 0)
                arrived(p, part, at(part, a, 2), 1)

    def kv_copy(k):
        kind = k // 4
        to = 2 * (2 * (k % 4) + c) + z // 4
        rows = pl.ds(pl.multiple_of(z * CTOK, CTOK), CTOK)
        local = pltpu.make_async_copy(proj.at[k], kv_ref.at[kind, rows], kr_sem.at[kind])
        away = remote(proj.at[k], kv_ref.at[kind, rows], ks_sem.at[k], kr_sem.at[kind], to, f)
        return to == s, local, away

    def project(p):
        for t in (2 * p, 2 * p + 1):
            res = jnp.dot(xs[...], wg[:, t * 256 : (t + 1) * 256], preferred_element_type=F32)
            for j in range(2):
                k = 2 * t + j
                block = res[:, j * HD : (j + 1) * HD]
                if k < 4:
                    block = rotated(block, cos_ref[...], sin_ref[...])
                proj[k] = block.astype(BF)
                mine, local, away = kv_copy(k)

                @pl.when(mine)
                def _():
                    local.start()

                @pl.when(jnp.logical_not(mine))
                def _():
                    away.start()

    shares = []

    def share(p):
        half = kv_ref.at[p, pl.ds(pl.multiple_of(c * (SEQLEN // 2), SEQLEN // 2), SEQLEN // 2)]
        pltpu.make_async_copy(half, half, kr_sem.at[p]).wait()
        copy = remote(half, half, fs_sem.at[p], fr_sem.at[p], sib, f)
        copy.start()
        shares.append(copy)

    for copy in load_w:
        copy.wait()
    begin(0)
    load_x.wait()
    give_x = remote(xs.at[own_tok], xs.at[own_tok], xr_sem.at[0], xr_sem.at[1], sib, f)
    give_x.start()

    own_seq = pl.ds(pl.multiple_of(s * TOK, TOK), TOK)
    own_head = pl.ds(pl.multiple_of(s * HD, HD), HD)
    keep = []
    for i, (src, dst) in enumerate(((q_ref, qh_ref), (g_ref, gh_ref))):
        keep.append(pltpu.make_async_copy(src.at[:, own_head], dst.at[own_seq], ql_sem.at[i]))
        keep[-1].start()
    for step in range(1, 2 * NZ):
        to = ring(s + step, 2 * NZ)
        head = pl.ds(pl.multiple_of(to * HD, HD), HD)
        for i, (src, dst) in enumerate(((q_ref, qh_ref), (g_ref, gh_ref))):
            remote(src.at[:, head], dst.at[own_seq], qs_sem.at[i], qr_sem.at[i], to, f).start()

    near_first(0)
    begin(1)
    near_second(0)
    far_first(0)
    near_first(1)
    rest_second(0)
    near_second(1)
    far_first(1)
    finish(0)
    give_x.wait_recv()
    project(0)
    rest_second(1)
    finish(1)
    project(1)
    share(0)
    for copy in sends:
        copy.wait_send()
    give_x.wait_send()
    for copy in keep:
        copy.wait()
    for i, dst in enumerate((qh_ref, gh_ref)):
        others = dst.at[pl.ds(0, SEQLEN - TOK)]
        pltpu.make_async_copy(others, others, qs_sem.at[i]).wait()
        pltpu.make_async_copy(others, others, qr_sem.at[i]).wait()
    share(1)
    for k in range(8):
        mine, _, away = kv_copy(k)

        @pl.when(jnp.logical_not(mine))
        def _():
            away.wait_send()

    for copy in shares:
        copy.wait()


def k1(x, q, w, g, cosine, sine):
    dma = pltpu.SemaphoreType.DMA
    seq_block = jax.ShapeDtypeStruct((SEQLEN, HD), BF)
    return pl.pallas_call(
        k1_kernel,
        out_shape=(
            seq_block,
            seq_block,
            jax.ShapeDtypeStruct((2, SEQLEN, HD), BF),
            jax.ShapeDtypeStruct((CTOK, D), BF),
            jax.ShapeDtypeStruct((D, HALF), BF),
        ),
        in_specs=[HBM, HBM, HBM, HBM, VM, VM],
        out_specs=(VM, VM, VM, VM, VM),
        scratch_shapes=[
            pltpu.VMEM((8, CTOK, HD), BF),
            dma((8,)),
            dma(()),
            dma((2,)),
            dma((80,)),
            dma((2, 2, 4, 4, 2)),
            dma((2,)),
            dma((2,)),
            dma((2,)),
            dma((8,)),
            dma((2,)),
            dma((2,)),
            dma((2,)),
        ],
        compiler_params=pltpu.CompilerParams(
            collective_id=0, has_side_effects=True, vmem_limit_bytes=16 << 20
        ),
        name="gather_project",
    )(x, q, w, g, cosine, sine)


QT = 256
KT = 256
NT = (((1,), (1,)), ((), ()))


LOG2E = 1.4426950408889634


def k2_kernel(len_ref, q_ref, g_ref, kv_ref, o_ref, dkv_ref, vt, wbuf, tbuf, dk, dv):
    ends = []
    total = 0
    for i in range(NDOC):
        total = total + len_ref[i]
        ends.append(total)
    dk[...] = jnp.zeros_like(dk)
    dv[...] = jnp.zeros_like(dv)

    def flip(i, carry):
        rows = pl.ds(pl.multiple_of(i * KT, KT), KT)
        vt[:, rows] = kv_ref[1, rows, :].T
        return carry

    lax.fori_loop(0, SEQLEN // KT, flip, 0)

    def one_tile(i, carry):
        base = i * QT
        rows = pl.ds(pl.multiple_of(base, QT), QT)
        pos = base + lax.broadcasted_iota(jnp.int32, (1, QT), 1)
        start = jnp.zeros((1, QT), jnp.int32)
        first = jnp.int32(0)
        for end in ends:
            start = jnp.where(pos >= end, end, start)
            first = jnp.where(base >= end, end, first)
        low = jnp.maximum(start, pos - (WIN - 1))
        first = jnp.maximum(first, base - (WIN - 1)) // KT
        count = i + 1 - first
        for n in range(1, 6):

            @pl.when(count == n)
            def _():
                qt = q_ref[rows, :]
                gt = g_ref[rows, :]
                acc = jnp.zeros((HD, QT), F32)
                norm = jnp.zeros((1, QT), F32)
                key = lax.broadcasted_iota(jnp.int32, (KT, QT), 0)
                spans = []
                for j in range(n):
                    spans.append(pl.ds(pl.multiple_of((first + j) * KT, KT), KT))
                for j in range(n):
                    st = lax.dot_general(
                        kv_ref[0, spans[j], :], qt, NT, preferred_element_type=F32
                    )
                    squashed = jnp.tanh(st * (SCALE / CAP))
                    allowed = key >= low - (first + j) * KT
                    if j == n - 1:
                        allowed = allowed & (key <= pos - (first + j) * KT)
                    weight = jnp.where(allowed, jnp.exp2((CAP * LOG2E) * squashed), 0.0)
                    short = weight.astype(BF)
                    norm = norm + jnp.sum(weight, axis=0, keepdims=True)
                    wbuf[j] = weight * (1.0 - squashed * squashed)
                    tbuf[j] = short
                    acc = acc + jnp.dot(vt[:, spans[j]], short, preferred_element_type=F32)
                inverse = 1.0 / norm
                out_t = (acc * inverse).astype(BF)
                o_ref[rows, :] = out_t.T
                gt_t = gt.astype(F32).T
                delta = jnp.sum(gt_t * out_t.astype(F32), axis=0, keepdims=True)
                scaled = (gt_t * inverse).T.astype(BF)
                for j in range(n):
                    dprob = lax.dot_general(
                        kv_ref[1, spans[j], :], gt, NT, preferred_element_type=F32
                    )
                    dscore = (wbuf[j] * inverse * (dprob - delta)).astype(BF)
                    dk[spans[j], :] += jnp.dot(dscore, qt, preferred_element_type=F32)
                    dv[spans[j], :] += jnp.dot(tbuf[j], scaled, preferred_element_type=F32)

        return carry

    lax.fori_loop(0, SEQLEN // QT, one_tile, 0)
    dkv_ref[0] = (dk[...] * SCALE).astype(BF)
    dkv_ref[1] = dv[...].astype(BF)


def k2(lengths, qh, gh, kv):
    return pl.pallas_call(
        k2_kernel,
        out_shape=(
            jax.ShapeDtypeStruct((SEQLEN, HD), BF),
            jax.ShapeDtypeStruct((2, SEQLEN, HD), BF),
        ),
        in_specs=[pl.BlockSpec(memory_space=pltpu.SMEM), VM, VM, VM],
        out_specs=(VM, VM),
        scratch_shapes=[
            pltpu.VMEM((HD, SEQLEN), BF),
            pltpu.VMEM((5, KT, QT), F32),
            pltpu.VMEM((5, KT, QT), BF),
            pltpu.VMEM((SEQLEN, HD), F32),
            pltpu.VMEM((SEQLEN, HD), F32),
        ],
        compiler_params=pltpu.CompilerParams(vmem_limit_bytes=16 << 20),
        name="attend",
    )(lengths, qh, gh, kv)


def k3_kernel(
    o_ref,
    dkv_ref,
    xs_ref,
    wv,
    cos_ref,
    sin_ref,
    out_ref,
    gin_ref,
    gw_ref,
    xt,
    theirs,
    total,
    got,
    dd,
    gi,
    gsend,
    grecv,
    part_sum,
    r1,
    r2,
    second,
    r3,
    third,
    zr,
    sib_sem,
    ds_sem,
    dr_sem,
    ol_sem,
    os_sem,
    or_sem,
    g_sem,
    s1_sem,
    r1_sem,
    s2_sem,
    r2_sem,
    s3_sem,
    r3_sem,
    zs_sem,
    zr_sem,
):
    s, f, z, c, x, y = where_am_i()
    sib = s + 1 - 2 * c
    enter(s, f, x, y)
    part_seq = SEQLEN // 2
    swap = remote(
        dkv_ref.at[:, pl.ds(pl.multiple_of((1 - c) * part_seq, part_seq), part_seq)],
        theirs,
        sib_sem.at[0],
        sib_sem.at[1],
        sib,
        f,
    )
    swap.start()

    def turn(i, carry):
        cols = pl.ds(pl.multiple_of(i * 256, 256), 256)
        xt[cols, :] = xs_ref[:, cols].T
        return carry

    lax.fori_loop(0, D // 256, turn, 0)
    swap.wait_recv()

    def d_copy(kind, j):
        chip = 4 * c + j
        rows = pl.ds(j * CTOK, CTOK)
        to = 2 * chip + lax.rem(z, 2)
        slot = 4 * kind + z // 2
        src = total.at[kind, rows]
        local = pltpu.make_async_copy(src, got.at[slot], dr_sem.at[kind])
        away = remote(src, got.at[slot], ds_sem.at[kind, j], dr_sem.at[kind], to, f)
        return to == s, local, away

    def add_up(kind):
        for j in range(4):
            there = pl.ds(pl.multiple_of((4 * c + j) * CTOK, CTOK), CTOK)
            rows = pl.ds(j * CTOK, CTOK)
            total[kind, rows, :] = (
                dkv_ref[kind, there, :].astype(F32) + theirs[kind, rows, :].astype(F32)
            ).astype(BF)

    def send_out(kind):
        for j in range(4):
            mine, local, away = d_copy(kind, j)

            @pl.when(mine)
            def _():
                local.start()

            @pl.when(jnp.logical_not(mine))
            def _():
                away.start()

    def take_in(kind):
        blocks = got.at[pl.ds(4 * kind, 4)]
        pltpu.make_async_copy(blocks, blocks, dr_sem.at[kind]).wait()
        for k in range(4 * kind, 4 * kind + 4):
            block = got[k]
            if kind == 0:
                block = rotated(block.astype(F32), cos_ref[...], -sin_ref[...]).astype(BF)
            dd[:, k * HD : (k + 1) * HD] = block

    wide = PART // 2

    def chunk(p, part, a):
        cols = pl.ds(p * PART + part * wide, wide)
        for j in range(4):
            cx, cy = (a, j) if part == 0 else (j, a)
            rows = pl.ds(pl.multiple_of((cx * NY + cy) * ROWS, 16), ROWS)
            part_sum[p, part, cx, cy] = jnp.dot(
                xt[rows, :], dd[:, cols], preferred_element_type=F32
            ).astype(BF)

    def chunk_ref(p, part, a, cols):
        if part == 0:
            return part_sum.at[p, part, a, :, :, cols]
        return part_sum.at[p, part, :, a, :, cols]

    first_axis = (x, y)
    second_axis = (y, x)

    def neighbour(part, level, d):
        if (part == 0) == (level == 0):
            return ring(x + d, NX) * NY + y
        return x * NY + ring(y + d, NY)

    halves = (pl.ds(0, wide // 2), pl.ds(wide // 2, wide // 2))
    full = pl.ds(0, wide)
    dirs = (1, -1)
    sent = []

    def landed(ref, sem):
        pltpu.make_async_copy(ref, ref, sem).wait()

    def go(src, dst, send, recv, to_f):
        copy = remote(src, dst, send, recv, s, to_f)
        copy.start()
        sent.append(copy)

    def far(p):
        for part in range(2):
            a = ring(first_axis[part] + 2, 4)
            chunk(p, part, a)
            for h, d in enumerate(dirs):
                go(
                    chunk_ref(p, part, a, halves[h]),
                    r1.at[p, part, h],
                    s1_sem.at[p, part, h],
                    r1_sem.at[p, part, h],
                    neighbour(part, 0, d),
                )

    def near(p):
        for part in range(2):
            for d in (1, -1, 0):
                chunk(p, part, ring(first_axis[part] + d, 4))

    def hop(p):
        for h, d in enumerate(dirs):
            for part in range(2):
                a = ring(first_axis[part] + d, 4)
                landed(r1.at[p, part, h], r1_sem.at[p, part, h])
                cols = slice(h * (wide // 2), (h + 1) * (wide // 2))
                for j in range(4):
                    idx = (p, part, a, j) if part == 0 else (p, part, j, a)
                    idx = idx + (slice(None), cols)
                    part_sum[idx] = (
                        part_sum[idx].astype(F32) + r1[p, part, h, j].astype(F32)
                    ).astype(BF)
                go(
                    chunk_ref(p, part, a, full),
                    r2.at[p, part, h],
                    s2_sem.at[p, part, h],
                    r2_sem.at[p, part, h],
                    neighbour(part, 0, d),
                )

    def across(p):
        for part in range(2):
            for h in range(2):
                landed(r2.at[p, part, h], r2_sem.at[p, part, h])
            for j in range(4):
                idx = (p, part, x, j) if part == 0 else (p, part, j, y)
                second[p, part, j] = (
                    part_sum[idx].astype(F32)
                    + r2[p, part, 0, j].astype(F32)
                    + r2[p, part, 1, j].astype(F32)
                ).astype(BF)
            for i, d in enumerate((2, 1, -1)):
                go(
                    second.at[p, part, ring(second_axis[part] + d, 4)],
                    r3.at[p, part, i],
                    s3_sem.at[p, part, i],
                    r3_sem.at[p, part, i],
                    neighbour(part, 1, d),
                )

    def z_copy(p, j):
        chip = 4 * p + j
        return chip != z, remote(
            third.at[chip], zr.at[z], zs_sem.at[chip], zr_sem, 2 * chip + c, f
        )

    def along(p):
        for part in range(2):
            acc = second[p, part, second_axis[part]].astype(F32)
            for i in range(3):
                landed(r3.at[p, part, i], r3_sem.at[p, part, i])
                acc = acc + r3[p, part, i].astype(F32)
            for k in range(2):
                j = 2 * part + k
                third[4 * p + j] = acc[:, k * HD : (k + 1) * HD].astype(BF)
                away, copy = z_copy(p, j)

                @pl.when(away)
                def _():
                    copy.start()

    add_up(0)
    send_out(0)
    add_up(1)
    take_in(0)
    send_out(1)
    far(0)
    near(0)
    hop(0)
    take_in(1)
    own_head = pl.ds(pl.multiple_of(s * HD, HD), HD)
    own_seq = pl.ds(pl.multiple_of(s * TOK, TOK), TOK)
    keep_o = pltpu.make_async_copy(o_ref.at[own_seq], out_ref.at[:, own_head], ol_sem)
    far(1)
    keep_o.start()
    for step in range(1, 2 * NZ):
        to = ring(s + step, 2 * NZ)
        theirs_tok = pl.ds(pl.multiple_of(to * TOK, TOK), TOK)
        remote(
            o_ref.at[theirs_tok], out_ref.at[:, own_head], os_sem, or_sem, to, f
        ).start()
    near(1)
    across(0)
    hop(1)

    def input_tile(i, carry):
        rows = pl.ds(pl.multiple_of(i * 256, 256), 256)
        gi[:, rows] = lax.dot_general(dd[...], wv[rows, :], NT, preferred_element_type=F32)
        return carry

    lax.fori_loop(0, D // 256, input_tile, 0)
    other_tok = pl.ds(pl.multiple_of((1 - c) * TOK, TOK), TOK)
    own_tok = pl.ds(pl.multiple_of(c * TOK, TOK), TOK)
    gsend[...] = gi[other_tok, :].astype(BF)
    give = remote(gsend, grecv, g_sem.at[0], g_sem.at[1], sib, f)
    give.start()
    along(0)
    give.wait()
    gin_ref[...] = (gi[own_tok, :] + grecv[...].astype(F32)).astype(BF)
    across(1)
    along(1)
    for copy in sent:
        copy.wait_send()
    swap.wait_send()
    for kind in range(2):
        for j in range(4):
            mine, _, away = d_copy(kind, j)

            @pl.when(jnp.logical_not(mine))
            def _():
                away.wait_send()

    keep_o.wait()
    others = o_ref.at[pl.ds(0, SEQLEN - TOK)]
    landed(others, os_sem)
    landed(others, or_sem)
    for p in range(2):
        for j in range(4):
            away, copy = z_copy(p, j)

            @pl.when(away)
            def _():
                copy.wait_send()

    rest = zr.at[pl.ds(1, NZ - 1)]
    landed(rest, zr_sem)
    acc = third[z].astype(F32)
    for step in range(1, NZ):
        acc = acc + zr[ring(z + step, NZ)].astype(F32)
    gw_ref[...] = acc


def k3(o, dkv, xs, wh, cosine, sine):
    dma = pltpu.SemaphoreType.DMA
    wide = PART // 2
    return pl.pallas_call(
        k3_kernel,
        out_shape=(
            jax.ShapeDtypeStruct((TOK, 2048), BF),
            jax.ShapeDtypeStruct((TOK, D), BF),
            jax.ShapeDtypeStruct((ROWS, HD), F32),
        ),
        in_specs=[VM, VM, VM, VM, VM, VM],
        out_specs=(VM, VM, VM),
        scratch_shapes=[
            pltpu.VMEM((D, CTOK), BF),
            pltpu.VMEM((2, SEQLEN // 2, HD), BF),
            pltpu.VMEM((2, SEQLEN // 2, HD), BF),
            pltpu.VMEM((8, CTOK, HD), BF),
            pltpu.VMEM((CTOK, HALF), BF),
            pltpu.VMEM((CTOK, D), F32),
            pltpu.VMEM((TOK, D), BF),
            pltpu.VMEM((TOK, D), BF),
            pltpu.VMEM((2, 2, 4, 4, ROWS, wide), BF),
            pltpu.VMEM((2, 2, 2, 4, ROWS, wide // 2), BF),
            pltpu.VMEM((2, 2, 2, 4, ROWS, wide), BF),
            pltpu.VMEM((2, 2, 4, ROWS, wide), BF),
            pltpu.VMEM((2, 2, 3, ROWS, wide), BF),
            pltpu.VMEM((8, ROWS, HD), BF),
            pltpu.VMEM((8, ROWS, HD), BF),
            dma((2,)),
            dma((2, 4)),
            dma((2,)),
            dma(()),
            dma(()),
            dma(()),
            dma((2,)),
            dma((2, 2, 2)),
            dma((2, 2, 2)),
            dma((2, 2, 2)),
            dma((2, 2, 2)),
            dma((2, 2, 3)),
            dma((2, 2, 3)),
            dma((8,)),
            dma(()),
        ],
        compiler_params=pltpu.CompilerParams(
            collective_id=1, has_side_effects=True, vmem_limit_bytes=28 << 20
        ),
        name="gradients",
    )(o, dkv, xs, wh, cosine, sine)


def tables(lengths):
    z = lax.axis_index("seq") // 2
    places = z * CTOK + jnp.arange(CTOK, dtype=jnp.int32)
    order = jnp.arange(NDOC)
    doc_ends = jnp.sum(jnp.where(order[:, None] <= order[None, :], lengths[:, None], 0), axis=0)
    ended = doc_ends[None, :] <= places[:, None]
    within = places - jnp.sum(jnp.where(ended, lengths[None, :], 0), axis=1)
    exponent = jnp.arange(HD // 2, dtype=F32) * (2.0 / HD)
    rate = jnp.power(ROPE_BASE, -exponent)
    angles = within.astype(F32)[:, None] * rate[None, :]
    cosine, sine = jnp.cos(angles), jnp.sin(angles)
    return (
        jnp.concatenate([cosine, cosine], axis=1),
        jnp.concatenate([-sine, sine], axis=1),
    )


def on_device(inputs, queries, w_kv, doc_lengths, grad_out):
    cosine, sine = tables(doc_lengths[0])
    held = [
        pltpu.with_memory_space_constraint(a, pltpu.HBM)
        for a in (inputs[0], queries[0], w_kv, grad_out[0])
    ]
    qh, gh, kv, xs, wh = k1(*held, cosine, sine)
    o, dkv = k2(doc_lengths[0], qh, gh, kv)
    out, gin, gw = k3(o, dkv, xs, wh, cosine, sine)
    return out[None], gin[None], gw


def solution(mesh):
    in_specs = (
        P("fsdp", "seq", None),
        P("fsdp", "seq", None),
        P("fsdp", None),
        P("fsdp", None),
        P("fsdp", "seq", None),
    )
    out_specs = (P("fsdp", "seq", None), P("fsdp", "seq", None), P("fsdp", "seq"))
    return jax.shard_map(
        on_device, mesh=mesh, in_specs=in_specs, out_specs=out_specs, check_vma=False
    )
```

```python
import functools

import jax
import jax.numpy as jnp
from jax import lax
from jax.experimental import pallas as pl
from jax.experimental.pallas import tpu as pltpu
from jax.sharding import PartitionSpec as P

D = 2304
HD = 128
WIN = 1024
SEQLEN = 2048
NDOC = 8
NZ = 8
NX = 4
NY = 4
ROWS = D // (NX * NY)
HALF = 1024
PART = 512
TOK = 128
CTOK = 256
CAP = 50.0
SCALE = 1.0 / 12.0
ROPE_BASE = 10000.0
MESH = pl.DeviceIdType.MESH
HBM = pl.BlockSpec(memory_space=pltpu.HBM)
VM = pl.BlockSpec(memory_space=pltpu.VMEM)
BF = jnp.bfloat16
F32 = jnp.float32


def where_am_i():
    s = lax.axis_index("seq")
    f = lax.axis_index("fsdp")
    z = s // 2
    c = s - 2 * z
    x = f // NY
    y = f - NY * x
    return s, f, z, c, x, y


def ring(v, n):
    return lax.rem(v + n, n)


def remote(src, dst, send, recv, s, f):
    return pltpu.make_async_remote_copy(
        src_ref=src,
        dst_ref=dst,
        send_sem=send,
        recv_sem=recv,
        device_id={"seq": s, "fsdp": f},
        device_id_type=MESH,
    )


def enter(s, f, x, y):
    barrier = pltpu.get_barrier_semaphore()
    for step in range(1, 2 * NZ):
        pl.semaphore_signal(
            barrier,
            inc=1,
            device_id={"seq": ring(s + step, 2 * NZ), "fsdp": f},
            device_id_type=MESH,
        )
    for dx, dy in ((1, 0), (-1, 0), (0, 1), (0, -1)):
        pl.semaphore_signal(
            barrier,
            inc=1,
            device_id={"seq": s, "fsdp": ring(x + dx, NX) * NY + ring(y + dy, NY)},
            device_id_type=MESH,
        )
    pl.semaphore_wait(barrier, 2 * NZ - 1 + 4)


def other_chip(s, z):
    return s + 2 - 4 * lax.rem(z, 2)


def rotated(values, cosine, sine):
    return values * cosine + pltpu.roll(values, HD // 2, 1) * sine


def k1_kernel(
    x_ref,
    q_ref,
    w_ref,
    g_ref,
    cos_ref,
    sin_ref,
    qh_ref,
    gh_ref,
    kv_ref,
    xt_ref,
    xp_ref,
    wg,
    xs,
    xp,
    proj,
    wl_sem,
    xl_sem,
    xr_sem,
    xp_sem,
    ws_sem,
    wr_sem,
    ql_sem,
    qs_sem,
    qr_sem,
    ks_sem,
    kr_sem,
    fs_sem,
    fr_sem,
):
    s, f, z, c, x, y = where_am_i()
    sib = s + 1 - 2 * c
    own_rows = pl.ds(pl.multiple_of(f * ROWS, 16), ROWS)
    load_w = []
    for k in range(8):
        cols = pl.ds(pl.multiple_of((2 * k + c) * HD, HD), HD)
        load_w.append(
            pltpu.make_async_copy(
                w_ref.at[:, cols], wg.at[own_rows, pl.ds(k * HD, HD)], wl_sem.at[k]
            )
        )
    for copy in load_w:
        copy.start()
    own_tok = pl.ds(pl.multiple_of(c * TOK, TOK), TOK)
    load_x = pltpu.make_async_copy(x_ref, xs.at[own_tok], xl_sem)
    load_x.start()
    enter(s, f, x, y)

    wide = PART // 2

    def piece(phase, part, off, half):
        origin = ring(x + off[0], NX) * NY + ring(y + off[1], NY)
        rows = pl.ds(pl.multiple_of(origin * ROWS, 16), ROWS)
        base = phase * PART + part * wide
        if half is None:
            return wg.at[rows, pl.ds(base, wide)]
        return wg.at[rows, pl.ds(base + half * (wide // 2), wide // 2)]

    sends = []

    def pass_on(phase, part, off, step, half=None):
        there = tuple((o - d) % 4 for o, d in zip(off, step))
        there = tuple(-1 if t == 3 else t for t in there)
        ref = piece(phase, part, off, half)
        copy = remote(
            ref,
            ref,
            ws_sem.at[len(sends)],
            wr_sem.at[phase, part, there[0] + 1, there[1] + 1, half or 0],
            s,
            ring(x + step[0], NX) * NY + ring(y + step[1], NY),
        )
        copy.start()
        sends.append(copy)

    def arrived(phase, part, off, half=None):
        ref = piece(phase, part, off, half)
        sem = wr_sem.at[phase, part, off[0] + 1, off[1] + 1, half or 0]
        pltpu.make_async_copy(ref, ref, sem).wait()

    def at(part, a, b):
        return (a, b) if part == 0 else (b, a)

    def begin(p):
        for d in (1, -1):
            for part in range(2):
                pass_on(p, part, (0, 0), at(part, d, 0))
        for d in (1, -1):
            for part in range(2):
                pass_on(p, part, (0, 0), at(part, 0, d))

    def near_first(p):
        for d in (-1, 1):
            for part in range(2):
                arrived(p, part, at(part, d, 0))
                pass_on(p, part, at(part, d, 0), at(part, -d, 0), 0 if d < 0 else 1)
                for e in (1, -1):
                    pass_on(p, part, at(part, d, 0), at(part, 0, e))

    def near_second(p):
        for d in (-1, 1):
            for part in range(2):
                arrived(p, part, at(part, 0, d))
                pass_on(p, part, at(part, 0, d), at(part, 0, -d), 0 if d < 0 else 1)

    def far_first(p):
        for part in range(2):
            arrived(p, part, at(part, 2, 0), 0)
            arrived(p, part, at(part, 2, 0), 1)
            for e in (1, -1):
                pass_on(p, part, at(part, 2, 0), at(part, 0, e))

    def rest_second(p):
        for a in (-1, 1, 2):
            for d in (-1, 1):
                for part in range(2):
                    arrived(p, part, at(part, a, d))
                    pass_on(p, part, at(part, a, d), at(part, 0, -d), 0 if d < 0 else 1)

    def finish(p):
        for a in (0, -1, 1, 2):
            for part in range(2):
                arrived(p, part, at(part, a, 2), 0)
                arrived(p, part, at(part, a, 2), 1)

    def kv_copy(k):
        kind = k // 4
        to = 2 * (2 * (k % 4) + c) + z // 4
        rows = pl.ds(pl.multiple_of(z * CTOK, CTOK), CTOK)
        local = pltpu.make_async_copy(proj.at[k], kv_ref.at[kind, rows], kr_sem.at[kind])
        away = remote(proj.at[k], kv_ref.at[kind, rows], ks_sem.at[k], kr_sem.at[kind], to, f)
        return to == s, local, away

    in_pair = pl.ds(pl.multiple_of(lax.rem(z, 2) * CTOK, CTOK), CTOK)

    def project(p):
        for t in (2 * p, 2 * p + 1):
            res = jnp.dot(xs[...], wg[:, t * 256 : (t + 1) * 256], preferred_element_type=F32)
            for j in range(2):
                k = 2 * t + j
                block = res[:, j * HD : (j + 1) * HD]
                if k < 4:
                    block = rotated(block, cos_ref[in_pair, :], sin_ref[in_pair, :])
                proj[k] = block.astype(BF)
                mine, local, away = kv_copy(k)

                @pl.when(mine)
                def _():
                    local.start()

                @pl.when(jnp.logical_not(mine))
                def _():
                    away.start()

    shares = []

    def share(p):
        half = kv_ref.at[p, pl.ds(pl.multiple_of(c * (SEQLEN // 2), SEQLEN // 2), SEQLEN // 2)]
        pltpu.make_async_copy(half, half, kr_sem.at[p]).wait()
        copy = remote(half, half, fs_sem.at[p], fr_sem.at[p], sib, f)
        copy.start()
        shares.append(copy)

    for copy in load_w:
        copy.wait()
    begin(0)
    load_x.wait()
    give_x = remote(xs.at[own_tok], xs.at[own_tok], xr_sem.at[0], xr_sem.at[1], sib, f)
    give_x.start()

    own_seq = pl.ds(pl.multiple_of(s * TOK, TOK), TOK)
    own_head = pl.ds(pl.multiple_of(s * HD, HD), HD)
    keep = []
    for i, (src, dst) in enumerate(((q_ref, qh_ref), (g_ref, gh_ref))):
        keep.append(pltpu.make_async_copy(src.at[:, own_head], dst.at[own_seq], ql_sem.at[i]))
        keep[-1].start()
    for step in range(1, 2 * NZ):
        to = ring(s + step, 2 * NZ)
        head = pl.ds(pl.multiple_of(to * HD, HD), HD)
        for i, (src, dst) in enumerate(((q_ref, qh_ref), (g_ref, gh_ref))):
            remote(src.at[:, head], dst.at[own_seq], qs_sem.at[i], qr_sem.at[i], to, f).start()
    cross = remote(
        xs.at[own_tok, pl.ds(0, D // 2)],
        xp.at[own_tok],
        xp_sem.at[0],
        xp_sem.at[1],
        other_chip(s, z),
        f,
    )
    cross.start()

    near_first(0)
    begin(1)
    near_second(0)
    far_first(0)
    near_first(1)
    rest_second(0)
    near_second(1)
    far_first(1)
    finish(0)
    give_x.wait_recv()
    project(0)
    cross.wait_recv()
    spread = remote(xp.at[own_tok], xp.at[own_tok], xp_sem.at[2], xp_sem.at[3], sib, f)
    spread.start()
    rest_second(1)
    finish(1)
    project(1)
    share(0)

    def turn(i, carry):
        cols = pl.ds(pl.multiple_of(i * 256, 256), 256)
        xt_ref[cols, :] = xs[:, cols].T
        return carry

    def turn_half(i, carry):
        cols = pl.ds(pl.multiple_of(i * 128, 128), 128)
        xp_ref[cols, :] = xp[:, cols].T
        return carry

    lax.fori_loop(0, D // 256, turn, 0)
    spread.wait()
    cross.wait_send()
    lax.fori_loop(0, D // 256, turn_half, 0)
    for copy in sends:
        copy.wait_send()
    give_x.wait_send()
    for copy in keep:
        copy.wait()
    for i, dst in enumerate((qh_ref, gh_ref)):
        others = dst.at[pl.ds(0, SEQLEN - TOK)]
        pltpu.make_async_copy(others, others, qs_sem.at[i]).wait()
        pltpu.make_async_copy(others, others, qr_sem.at[i]).wait()
    share(1)
    for k in range(8):
        mine, _, away = kv_copy(k)

        @pl.when(jnp.logical_not(mine))
        def _():
            away.wait_send()

    for copy in shares:
        copy.wait()


def k1(x, q, w, g, cosine, sine):
    dma = pltpu.SemaphoreType.DMA
    seq_block = jax.ShapeDtypeStruct((SEQLEN, HD), BF)
    return pl.pallas_call(
        k1_kernel,
        out_shape=(
            seq_block,
            seq_block,
            jax.ShapeDtypeStruct((2, SEQLEN, HD), BF),
            jax.ShapeDtypeStruct((D, CTOK), BF),
            jax.ShapeDtypeStruct((D // 2, CTOK), BF),
            jax.ShapeDtypeStruct((D, HALF), BF),
        ),
        in_specs=[HBM, HBM, HBM, HBM, VM, VM],
        out_specs=(VM, VM, VM, VM, VM, VM),
        scratch_shapes=[
            pltpu.VMEM((CTOK, D), BF),
            pltpu.VMEM((CTOK, D // 2), BF),
            pltpu.VMEM((8, CTOK, HD), BF),
            dma((8,)),
            dma(()),
            dma((2,)),
            dma((4,)),
            dma((80,)),
            dma((2, 2, 4, 4, 2)),
            dma((2,)),
            dma((2,)),
            dma((2,)),
            dma((8,)),
            dma((2,)),
            dma((2,)),
            dma((2,)),
        ],
        compiler_params=pltpu.CompilerParams(
            collective_id=0, has_side_effects=True, vmem_limit_bytes=16 << 20
        ),
        name="gather_project",
    )(x, q, w, g, cosine, sine)


QT = 256
KT = 256
NT = (((1,), (1,)), ((), ()))
LOG2E = 1.4426950408889634


def k3_kernel(
    len_ref,
    q_ref,
    g_ref,
    kv_ref,
    xt,
    xp1,
    wv,
    cos_ref,
    sin_ref,
    out_ref,
    gin_ref,
    gw_ref,
    vt,
    wbuf,
    tbuf,
    dk,
    dv,
    obuf,
    dkv,
    theirs,
    total,
    got,
    dd,
    da,
    xp,
    gi,
    gsend,
    grecv,
    part_sum,
    r1,
    r2,
    second,
    r3,
    third,
    zr,
    x_sem,
    ws_sem,
    wr_sem,
    ds_sem,
    dr_sem,
    ol_sem,
    os_sem,
    or_sem,
    as_sem,
    ar_sem,
    g_sem,
    s1_sem,
    r1_sem,
    s2_sem,
    r2_sem,
    s3_sem,
    r3_sem,
    zs_sem,
    zr_sem,
):
    s, f, z, c, x, y = where_am_i()
    sib = s + 1 - 2 * c
    e = lax.rem(z, 2)
    pair = z // 2
    partner = other_chip(s, z)
    half_d = D // 2
    keep_x = pltpu.make_async_copy(xp1, xp.at[pl.ds(0, half_d)], x_sem.at[0])
    keep_x.start()
    enter(s, f, x, y)

    def landed(ref, sem):
        pltpu.make_async_copy(ref, ref, sem).wait()

    own_cols = pl.ds(pl.multiple_of(c * TOK, TOK), TOK)
    cross = remote(
        xt.at[pl.ds(half_d, half_d), own_cols],
        xp.at[pl.ds(half_d, half_d), own_cols],
        x_sem.at[1],
        x_sem.at[2],
        partner,
        f,
    )
    cross.start()
    spread = remote(
        xp.at[pl.ds(half_d, half_d), own_cols],
        xp.at[pl.ds(half_d, half_d), own_cols],
        x_sem.at[3],
        x_sem.at[4],
        sib,
        f,
    )

    ends = []
    so_far = 0
    for i in range(NDOC):
        so_far = so_far + len_ref[i]
        ends.append(so_far)
    dk[...] = jnp.zeros_like(dk)
    dv[...] = jnp.zeros_like(dv)

    def flip(i, carry):
        rows = pl.ds(pl.multiple_of(i * KT, KT), KT)
        vt[:, rows] = kv_ref[1, rows, :].T
        return carry

    lax.fori_loop(0, SEQLEN // KT, flip, 0)

    def tile_rows(i):
        return pl.ds(pl.multiple_of(i * KT, KT), KT)

    def swap(i):
        rows = tile_rows(i)
        return remote(
            dkv.at[1 - c, rows], theirs.at[rows], ws_sem.at[i], wr_sem.at[i], sib, f
        )

    def attend(i, n):
        base = i * QT
        rows = tile_rows(i)
        pos = base + lax.broadcasted_iota(jnp.int32, (1, QT), 1)
        start = jnp.zeros((1, QT), jnp.int32)
        for end in ends:
            start = jnp.where(pos >= end, end, start)
        low = jnp.maximum(start, pos - (WIN - 1))
        first = i + 1 - n
        qt = q_ref[rows, :]
        gt = g_ref[rows, :]
        acc = jnp.zeros((HD, QT), F32)
        norm = jnp.zeros((1, QT), F32)
        key = lax.broadcasted_iota(jnp.int32, (KT, QT), 0)
        spans = [tile_rows(first + j) for j in range(n)]
        for j in range(n):
            st = lax.dot_general(kv_ref[0, spans[j], :], qt, NT, preferred_element_type=F32)
            squashed = jnp.tanh(st * (SCALE / CAP))
            allowed = key >= low - (first + j) * KT
            if j == n - 1:
                allowed = allowed & (key <= pos - (first + j) * KT)
            weight = jnp.where(allowed, jnp.exp2((CAP * LOG2E) * squashed), 0.0)
            short = weight.astype(BF)
            norm = norm + jnp.sum(weight, axis=0, keepdims=True)
            wbuf[j] = weight * (1.0 - squashed * squashed)
            tbuf[j] = short
            acc = acc + jnp.dot(vt[:, spans[j]], short, preferred_element_type=F32)
        inverse = 1.0 / norm
        out_t = (acc * inverse).astype(BF)
        obuf[rows, :] = out_t.T
        gt_t = gt.astype(F32).T
        delta = jnp.sum(gt_t * out_t.astype(F32), axis=0, keepdims=True)
        scaled = (gt_t * inverse).T.astype(BF)
        for j in range(n):
            dprob = lax.dot_general(kv_ref[1, spans[j], :], gt, NT, preferred_element_type=F32)
            dscore = (wbuf[j] * inverse * (dprob - delta)).astype(BF)
            dk[spans[j], :] += jnp.dot(dscore, qt, preferred_element_type=F32)
            dv[spans[j], :] += jnp.dot(tbuf[j], scaled, preferred_element_type=F32)
        dkv[0, rows, :] = (dk[rows, :] * SCALE).astype(BF)
        dkv[1, rows, :] = dv[rows, :].astype(BF)
        swap(i).start()

    head_dev = lax.rem(z, 4)

    def d_copy(i):
        rows = tile_rows(i)
        to = 4 * (i // 2) + head_dev
        dst = got.at[2 * c + z // 4, pl.ds(pl.multiple_of(lax.rem(i, 2) * CTOK, CTOK), CTOK)]
        local = pltpu.make_async_copy(total.at[rows], dst, dr_sem.at[c])
        away = remote(total.at[rows], dst, ds_sem.at[i], dr_sem.at[c], to, f)
        return to == s, local, away

    def hand_over(i):
        rows = tile_rows(i)
        landed(theirs.at[rows], wr_sem.at[i])
        total[rows, :] = (dkv[c, rows, :].astype(F32) + theirs[rows, :].astype(F32)).astype(BF)
        mine, local, away = d_copy(i)

        @pl.when(mine)
        def _():
            local.start()

        @pl.when(jnp.logical_not(mine))
        def _():
            away.start()

    def long_tile(k, carry):
        i = SEQLEN // QT - 1 - k
        attend(i, 5)

        @pl.when(k > 0)
        def _():
            hand_over(i + 1)

        return carry

    lax.fori_loop(0, 4, long_tile, 0)
    for i in (3, 2, 1, 0):
        attend(jnp.int32(i), i + 1)
        hand_over(jnp.int32(i + 1))
        if i == 2:
            cross.wait_recv()
            spread.start()
    hand_over(jnp.int32(0))

    own_head = pl.ds(pl.multiple_of(s * HD, HD), HD)
    own_seq = pl.ds(pl.multiple_of(s * TOK, TOK), TOK)
    keep_o = pltpu.make_async_copy(obuf.at[own_seq], out_ref.at[:, own_head], ol_sem)
    keep_o.start()
    for step in range(1, 2 * NZ):
        to = ring(s + step, 2 * NZ)
        theirs_tok = pl.ds(pl.multiple_of(to * TOK, TOK), TOK)
        remote(
            obuf.at[theirs_tok], out_ref.at[:, own_head], os_sem, or_sem, to, f
        ).start()
    keep_x.wait()
    spread.wait_recv()

    own_tok = pl.ds(pl.multiple_of(e * CTOK, CTOK), CTOK)
    pair_tok = pl.ds(pl.multiple_of((1 - e) * CTOK, CTOK), CTOK)

    def a_cols(b, side):
        return pl.ds(pl.multiple_of((side + 2 * b) * HD, HD), HD)

    def a_copy(b):
        return remote(
            dd.at[b, pair_tok], da.at[:, a_cols(b, e)], as_sem.at[b], ar_sem.at[b], partner, f
        )

    def take_in(kind):
        blocks = got.at[pl.ds(2 * kind, 2)]
        landed(blocks, dr_sem.at[kind])
        for b in range(2 * kind, 2 * kind + 2):
            block = got[b]
            if kind == 0:
                block = rotated(block.astype(F32), cos_ref[...], -sin_ref[...]).astype(BF)
            dd[b] = block

    def trade(kind):
        for b in range(2 * kind, 2 * kind + 2):
            a_copy(b).start()
            da[:, a_cols(b, e)] = dd[b, own_tok, :]

    def chunk(p, part, a):
        for j in range(4):
            cx, cy = (a, j) if part == 0 else (j, a)
            rows = pl.ds(pl.multiple_of((cx * NY + cy) * ROWS, 16), ROWS)
            part_sum[p, part, cx, cy] = (
                jnp.dot(xt[rows, :], dd[2 * p + part, own_tok, :], preferred_element_type=F32)
                + jnp.dot(xp[rows, :], dd[2 * p + part, pair_tok, :], preferred_element_type=F32)
            ).astype(BF)

    def chunk_ref(p, part, a, which):
        if part == 0:
            return part_sum.at[p, part, a, which]
        return part_sum.at[p, part, which, a]

    first_axis = (x, y)
    second_axis = (y, x)

    def neighbour(part, level, d):
        if (part == 0) == (level == 0):
            return ring(x + d, NX) * NY + y
        return x * NY + ring(y + d, NY)

    halves = (pl.ds(0, 2), pl.ds(2, 2))
    full = pl.ds(0, 4)
    dirs = (1, -1)
    sent = []

    def go(src, dst, send, recv, to_f):
        copy = remote(src, dst, send, recv, s, to_f)
        copy.start()
        sent.append(copy)

    def far(p):
        for part in range(2):
            a = ring(first_axis[part] + 2, 4)
            chunk(p, part, a)
            for h, d in enumerate(dirs):
                go(
                    chunk_ref(p, part, a, halves[h]),
                    r1.at[p, part, h],
                    s1_sem.at[p, part, h],
                    r1_sem.at[p, part, h],
                    neighbour(part, 0, d),
                )

    def near(p):
        for part in range(2):
            for d in (1, -1, 0):
                chunk(p, part, ring(first_axis[part] + d, 4))

    def hop(p):
        for h, d in enumerate(dirs):
            for part in range(2):
                a = ring(first_axis[part] + d, 4)
                landed(r1.at[p, part, h], r1_sem.at[p, part, h])
                for k in range(2):
                    j = 2 * h + k
                    idx = (p, part, a, j) if part == 0 else (p, part, j, a)
                    part_sum[idx] = (
                        part_sum[idx].astype(F32) + r1[p, part, h, k].astype(F32)
                    ).astype(BF)
                go(
                    chunk_ref(p, part, a, full),
                    r2.at[p, part, h],
                    s2_sem.at[p, part, h],
                    r2_sem.at[p, part, h],
                    neighbour(part, 0, d),
                )

    def across(p):
        for part in range(2):
            for h in range(2):
                landed(r2.at[p, part, h], r2_sem.at[p, part, h])
            for j in range(4):
                idx = (p, part, x, j) if part == 0 else (p, part, j, y)
                second[p, part, j] = (
                    part_sum[idx].astype(F32)
                    + r2[p, part, 0, j].astype(F32)
                    + r2[p, part, 1, j].astype(F32)
                ).astype(BF)
            for i, d in enumerate((2, 1, -1)):
                go(
                    second.at[p, part, ring(second_axis[part] + d, 4)],
                    r3.at[p, part, i],
                    s3_sem.at[p, part, i],
                    r3_sem.at[p, part, i],
                    neighbour(part, 1, d),
                )

    def z_copy(b):
        to = 2 * (2 * b + e) + c
        return pair != b, remote(third.at[b], zr.at[pair], zs_sem.at[b], zr_sem, to, f)

    def along(p):
        for part in range(2):
            b = 2 * p + part
            acc = second[p, part, second_axis[part]].astype(F32)
            for i in range(3):
                landed(r3.at[p, part, i], r3_sem.at[p, part, i])
                acc = acc + r3[p, part, i].astype(F32)
            third[b] = acc.astype(BF)
            away, copy = z_copy(b)

            @pl.when(away)
            def _():
                copy.start()

    take_in(0)
    far(0)
    near(0)
    take_in(1)
    far(1)
    trade(0)
    trade(1)
    hop(0)
    near(1)
    hop(1)
    across(0)

    for b in range(4):
        landed(da.at[:, a_cols(b, 1 - e)], ar_sem.at[b])

    def input_tile(i, carry):
        rows = pl.ds(pl.multiple_of(i * 256, 256), 256)
        gi[:, rows] = lax.dot_general(da[...], wv[rows, :], NT, preferred_element_type=F32)
        return carry

    lax.fori_loop(0, D // 256, input_tile, 0)
    mine_tok = pl.ds(pl.multiple_of(c * TOK, TOK), TOK)
    sib_tok = pl.ds(pl.multiple_of((1 - c) * TOK, TOK), TOK)
    gsend[...] = gi[sib_tok, :].astype(BF)
    give = remote(gsend, grecv, g_sem.at[0], g_sem.at[1], sib, f)
    give.start()
    along(0)
    across(1)
    give.wait()
    gin_ref[...] = (gi[mine_tok, :] + grecv[...].astype(F32)).astype(BF)
    along(1)
    for copy in sent:
        copy.wait_send()
    cross.wait_send()
    spread.wait_send()
    for b in range(4):
        a_copy(b).wait_send()

    def settle(i, carry):
        swap(i).wait_send()
        mine, _, away = d_copy(i)

        @pl.when(jnp.logical_not(mine))
        def _():
            away.wait_send()

        return carry

    lax.fori_loop(0, SEQLEN // QT, settle, 0)
    keep_o.wait()
    others = obuf.at[pl.ds(0, SEQLEN - TOK)]
    landed(others, os_sem)
    landed(others, or_sem)
    for b in range(4):
        away, copy = z_copy(b)

        @pl.when(away)
        def _():
            copy.wait_send()

    rest = zr.at[pl.ds(1, 3)]
    landed(rest, zr_sem)
    acc = third[pair].astype(F32)
    for step in range(1, 4):
        acc = acc + zr[ring(pair + step, 4)].astype(F32)
    gw_ref[...] = acc


def k3(lengths, qh, gh, kv, xt, xp, wh, cosine, sine):
    dma = pltpu.SemaphoreType.DMA
    return pl.pallas_call(
        k3_kernel,
        out_shape=(
            jax.ShapeDtypeStruct((TOK, 2048), BF),
            jax.ShapeDtypeStruct((TOK, D), BF),
            jax.ShapeDtypeStruct((ROWS, HD), F32),
        ),
        in_specs=[pl.BlockSpec(memory_space=pltpu.SMEM)] + [VM] * 8,
        out_specs=(VM, VM, VM),
        scratch_shapes=[
            pltpu.VMEM((HD, SEQLEN), BF),
            pltpu.VMEM((5, KT, QT), F32),
            pltpu.VMEM((5, KT, QT), BF),
            pltpu.VMEM((SEQLEN, HD), F32),
            pltpu.VMEM((SEQLEN, HD), F32),
            pltpu.VMEM((SEQLEN, HD), BF),
            pltpu.VMEM((2, SEQLEN, HD), BF),
            pltpu.VMEM((SEQLEN, HD), BF),
            pltpu.VMEM((SEQLEN, HD), BF),
            pltpu.VMEM((4, 2 * CTOK, HD), BF),
            pltpu.VMEM((4, 2 * CTOK, HD), BF),
            pltpu.VMEM((CTOK, HALF), BF),
            pltpu.VMEM((D, CTOK), BF),
            pltpu.VMEM((CTOK, D), F32),
            pltpu.VMEM((TOK, D), BF),
            pltpu.VMEM((TOK, D), BF),
            pltpu.VMEM((2, 2, 4, 4, ROWS, HD), BF),
            pltpu.VMEM((2, 2, 2, 2, ROWS, HD), BF),
            pltpu.VMEM((2, 2, 2, 4, ROWS, HD), BF),
            pltpu.VMEM((2, 2, 4, ROWS, HD), BF),
            pltpu.VMEM((2, 2, 3, ROWS, HD), BF),
            pltpu.VMEM((4, ROWS, HD), BF),
            pltpu.VMEM((4, ROWS, HD), BF),
            dma((5,)),
            dma((8,)),
            dma((8,)),
            dma((8,)),
            dma((2,)),
            dma(()),
            dma(()),
            dma(()),
            dma((4,)),
            dma((4,)),
            dma((2,)),
            dma((2, 2, 2)),
            dma((2, 2, 2)),
            dma((2, 2, 2)),
            dma((2, 2, 2)),
            dma((2, 2, 3)),
            dma((2, 2, 3)),
            dma((4,)),
            dma(()),
        ],
        compiler_params=pltpu.CompilerParams(
            collective_id=1, has_side_effects=True, vmem_limit_bytes=32 << 20
        ),
        name="gradients",
    )(lengths, qh, gh, kv, xt, xp, wh, cosine, sine)


def tables(lengths):
    pair = lax.axis_index("seq") // 4
    places = pair * (2 * CTOK) + jnp.arange(2 * CTOK, dtype=jnp.int32)
    order = jnp.arange(NDOC)
    doc_ends = jnp.sum(jnp.where(order[:, None] <= order[None, :], lengths[:, None], 0), axis=0)
    ended = doc_ends[None, :] <= places[:, None]
    within = places - jnp.sum(jnp.where(ended, lengths[None, :], 0), axis=1)
    exponent = jnp.arange(HD // 2, dtype=F32) * (2.0 / HD)
    rate = jnp.power(ROPE_BASE, -exponent)
    angles = within.astype(F32)[:, None] * rate[None, :]
    cosine, sine = jnp.cos(angles), jnp.sin(angles)
    return (
        jnp.concatenate([cosine, cosine], axis=1),
        jnp.concatenate([-sine, sine], axis=1),
    )


def on_device(inputs, queries, w_kv, doc_lengths, grad_out):
    cosine, sine = tables(doc_lengths[0])
    held = [
        pltpu.with_memory_space_constraint(a, pltpu.HBM)
        for a in (inputs[0], queries[0], w_kv, grad_out[0])
    ]
    qh, gh, kv, xt, xp, wh = k1(*held, cosine, sine)
    out, gin, gw = k3(doc_lengths[0], qh, gh, kv, xt, xp, wh, cosine, sine)
    return out[None], gin[None], gw


def solution(mesh):
    in_specs = (
        P("fsdp", "seq", None),
        P("fsdp", "seq", None),
        P("fsdp", None),
        P("fsdp", None),
        P("fsdp", "seq", None),
    )
    out_specs = (P("fsdp", "seq", None), P("fsdp", "seq", None), P("fsdp", "seq"))
    return jax.shard_map(
        on_device, mesh=mesh, in_specs=in_specs, out_specs=out_specs, check_vma=False
    )
```

```python
import functools

import jax
import jax.numpy as jnp
from jax import lax
from jax.experimental import pallas as pl
from jax.experimental.pallas import tpu as pltpu
from jax.sharding import PartitionSpec as P

D = 2304
HD = 128
WIN = 1024
SEQLEN = 2048
NDOC = 8
NZ = 8
NX = 4
NY = 4
ROWS = D // (NX * NY)
HALF = 1024
PART = 512
TOK = 128
CTOK = 256
CAP = 50.0
SCALE = 1.0 / 12.0
ROPE_BASE = 10000.0
MESH = pl.DeviceIdType.MESH
HBM = pl.BlockSpec(memory_space=pltpu.HBM)
VM = pl.BlockSpec(memory_space=pltpu.VMEM)
BF = jnp.bfloat16
F32 = jnp.float32


def where_am_i():
    s = lax.axis_index("seq")
    f = lax.axis_index("fsdp")
    z = s // 2
    c = s - 2 * z
    x = f // NY
    y = f - NY * x
    return s, f, z, c, x, y


def ring(v, n):
    return lax.rem(v + n, n)


def remote(src, dst, send, recv, s, f):
    return pltpu.make_async_remote_copy(
        src_ref=src,
        dst_ref=dst,
        send_sem=send,
        recv_sem=recv,
        device_id={"seq": s, "fsdp": f},
        device_id_type=MESH,
    )


def enter(s, f, x, y):
    barrier = pltpu.get_barrier_semaphore()
    for step in range(1, 2 * NZ):
        pl.semaphore_signal(
            barrier,
            inc=1,
            device_id={"seq": ring(s + step, 2 * NZ), "fsdp": f},
            device_id_type=MESH,
        )
    for dx, dy in ((1, 0), (-1, 0), (0, 1), (0, -1)):
        pl.semaphore_signal(
            barrier,
            inc=1,
            device_id={"seq": s, "fsdp": ring(x + dx, NX) * NY + ring(y + dy, NY)},
            device_id_type=MESH,
        )
    pl.semaphore_wait(barrier, 2 * NZ - 1 + 4)


def other_chip(s, z):
    return s + 2 - 4 * lax.rem(z, 2)


def rotated(values, cosine, sine):
    return values * cosine + pltpu.roll(values, HD // 2, 1) * sine


def k1_kernel(
    x_ref,
    q_ref,
    w_ref,
    g_ref,
    cos_ref,
    sin_ref,
    qh_ref,
    gh_ref,
    kv_ref,
    xt_ref,
    wg,
    xs,
    proj,
    wl_sem,
    xl_sem,
    xr_sem,
    ws_sem,
    wr_sem,
    ql_sem,
    qs_sem,
    qr_sem,
    ks_sem,
    kr_sem,
    fs_sem,
    fr_sem,
):
    s, f, z, c, x, y = where_am_i()
    sib = s + 1 - 2 * c
    own_rows = pl.ds(pl.multiple_of(f * ROWS, 16), ROWS)
    load_w = []
    for k in range(8):
        cols = pl.ds(pl.multiple_of((2 * k + c) * HD, HD), HD)
        load_w.append(
            pltpu.make_async_copy(
                w_ref.at[:, cols], wg.at[own_rows, pl.ds(k * HD, HD)], wl_sem.at[k]
            )
        )
    for copy in load_w:
        copy.start()
    own_tok = pl.ds(pl.multiple_of(c * TOK, TOK), TOK)
    load_x = pltpu.make_async_copy(x_ref, xs.at[own_tok], xl_sem)
    load_x.start()
    enter(s, f, x, y)

    wide = PART // 2

    def piece(phase, part, off, half):
        origin = ring(x + off[0], NX) * NY + ring(y + off[1], NY)
        rows = pl.ds(pl.multiple_of(origin * ROWS, 16), ROWS)
        base = phase * PART + part * wide
        if half is None:
            return wg.at[rows, pl.ds(base, wide)]
        return wg.at[rows, pl.ds(base + half * (wide // 2), wide // 2)]

    sends = []

    def pass_on(phase, part, off, step, half=None):
        there = tuple((o - d) % 4 for o, d in zip(off, step))
        there = tuple(-1 if t == 3 else t for t in there)
        ref = piece(phase, part, off, half)
        copy = remote(
            ref,
            ref,
            ws_sem.at[len(sends)],
            wr_sem.at[phase, part, there[0] + 1, there[1] + 1, half or 0],
            s,
            ring(x + step[0], NX) * NY + ring(y + step[1], NY),
        )
        copy.start()
        sends.append(copy)

    def arrived(phase, part, off, half=None):
        ref = piece(phase, part, off, half)
        sem = wr_sem.at[phase, part, off[0] + 1, off[1] + 1, half or 0]
        pltpu.make_async_copy(ref, ref, sem).wait()

    def at(part, a, b):
        return (a, b) if part == 0 else (b, a)

    def begin(p):
        for d in (1, -1):
            for part in range(2):
                pass_on(p, part, (0, 0), at(part, d, 0))
        for d in (1, -1):
            for part in range(2):
                pass_on(p, part, (0, 0), at(part, 0, d))

    def near_first(p):
        for d in (-1, 1):
            for part in range(2):
                arrived(p, part, at(part, d, 0))
                pass_on(p, part, at(part, d, 0), at(part, -d, 0), 0 if d < 0 else 1)
                for e in (1, -1):
                    pass_on(p, part, at(part, d, 0), at(part, 0, e))

    def near_second(p):
        for d in (-1, 1):
            for part in range(2):
                arrived(p, part, at(part, 0, d))
                pass_on(p, part, at(part, 0, d), at(part, 0, -d), 0 if d < 0 else 1)

    def far_first(p):
        for part in range(2):
            arrived(p, part, at(part, 2, 0), 0)
            arrived(p, part, at(part, 2, 0), 1)
            for e in (1, -1):
                pass_on(p, part, at(part, 2, 0), at(part, 0, e))

    def rest_second(p):
        for a in (-1, 1, 2):
            for d in (-1, 1):
                for part in range(2):
                    arrived(p, part, at(part, a, d))
                    pass_on(p, part, at(part, a, d), at(part, 0, -d), 0 if d < 0 else 1)

    def finish(p):
        for a in (0, -1, 1, 2):
            for part in range(2):
                arrived(p, part, at(part, a, 2), 0)
                arrived(p, part, at(part, a, 2), 1)

    def kv_copy(k):
        kind = k // 4
        to = 2 * (2 * (k % 4) + c) + z // 4
        rows = pl.ds(pl.multiple_of(z * CTOK, CTOK), CTOK)
        local = pltpu.make_async_copy(proj.at[k], kv_ref.at[kind, rows], kr_sem.at[kind])
        away = remote(proj.at[k], kv_ref.at[kind, rows], ks_sem.at[k], kr_sem.at[kind], to, f)
        return to == s, local, away

    in_pair = pl.ds(pl.multiple_of(lax.rem(z, 2) * CTOK, CTOK), CTOK)

    def project(p):
        for t in (2 * p, 2 * p + 1):
            res = jnp.dot(xs[...], wg[:, t * 256 : (t + 1) * 256], preferred_element_type=F32)
            for j in range(2):
                k = 2 * t + j
                block = res[:, j * HD : (j + 1) * HD]
                if k < 4:
                    block = rotated(block, cos_ref[in_pair, :], sin_ref[in_pair, :])
                proj[k] = block.astype(BF)
                mine, local, away = kv_copy(k)

                @pl.when(mine)
                def _():
                    local.start()

                @pl.when(jnp.logical_not(mine))
                def _():
                    away.start()

    shares = []

    def share(p):
        half = kv_ref.at[p, pl.ds(pl.multiple_of(c * (SEQLEN // 2), SEQLEN // 2), SEQLEN // 2)]
        pltpu.make_async_copy(half, half, kr_sem.at[p]).wait()
        copy = remote(half, half, fs_sem.at[p], fr_sem.at[p], sib, f)
        copy.start()
        shares.append(copy)

    for copy in load_w:
        copy.wait()
    begin(0)
    load_x.wait()
    give_x = remote(xs.at[own_tok], xs.at[own_tok], xr_sem.at[0], xr_sem.at[1], sib, f)
    give_x.start()

    own_seq = pl.ds(pl.multiple_of(s * TOK, TOK), TOK)
    own_head = pl.ds(pl.multiple_of(s * HD, HD), HD)
    keep = []
    for i, (src, dst) in enumerate(((q_ref, qh_ref), (g_ref, gh_ref))):
        keep.append(pltpu.make_async_copy(src.at[:, own_head], dst.at[own_seq], ql_sem.at[i]))
        keep[-1].start()
    for step in range(1, 2 * NZ):
        to = ring(s + step, 2 * NZ)
        head = pl.ds(pl.multiple_of(to * HD, HD), HD)
        for i, (src, dst) in enumerate(((q_ref, qh_ref), (g_ref, gh_ref))):
            remote(src.at[:, head], dst.at[own_seq], qs_sem.at[i], qr_sem.at[i], to, f).start()

    near_first(0)
    begin(1)
    near_second(0)
    far_first(0)
    near_first(1)
    rest_second(0)
    near_second(1)
    far_first(1)
    finish(0)
    give_x.wait_recv()
    project(0)
    rest_second(1)
    finish(1)
    project(1)
    share(0)

    def turn(i, carry):
        cols = pl.ds(pl.multiple_of(i * 256, 256), 256)
        xt_ref[cols, :] = xs[:, cols].T
        return carry

    lax.fori_loop(0, D // 256, turn, 0)
    for copy in sends:
        copy.wait_send()
    give_x.wait_send()
    for copy in keep:
        copy.wait()
    for i, dst in enumerate((qh_ref, gh_ref)):
        others = dst.at[pl.ds(0, SEQLEN - TOK)]
        pltpu.make_async_copy(others, others, qs_sem.at[i]).wait()
        pltpu.make_async_copy(others, others, qr_sem.at[i]).wait()
    share(1)
    for k in range(8):
        mine, _, away = kv_copy(k)

        @pl.when(jnp.logical_not(mine))
        def _():
            away.wait_send()

    for copy in shares:
        copy.wait()


def k1(x, q, w, g, cosine, sine):
    dma = pltpu.SemaphoreType.DMA
    seq_block = jax.ShapeDtypeStruct((SEQLEN, HD), BF)
    return pl.pallas_call(
        k1_kernel,
        out_shape=(
            seq_block,
            seq_block,
            jax.ShapeDtypeStruct((2, SEQLEN, HD), BF),
            jax.ShapeDtypeStruct((D, CTOK), BF),
            jax.ShapeDtypeStruct((D, HALF), BF),
        ),
        in_specs=[HBM, HBM, HBM, HBM, VM, VM],
        out_specs=(VM, VM, VM, VM, VM),
        scratch_shapes=[
            pltpu.VMEM((CTOK, D), BF),
            pltpu.VMEM((8, CTOK, HD), BF),
            dma((8,)),
            dma(()),
            dma((2,)),
            dma((80,)),
            dma((2, 2, 4, 4, 2)),
            dma((2,)),
            dma((2,)),
            dma((2,)),
            dma((8,)),
            dma((2,)),
            dma((2,)),
            dma((2,)),
        ],
        compiler_params=pltpu.CompilerParams(
            collective_id=0, has_side_effects=True, vmem_limit_bytes=16 << 20
        ),
        name="gather_project",
    )(x, q, w, g, cosine, sine)


QT = 256
KT = 256
NT = (((1,), (1,)), ((), ()))
LOG2E = 1.4426950408889634


def k3_kernel(
    len_ref,
    q_ref,
    g_ref,
    kv_ref,
    xt,
    wv,
    cos_ref,
    sin_ref,
    out_ref,
    gin_ref,
    gw_ref,
    vt,
    wbuf,
    tbuf,
    inv,
    delt,
    gs,
    obuf,
    dkv,
    theirs,
    total,
    got,
    dd,
    da,
    xp,
    gi,
    gsend,
    grecv,
    part_sum,
    r1,
    r2,
    second,
    r3,
    third,
    zr,
    x_sem,
    ws_sem,
    wr_sem,
    ds_sem,
    dr_sem,
    ol_sem,
    os_sem,
    or_sem,
    as_sem,
    ar_sem,
    g_sem,
    s1_sem,
    r1_sem,
    s2_sem,
    r2_sem,
    s3_sem,
    r3_sem,
    zs_sem,
    zr_sem,
):
    s, f, z, c, x, y = where_am_i()
    sib = s + 1 - 2 * c
    e = lax.rem(z, 2)
    pair = z // 2
    partner = other_chip(s, z)
    enter(s, f, x, y)

    def landed(ref, sem):
        pltpu.make_async_copy(ref, ref, sem).wait()

    own_cols = pl.ds(pl.multiple_of(c * TOK, TOK), TOK)
    cross, spread = [], []
    for h in range(2):
        rows = pl.ds(h * (D // 2), D // 2)
        here, there = xt.at[rows, own_cols], xp.at[rows, own_cols]
        cross.append(remote(here, there, x_sem.at[0, h], x_sem.at[1, h], partner, f))
        spread.append(remote(there, there, x_sem.at[2, h], x_sem.at[3, h], sib, f))
        cross[h].start()

    ends = []
    so_far = 0
    for i in range(NDOC):
        so_far = so_far + len_ref[i]
        ends.append(so_far)

    def flip(i, carry):
        rows = pl.ds(pl.multiple_of(i * KT, KT), KT)
        vt[:, rows] = kv_ref[1, rows, :].T
        return carry

    lax.fori_loop(0, SEQLEN // KT, flip, 0)

    def tile_rows(i):
        return pl.ds(pl.multiple_of(i * KT, KT), KT)

    def swap(i):
        rows = tile_rows(i)
        return remote(
            dkv.at[1 - c, rows], theirs.at[rows], ws_sem.at[i], wr_sem.at[i], sib, f
        )

    def forward(i, n):
        base = i * QT
        rows = tile_rows(i)
        pos = base + lax.broadcasted_iota(jnp.int32, (1, QT), 1)
        start = jnp.zeros((1, QT), jnp.int32)
        for end in ends:
            start = jnp.where(pos >= end, end, start)
        low = jnp.maximum(start, pos - (WIN - 1))
        first = i + 1 - n
        qt = q_ref[rows, :]
        acc = jnp.zeros((HD, QT), F32)
        norm = jnp.zeros((1, QT), F32)
        key = lax.broadcasted_iota(jnp.int32, (KT, QT), 0)
        for j in range(n):
            span = tile_rows(first + j)
            st = lax.dot_general(kv_ref[0, span, :], qt, NT, preferred_element_type=F32)
            squashed = jnp.tanh(st * (SCALE / CAP))
            allowed = key >= low - (first + j) * KT
            if j == n - 1:
                allowed = allowed & (key <= pos - (first + j) * KT)
            weight = jnp.where(allowed, jnp.exp2((CAP * LOG2E) * squashed), 0.0)
            short = weight.astype(BF)
            norm = norm + jnp.sum(weight, axis=0, keepdims=True)
            wbuf[first + j, n - 1 - j] = weight * (1.0 - squashed * squashed)
            tbuf[first + j, n - 1 - j] = short
            acc = acc + jnp.dot(vt[:, span], short, preferred_element_type=F32)
        inverse = 1.0 / norm
        out_t = (acc * inverse).astype(BF)
        obuf[rows, :] = out_t.T
        gt_t = g_ref[rows, :].astype(F32).T
        delt[i] = jnp.sum(gt_t * out_t.astype(F32), axis=0, keepdims=True)
        inv[i] = inverse
        gs[rows, :] = (gt_t * inverse).T.astype(BF)

    def backward(t, n):
        span = tile_rows(t)
        dk = jnp.zeros((KT, HD), F32)
        dv = jnp.zeros((KT, HD), F32)
        for j in range(n):
            rows = tile_rows(t + j)
            dprob = lax.dot_general(
                kv_ref[1, span, :], g_ref[rows, :], NT, preferred_element_type=F32
            )
            dscore = (wbuf[t, j] * inv[t + j] * (dprob - delt[t + j])).astype(BF)
            dk = dk + jnp.dot(dscore, q_ref[rows, :], preferred_element_type=F32)
            dv = dv + jnp.dot(tbuf[t, j], gs[rows, :], preferred_element_type=F32)
        dkv[0, span, :] = (dk * SCALE).astype(BF)
        dkv[1, span, :] = dv.astype(BF)

    head_dev = lax.rem(z, 4)

    def d_copy(i):
        rows = tile_rows(i)
        to = 4 * (i // 2) + head_dev
        dst = got.at[2 * c + z // 4, pl.ds(pl.multiple_of(lax.rem(i, 2) * CTOK, CTOK), CTOK)]
        local = pltpu.make_async_copy(total.at[rows], dst, dr_sem.at[c])
        away = remote(total.at[rows], dst, ds_sem.at[i], dr_sem.at[c], to, f)
        return to == s, local, away

    def hand_over(i):
        rows = tile_rows(i)
        landed(theirs.at[rows], wr_sem.at[i])
        total[rows, :] = (dkv[c, rows, :].astype(F32) + theirs[rows, :].astype(F32)).astype(BF)
        mine, local, away = d_copy(i)

        @pl.when(mine)
        def _():
            local.start()

        @pl.when(jnp.logical_not(mine))
        def _():
            away.start()

    def long_tile(k, carry):
        forward(k + 4, 5)
        return carry

    for i in range(4):
        forward(jnp.int32(i), i + 1)
    lax.fori_loop(0, 4, long_tile, 0)

    tiles = SEQLEN // KT

    def key_tile(k, carry):
        t = ring(z + k, tiles)
        count = jnp.minimum(tiles - t, 5)
        for n in range(1, 6):

            @pl.when(count == n)
            def _():
                backward(t, n)

        swap(t).start()

        @pl.when(k > 0)
        def _():
            hand_over(ring(t - 1, tiles))

        for h in range(2):

            @pl.when(k == 4 + 3 * h)
            def _():
                cross[h].wait_recv()
                spread[h].start()

        return carry

    lax.fori_loop(0, tiles, key_tile, 0)
    hand_over(ring(z - 1, tiles))
    for h in range(2):
        spread[h].wait_recv()

    own_tok = pl.ds(pl.multiple_of(e * CTOK, CTOK), CTOK)
    pair_tok = pl.ds(pl.multiple_of((1 - e) * CTOK, CTOK), CTOK)

    def a_cols(b, side):
        return pl.ds(pl.multiple_of((side + 2 * b) * HD, HD), HD)

    def a_copy(b):
        return remote(
            dd.at[b, pair_tok], da.at[:, a_cols(b, e)], as_sem.at[b], ar_sem.at[b], partner, f
        )

    def take_in(kind):
        blocks = got.at[pl.ds(2 * kind, 2)]
        landed(blocks, dr_sem.at[kind])
        for b in range(2 * kind, 2 * kind + 2):
            block = got[b]
            if kind == 0:
                block = rotated(block.astype(F32), cos_ref[...], -sin_ref[...]).astype(BF)
            dd[b] = block

    def trade(kind):
        for b in range(2 * kind, 2 * kind + 2):
            a_copy(b).start()
            da[:, a_cols(b, e)] = dd[b, own_tok, :]

    def chunk(p, part, a):
        for j in range(4):
            cx, cy = (a, j) if part == 0 else (j, a)
            rows = pl.ds(pl.multiple_of((cx * NY + cy) * ROWS, 16), ROWS)
            part_sum[p, part, cx, cy] = (
                jnp.dot(xt[rows, :], dd[2 * p + part, own_tok, :], preferred_element_type=F32)
                + jnp.dot(xp[rows, :], dd[2 * p + part, pair_tok, :], preferred_element_type=F32)
            ).astype(BF)

    def chunk_ref(p, part, a, which):
        if part == 0:
            return part_sum.at[p, part, a, which]
        return part_sum.at[p, part, which, a]

    first_axis = (x, y)
    second_axis = (y, x)

    def neighbour(part, level, d):
        if (part == 0) == (level == 0):
            return ring(x + d, NX) * NY + y
        return x * NY + ring(y + d, NY)

    halves = (pl.ds(0, 2), pl.ds(2, 2))
    full = pl.ds(0, 4)
    dirs = (1, -1)
    sent = []

    def go(src, dst, send, recv, to_f):
        copy = remote(src, dst, send, recv, s, to_f)
        copy.start()
        sent.append(copy)

    def far(p):
        for part in range(2):
            a = ring(first_axis[part] + 2, 4)
            chunk(p, part, a)
            for h, d in enumerate(dirs):
                go(
                    chunk_ref(p, part, a, halves[h]),
                    r1.at[p, part, h],
                    s1_sem.at[p, part, h],
                    r1_sem.at[p, part, h],
                    neighbour(part, 0, d),
                )

    def near(p):
        for part in range(2):
            for d in (1, -1, 0):
                chunk(p, part, ring(first_axis[part] + d, 4))

    def hop(p):
        for h, d in enumerate(dirs):
            for part in range(2):
                a = ring(first_axis[part] + d, 4)
                landed(r1.at[p, part, h], r1_sem.at[p, part, h])
                for k in range(2):
                    j = 2 * h + k
                    idx = (p, part, a, j) if part == 0 else (p, part, j, a)
                    part_sum[idx] = (
                        part_sum[idx].astype(F32) + r1[p, part, h, k].astype(F32)
                    ).astype(BF)
                go(
                    chunk_ref(p, part, a, full),
                    r2.at[p, part, h],
                    s2_sem.at[p, part, h],
                    r2_sem.at[p, part, h],
                    neighbour(part, 0, d),
                )

    def across(p):
        for part in range(2):
            for h in range(2):
                landed(r2.at[p, part, h], r2_sem.at[p, part, h])
            for j in range(4):
                idx = (p, part, x, j) if part == 0 else (p, part, j, y)
                second[p, part, j] = (
                    part_sum[idx].astype(F32)
                    + r2[p, part, 0, j].astype(F32)
                    + r2[p, part, 1, j].astype(F32)
                ).astype(BF)
            for i, d in enumerate((2, 1, -1)):
                go(
                    second.at[p, part, ring(second_axis[part] + d, 4)],
                    r3.at[p, part, i],
                    s3_sem.at[p, part, i],
                    r3_sem.at[p, part, i],
                    neighbour(part, 1, d),
                )

    def z_copy(b):
        to = 2 * (2 * b + e) + c
        return pair != b, remote(third.at[b], zr.at[pair], zs_sem.at[b], zr_sem, to, f)

    def along(p):
        for part in range(2):
            b = 2 * p + part
            acc = second[p, part, second_axis[part]].astype(F32)
            for i in range(3):
                landed(r3.at[p, part, i], r3_sem.at[p, part, i])
                acc = acc + r3[p, part, i].astype(F32)
            third[b] = acc.astype(BF)
            away, copy = z_copy(b)

            @pl.when(away)
            def _():
                copy.start()

    take_in(0)
    far(0)
    near(0)
    take_in(1)
    far(1)
    trade(0)
    trade(1)
    own_head = pl.ds(pl.multiple_of(s * HD, HD), HD)
    own_seq = pl.ds(pl.multiple_of(s * TOK, TOK), TOK)
    keep_o = pltpu.make_async_copy(obuf.at[own_seq], out_ref.at[:, own_head], ol_sem)
    keep_o.start()
    for step in range(1, 2 * NZ):
        to = ring(s + step, 2 * NZ)
        theirs_tok = pl.ds(pl.multiple_of(to * TOK, TOK), TOK)
        remote(
            obuf.at[theirs_tok], out_ref.at[:, own_head], os_sem, or_sem, to, f
        ).start()
    hop(0)
    near(1)
    hop(1)
    across(0)

    for b in range(4):
        landed(da.at[:, a_cols(b, 1 - e)], ar_sem.at[b])

    def input_tile(i, carry):
        rows = pl.ds(pl.multiple_of(i * 256, 256), 256)
        gi[:, rows] = lax.dot_general(da[...], wv[rows, :], NT, preferred_element_type=F32)
        return carry

    lax.fori_loop(0, D // 256, input_tile, 0)
    mine_tok = pl.ds(pl.multiple_of(c * TOK, TOK), TOK)
    sib_tok = pl.ds(pl.multiple_of((1 - c) * TOK, TOK), TOK)
    gsend[...] = gi[sib_tok, :].astype(BF)
    give = remote(gsend, grecv, g_sem.at[0], g_sem.at[1], sib, f)
    give.start()
    along(0)
    across(1)
    give.wait()
    gin_ref[...] = (gi[mine_tok, :] + grecv[...].astype(F32)).astype(BF)
    along(1)
    for copy in sent:
        copy.wait_send()
    for h in range(2):
        cross[h].wait_send()
        spread[h].wait_send()
    for b in range(4):
        a_copy(b).wait_send()

    def settle(i, carry):
        swap(i).wait_send()
        mine, _, away = d_copy(i)

        @pl.when(jnp.logical_not(mine))
        def _():
            away.wait_send()

        return carry

    lax.fori_loop(0, SEQLEN // QT, settle, 0)
    keep_o.wait()
    others = obuf.at[pl.ds(0, SEQLEN - TOK)]
    landed(others, os_sem)
    landed(others, or_sem)
    for b in range(4):
        away, copy = z_copy(b)

        @pl.when(away)
        def _():
            copy.wait_send()

    rest = zr.at[pl.ds(1, 3)]
    landed(rest, zr_sem)
    acc = third[pair].astype(F32)
    for step in range(1, 4):
        acc = acc + zr[ring(pair + step, 4)].astype(F32)
    gw_ref[...] = acc


def k3(lengths, qh, gh, kv, xt, wh, cosine, sine):
    dma = pltpu.SemaphoreType.DMA
    return pl.pallas_call(
        k3_kernel,
        out_shape=(
            jax.ShapeDtypeStruct((TOK, 2048), BF),
            jax.ShapeDtypeStruct((TOK, D), BF),
            jax.ShapeDtypeStruct((ROWS, HD), F32),
        ),
        in_specs=[pl.BlockSpec(memory_space=pltpu.SMEM)] + [VM] * 7,
        out_specs=(VM, VM, VM),
        scratch_shapes=[
            pltpu.VMEM((HD, SEQLEN), BF),
            pltpu.VMEM((8, 5, KT, QT), F32),
            pltpu.VMEM((8, 5, KT, QT), BF),
            pltpu.VMEM((8, 1, QT), F32),
            pltpu.VMEM((8, 1, QT), F32),
            pltpu.VMEM((SEQLEN, HD), BF),
            pltpu.VMEM((SEQLEN, HD), BF),
            pltpu.VMEM((2, SEQLEN, HD), BF),
            pltpu.VMEM((SEQLEN, HD), BF),
            pltpu.VMEM((SEQLEN, HD), BF),
            pltpu.VMEM((4, 2 * CTOK, HD), BF),
            pltpu.VMEM((4, 2 * CTOK, HD), BF),
            pltpu.VMEM((CTOK, HALF), BF),
            pltpu.VMEM((D, CTOK), BF),
            pltpu.VMEM((CTOK, D), F32),
            pltpu.VMEM((TOK, D), BF),
            pltpu.VMEM((TOK, D), BF),
            pltpu.VMEM((2, 2, 4, 4, ROWS, HD), BF),
            pltpu.VMEM((2, 2, 2, 2, ROWS, HD), BF),
            pltpu.VMEM((2, 2, 2, 4, ROWS, HD), BF),
            pltpu.VMEM((2, 2, 4, ROWS, HD), BF),
            pltpu.VMEM((2, 2, 3, ROWS, HD), BF),
            pltpu.VMEM((4, ROWS, HD), BF),
            pltpu.VMEM((4, ROWS, HD), BF),
            dma((4, 2)),
            dma((8,)),
            dma((8,)),
            dma((8,)),
            dma((2,)),
            dma(()),
            dma(()),
            dma(()),
            dma((4,)),
            dma((4,)),
            dma((2,)),
            dma((2, 2, 2)),
            dma((2, 2, 2)),
            dma((2, 2, 2)),
            dma((2, 2, 2)),
            dma((2, 2, 3)),
            dma((2, 2, 3)),
            dma((4,)),
            dma(()),
        ],
        compiler_params=pltpu.CompilerParams(
            collective_id=1, has_side_effects=True, vmem_limit_bytes=40 << 20
        ),
        name="gradients",
    )(lengths, qh, gh, kv, xt, wh, cosine, sine)


def tables(lengths):
    pair = lax.axis_index("seq") // 4
    places = pair * (2 * CTOK) + jnp.arange(2 * CTOK, dtype=jnp.int32)
    order = jnp.arange(NDOC)
    doc_ends = jnp.sum(jnp.where(order[:, None] <= order[None, :], lengths[:, None], 0), axis=0)
    ended = doc_ends[None, :] <= places[:, None]
    within = places - jnp.sum(jnp.where(ended, lengths[None, :], 0), axis=1)
    exponent = jnp.arange(HD // 2, dtype=F32) * (2.0 / HD)
    rate = jnp.power(ROPE_BASE, -exponent)
    angles = within.astype(F32)[:, None] * rate[None, :]
    cosine, sine = jnp.cos(angles), jnp.sin(angles)
    return (
        jnp.concatenate([cosine, cosine], axis=1),
        jnp.concatenate([-sine, sine], axis=1),
    )


def on_device(inputs, queries, w_kv, doc_lengths, grad_out):
    cosine, sine = tables(doc_lengths[0])
    held = [
        pltpu.with_memory_space_constraint(a, pltpu.HBM)
        for a in (inputs[0], queries[0], w_kv, grad_out[0])
    ]
    qh, gh, kv, xt, wh = k1(*held, cosine, sine)
    out, gin, gw = k3(doc_lengths[0], qh, gh, kv, xt, wh, cosine, sine)
    return out[None], gin[None], gw


def solution(mesh):
    in_specs = (
        P("fsdp", "seq", None),
        P("fsdp", "seq", None),
        P("fsdp", None),
        P("fsdp", None),
        P("fsdp", "seq", None),
    )
    out_specs = (P("fsdp", "seq", None), P("fsdp", "seq", None), P("fsdp", "seq"))
    return jax.shard_map(
        on_device, mesh=mesh, in_specs=in_specs, out_specs=out_specs, check_vma=False
    )
```

```python
import functools

import jax
import jax.numpy as jnp
from jax import lax
from jax.experimental import pallas as pl
from jax.experimental.pallas import tpu as pltpu
from jax.sharding import PartitionSpec as P

D = 2304
HD = 128
WIN = 1024
SEQLEN = 2048
NDOC = 8
NZ = 8
NX = 4
NY = 4
ROWS = D // (NX * NY)
HALF = 1024
PART = 512
TOK = 128
CTOK = 256
CAP = 50.0
SCALE = 1.0 / 12.0
ROPE_BASE = 10000.0
MESH = pl.DeviceIdType.MESH
HBM = pl.BlockSpec(memory_space=pltpu.HBM)
VM = pl.BlockSpec(memory_space=pltpu.VMEM)
BF = jnp.bfloat16
F32 = jnp.float32


def where_am_i():
    s = lax.axis_index("seq")
    f = lax.axis_index("fsdp")
    z = s // 2
    c = s - 2 * z
    x = f // NY
    y = f - NY * x
    return s, f, z, c, x, y


def ring(v, n):
    return lax.rem(v + n, n)


def remote(src, dst, send, recv, s, f):
    return pltpu.make_async_remote_copy(
        src_ref=src,
        dst_ref=dst,
        send_sem=send,
        recv_sem=recv,
        device_id={"seq": s, "fsdp": f},
        device_id_type=MESH,
    )


def enter(s, f, x, y):
    barrier = pltpu.get_barrier_semaphore()
    for step in range(1, 2 * NZ):
        pl.semaphore_signal(
            barrier,
            inc=1,
            device_id={"seq": ring(s + step, 2 * NZ), "fsdp": f},
            device_id_type=MESH,
        )
    for dx, dy in ((1, 0), (-1, 0), (0, 1), (0, -1)):
        pl.semaphore_signal(
            barrier,
            inc=1,
            device_id={"seq": s, "fsdp": ring(x + dx, NX) * NY + ring(y + dy, NY)},
            device_id_type=MESH,
        )
    pl.semaphore_wait(barrier, 2 * NZ - 1 + 4)


def other_chip(s, z):
    return s + 2 - 4 * lax.rem(z, 2)


def rotated(values, cosine, sine):
    return values * cosine + pltpu.roll(values, HD // 2, 1) * sine


def project_part(
    x_ref,
    q_ref,
    w_ref,
    g_ref,
    cos_ref,
    sin_ref,
    qh_ref,
    gh_ref,
    kv_ref,
    xt,
    xp,
    wg,
    xs,
    xo,
    proj,
    wl_sem,
    xl_sem,
    xr_sem,
    xc_sem,
    ws_sem,
    wr_sem,
    ql_sem,
    qs_sem,
    qr_sem,
    ks_sem,
    kr_sem,
    fs_sem,
    fr_sem,
):
    s, f, z, c, x, y = where_am_i()
    sib = s + 1 - 2 * c
    own_rows = pl.ds(pl.multiple_of(f * ROWS, 16), ROWS)
    load_w = []
    for k in range(8):
        cols = pl.ds(pl.multiple_of((2 * k + c) * HD, HD), HD)
        load_w.append(
            pltpu.make_async_copy(
                w_ref.at[:, cols], wg.at[own_rows, pl.ds(k * HD, HD)], wl_sem.at[k]
            )
        )
    for copy in load_w:
        copy.start()
    own_tok = pl.ds(pl.multiple_of(c * TOK, TOK), TOK)
    load_x = pltpu.make_async_copy(x_ref, xs.at[own_tok], xl_sem)
    load_x.start()
    enter(s, f, x, y)

    wide = PART // 2

    def piece(phase, part, off, half):
        origin = ring(x + off[0], NX) * NY + ring(y + off[1], NY)
        rows = pl.ds(pl.multiple_of(origin * ROWS, 16), ROWS)
        base = phase * PART + part * wide
        if half is None:
            return wg.at[rows, pl.ds(base, wide)]
        return wg.at[rows, pl.ds(base + half * (wide // 2), wide // 2)]

    sends = []

    def pass_on(phase, part, off, step, half=None):
        there = tuple((o - d) % 4 for o, d in zip(off, step))
        there = tuple(-1 if t == 3 else t for t in there)
        ref = piece(phase, part, off, half)
        copy = remote(
            ref,
            ref,
            ws_sem.at[len(sends)],
            wr_sem.at[phase, part, there[0] + 1, there[1] + 1, half or 0],
            s,
            ring(x + step[0], NX) * NY + ring(y + step[1], NY),
        )
        copy.start()
        sends.append(copy)

    def arrived(phase, part, off, half=None):
        ref = piece(phase, part, off, half)
        sem = wr_sem.at[phase, part, off[0] + 1, off[1] + 1, half or 0]
        pltpu.make_async_copy(ref, ref, sem).wait()

    def at(part, a, b):
        return (a, b) if part == 0 else (b, a)

    def begin(p):
        for d in (1, -1):
            for part in range(2):
                pass_on(p, part, (0, 0), at(part, d, 0))
        for d in (1, -1):
            for part in range(2):
                pass_on(p, part, (0, 0), at(part, 0, d))

    def near_first(p):
        for d in (-1, 1):
            for part in range(2):
                arrived(p, part, at(part, d, 0))
                pass_on(p, part, at(part, d, 0), at(part, -d, 0), 0 if d < 0 else 1)
                for e in (1, -1):
                    pass_on(p, part, at(part, d, 0), at(part, 0, e))

    def near_second(p):
        for d in (-1, 1):
            for part in range(2):
                arrived(p, part, at(part, 0, d))
                pass_on(p, part, at(part, 0, d), at(part, 0, -d), 0 if d < 0 else 1)

    def far_first(p):
        for part in range(2):
            arrived(p, part, at(part, 2, 0), 0)
            arrived(p, part, at(part, 2, 0), 1)
            for e in (1, -1):
                pass_on(p, part, at(part, 2, 0), at(part, 0, e))

    def rest_second(p):
        for a in (-1, 1, 2):
            for d in (-1, 1):
                for part in range(2):
                    arrived(p, part, at(part, a, d))
                    pass_on(p, part, at(part, a, d), at(part, 0, -d), 0 if d < 0 else 1)

    def finish(p):
        for a in (0, -1, 1, 2):
            for part in range(2):
                arrived(p, part, at(part, a, 2), 0)
                arrived(p, part, at(part, a, 2), 1)

    def kv_copy(k):
        kind = k // 4
        to = 2 * (2 * (k % 4) + c) + z // 4
        rows = pl.ds(pl.multiple_of(z * CTOK, CTOK), CTOK)
        local = pltpu.make_async_copy(proj.at[k], kv_ref.at[kind, rows], kr_sem.at[kind])
        away = remote(proj.at[k], kv_ref.at[kind, rows], ks_sem.at[k], kr_sem.at[kind], to, f)
        return to == s, local, away

    in_pair = pl.ds(pl.multiple_of(lax.rem(z, 2) * CTOK, CTOK), CTOK)

    def project(p):
        for t in (2 * p, 2 * p + 1):
            res = jnp.dot(xs[...], wg[:, t * 256 : (t + 1) * 256], preferred_element_type=F32)
            for j in range(2):
                k = 2 * t + j
                block = res[:, j * HD : (j + 1) * HD]
                if k < 4:
                    block = rotated(block, cos_ref[in_pair, :], sin_ref[in_pair, :])
                proj[k] = block.astype(BF)
                mine, local, away = kv_copy(k)

                @pl.when(mine)
                def _():
                    local.start()

                @pl.when(jnp.logical_not(mine))
                def _():
                    away.start()

    shares = []

    def share(p):
        half = kv_ref.at[p, pl.ds(pl.multiple_of(c * (SEQLEN // 2), SEQLEN // 2), SEQLEN // 2)]
        pltpu.make_async_copy(half, half, kr_sem.at[p]).wait()
        copy = remote(half, half, fs_sem.at[p], fr_sem.at[p], sib, f)
        copy.start()
        shares.append(copy)

    for copy in load_w:
        copy.wait()
    begin(0)
    load_x.wait()
    give_x = remote(xs.at[own_tok], xs.at[own_tok], xr_sem.at[0], xr_sem.at[1], sib, f)
    give_x.start()

    own_seq = pl.ds(pl.multiple_of(s * TOK, TOK), TOK)
    own_head = pl.ds(pl.multiple_of(s * HD, HD), HD)

    def deal(i, src, dst):
        pltpu.make_async_copy(src.at[:, own_head], dst.at[own_seq], ql_sem.at[i]).start()
        for step in range(1, 2 * NZ):
            to = ring(s + step, 2 * NZ)
            head = pl.ds(pl.multiple_of(to * HD, HD), HD)
            remote(src.at[:, head], dst.at[own_seq], qs_sem.at[i], qr_sem.at[i], to, f).start()

    def dealt(i, src, dst):
        pltpu.make_async_copy(src.at[:, own_head], dst.at[own_seq], ql_sem.at[i]).wait()
        others = dst.at[pl.ds(0, SEQLEN - TOK)]
        pltpu.make_async_copy(others, others, qs_sem.at[i]).wait()
        pltpu.make_async_copy(others, others, qr_sem.at[i]).wait()

    deal(0, q_ref, qh_ref)
    cross = remote(
        xs.at[own_tok], xo.at[own_tok], xc_sem.at[0], xc_sem.at[1], other_chip(s, z), f
    )
    cross.start()

    near_first(0)
    begin(1)
    near_second(0)
    far_first(0)
    near_first(1)
    rest_second(0)
    near_second(1)
    far_first(1)
    finish(0)
    give_x.wait_recv()
    project(0)
    rest_second(1)
    finish(1)
    project(1)
    deal(1, g_ref, gh_ref)
    share(0)
    cross.wait_recv()
    spread = remote(xo.at[own_tok], xo.at[own_tok], xc_sem.at[2], xc_sem.at[3], sib, f)
    spread.start()

    def turn(i, carry):
        cols = pl.ds(pl.multiple_of(i * 256, 256), 256)
        xt[cols, :] = xs[:, cols].T
        return carry

    def turn_other(i, carry):
        cols = pl.ds(pl.multiple_of(i * 256, 256), 256)
        xp[cols, :] = xo[:, cols].T
        return carry

    lax.fori_loop(0, D // 256, turn, 0)
    spread.wait()
    lax.fori_loop(0, D // 256, turn_other, 0)
    cross.wait_send()
    for copy in sends:
        copy.wait_send()
    give_x.wait_send()
    dealt(0, q_ref, qh_ref)
    share(1)
    for k in range(8):
        mine, _, away = kv_copy(k)

        @pl.when(jnp.logical_not(mine))
        def _():
            away.wait_send()

    for copy in shares:
        copy.wait()
    return lambda: dealt(1, g_ref, gh_ref)


QT = 256
KT = 256
NT = (((1,), (1,)), ((), ()))
LOG2E = 1.4426950408889634


def gradient_part(
    wait_g,
    len_ref,
    q_ref,
    g_ref,
    kv_ref,
    xt,
    xp,
    wv,
    cos_ref,
    sin_ref,
    out_ref,
    gin_ref,
    gw_ref,
    vt,
    ot,
    wbuf,
    tbuf,
    inv,
    delt,
    gs,
    obuf,
    dkv,
    theirs,
    total,
    got,
    dd,
    da,
    gi,
    gsend,
    grecv,
    part_sum,
    r1,
    r2,
    second,
    r3,
    third,
    zr,
    ws_sem,
    wr_sem,
    ds_sem,
    dr_sem,
    ol_sem,
    os_sem,
    or_sem,
    as_sem,
    ar_sem,
    g_sem,
    s1_sem,
    r1_sem,
    s2_sem,
    r2_sem,
    s3_sem,
    r3_sem,
    zs_sem,
    zr_sem,
):
    s, f, z, c, x, y = where_am_i()
    sib = s + 1 - 2 * c
    e = lax.rem(z, 2)
    pair = z // 2
    partner = other_chip(s, z)
    def landed(ref, sem):
        pltpu.make_async_copy(ref, ref, sem).wait()

    ends = []
    so_far = 0
    for i in range(NDOC):
        so_far = so_far + len_ref[i]
        ends.append(so_far)

    def flip(i, carry):
        rows = pl.ds(pl.multiple_of(i * KT, KT), KT)
        vt[:, rows] = kv_ref[1, rows, :].T
        return carry

    lax.fori_loop(0, SEQLEN // KT, flip, 0)

    def tile_rows(i):
        return pl.ds(pl.multiple_of(i * KT, KT), KT)

    def swap(i):
        rows = tile_rows(i)
        return remote(
            dkv.at[1 - c, rows], theirs.at[rows], ws_sem.at[i], wr_sem.at[i], sib, f
        )

    def forward(i, n):
        base = i * QT
        rows = tile_rows(i)
        pos = base + lax.broadcasted_iota(jnp.int32, (1, QT), 1)
        start = jnp.zeros((1, QT), jnp.int32)
        for end in ends:
            start = jnp.where(pos >= end, end, start)
        low = jnp.maximum(start, pos - (WIN - 1))
        first = i + 1 - n
        qt = q_ref[rows, :]
        acc = jnp.zeros((HD, QT), F32)
        norm = jnp.zeros((1, QT), F32)
        key = lax.broadcasted_iota(jnp.int32, (KT, QT), 0)
        for j in range(n):
            span = tile_rows(first + j)
            st = lax.dot_general(kv_ref[0, span, :], qt, NT, preferred_element_type=F32)
            squashed = jnp.tanh(st * (SCALE / CAP))
            allowed = key >= low - (first + j) * KT
            if j == n - 1:
                allowed = allowed & (key <= pos - (first + j) * KT)
            weight = jnp.where(allowed, jnp.exp2((CAP * LOG2E) * squashed), 0.0)
            short = weight.astype(BF)
            norm = norm + jnp.sum(weight, axis=0, keepdims=True)
            wbuf[first + j, n - 1 - j] = weight * (1.0 - squashed * squashed)
            tbuf[first + j, n - 1 - j] = short
            acc = acc + jnp.dot(vt[:, span], short, preferred_element_type=F32)
        inverse = 1.0 / norm
        out_t = (acc * inverse).astype(BF)
        obuf[rows, :] = out_t.T
        inv[i] = inverse
        ot[:, rows] = out_t

    def prepare(i, carry):
        rows = tile_rows(i)
        gt_t = g_ref[rows, :].astype(F32).T
        delt[i] = jnp.sum(gt_t * ot[:, rows].astype(F32), axis=0, keepdims=True)
        gs[rows, :] = (gt_t * inv[i]).T.astype(BF)
        return carry

    def backward(t, n):
        span = tile_rows(t)
        dk = jnp.zeros((KT, HD), F32)
        dv = jnp.zeros((KT, HD), F32)
        for j in range(n):
            rows = tile_rows(t + j)
            dprob = lax.dot_general(
                kv_ref[1, span, :], g_ref[rows, :], NT, preferred_element_type=F32
            )
            dscore = (wbuf[t, j] * inv[t + j] * (dprob - delt[t + j])).astype(BF)
            dk = dk + jnp.dot(dscore, q_ref[rows, :], preferred_element_type=F32)
            dv = dv + jnp.dot(tbuf[t, j], gs[rows, :], preferred_element_type=F32)
        dkv[0, span, :] = (dk * SCALE).astype(BF)
        dkv[1, span, :] = dv.astype(BF)

    head_dev = lax.rem(z, 4)

    def d_copy(i):
        rows = tile_rows(i)
        to = 4 * (i // 2) + head_dev
        dst = got.at[2 * c + z // 4, pl.ds(pl.multiple_of(lax.rem(i, 2) * CTOK, CTOK), CTOK)]
        local = pltpu.make_async_copy(total.at[rows], dst, dr_sem.at[c])
        away = remote(total.at[rows], dst, ds_sem.at[i], dr_sem.at[c], to, f)
        return to == s, local, away

    def hand_over(i):
        rows = tile_rows(i)
        landed(theirs.at[rows], wr_sem.at[i])
        total[rows, :] = (dkv[c, rows, :].astype(F32) + theirs[rows, :].astype(F32)).astype(BF)
        mine, local, away = d_copy(i)

        @pl.when(mine)
        def _():
            local.start()

        @pl.when(jnp.logical_not(mine))
        def _():
            away.start()

    def long_tile(k, carry):
        forward(k + 4, 5)
        return carry

    for i in range(4):
        forward(jnp.int32(i), i + 1)
    lax.fori_loop(0, 4, long_tile, 0)

    wait_g()
    lax.fori_loop(0, SEQLEN // QT, prepare, 0)

    tiles = SEQLEN // KT

    def key_tile(k, carry):
        t = ring(z + k, tiles)
        count = jnp.minimum(tiles - t, 5)
        for n in range(1, 6):

            @pl.when(count == n)
            def _():
                backward(t, n)

        swap(t).start()

        @pl.when(k > 0)
        def _():
            hand_over(ring(t - 1, tiles))

        return carry

    lax.fori_loop(0, tiles, key_tile, 0)
    hand_over(ring(z - 1, tiles))

    own_tok = pl.ds(pl.multiple_of(e * CTOK, CTOK), CTOK)
    pair_tok = pl.ds(pl.multiple_of((1 - e) * CTOK, CTOK), CTOK)

    def a_cols(b, side):
        return pl.ds(pl.multiple_of((side + 2 * b) * HD, HD), HD)

    def a_copy(b):
        return remote(
            dd.at[b, pair_tok], da.at[:, a_cols(b, e)], as_sem.at[b], ar_sem.at[b], partner, f
        )

    def take_in(kind):
        blocks = got.at[pl.ds(2 * kind, 2)]
        landed(blocks, dr_sem.at[kind])
        for b in range(2 * kind, 2 * kind + 2):
            block = got[b]
            if kind == 0:
                block = rotated(block.astype(F32), cos_ref[...], -sin_ref[...]).astype(BF)
            dd[b] = block

    def trade(kind):
        for b in range(2 * kind, 2 * kind + 2):
            a_copy(b).start()
            da[:, a_cols(b, e)] = dd[b, own_tok, :]

    def chunk(p, part, a):
        for j in range(4):
            cx, cy = (a, j) if part == 0 else (j, a)
            rows = pl.ds(pl.multiple_of((cx * NY + cy) * ROWS, 16), ROWS)
            part_sum[p, part, cx, cy] = (
                jnp.dot(xt[rows, :], dd[2 * p + part, own_tok, :], preferred_element_type=F32)
                + jnp.dot(xp[rows, :], dd[2 * p + part, pair_tok, :], preferred_element_type=F32)
            ).astype(BF)

    def chunk_ref(p, part, a, which):
        if part == 0:
            return part_sum.at[p, part, a, which]
        return part_sum.at[p, part, which, a]

    first_axis = (x, y)
    second_axis = (y, x)

    def neighbour(part, level, d):
        if (part == 0) == (level == 0):
            return ring(x + d, NX) * NY + y
        return x * NY + ring(y + d, NY)

    halves = (pl.ds(0, 2), pl.ds(2, 2))
    full = pl.ds(0, 4)
    dirs = (1, -1)
    sent = []

    def go(src, dst, send, recv, to_f):
        copy = remote(src, dst, send, recv, s, to_f)
        copy.start()
        sent.append(copy)

    def far(p):
        for part in range(2):
            a = ring(first_axis[part] + 2, 4)
            chunk(p, part, a)
            for h, d in enumerate(dirs):
                go(
                    chunk_ref(p, part, a, halves[h]),
                    r1.at[p, part, h],
                    s1_sem.at[p, part, h],
                    r1_sem.at[p, part, h],
                    neighbour(part, 0, d),
                )

    def near(p):
        for part in range(2):
            for d in (1, -1, 0):
                chunk(p, part, ring(first_axis[part] + d, 4))

    def hop(p):
        for h, d in enumerate(dirs):
            for part in range(2):
                a = ring(first_axis[part] + d, 4)
                landed(r1.at[p, part, h], r1_sem.at[p, part, h])
                for k in range(2):
                    j = 2 * h + k
                    idx = (p, part, a, j) if part == 0 else (p, part, j, a)
                    part_sum[idx] = (
                        part_sum[idx].astype(F32) + r1[p, part, h, k].astype(F32)
                    ).astype(BF)
                go(
                    chunk_ref(p, part, a, full),
                    r2.at[p, part, h],
                    s2_sem.at[p, part, h],
                    r2_sem.at[p, part, h],
                    neighbour(part, 0, d),
                )

    def across(p):
        for part in range(2):
            for h in range(2):
                landed(r2.at[p, part, h], r2_sem.at[p, part, h])
            for j in range(4):
                idx = (p, part, x, j) if part == 0 else (p, part, j, y)
                second[p, part, j] = (
                    part_sum[idx].astype(F32)
                    + r2[p, part, 0, j].astype(F32)
                    + r2[p, part, 1, j].astype(F32)
                ).astype(BF)
            for i, d in enumerate((2, 1, -1)):
                go(
                    second.at[p, part, ring(second_axis[part] + d, 4)],
                    r3.at[p, part, i],
                    s3_sem.at[p, part, i],
                    r3_sem.at[p, part, i],
                    neighbour(part, 1, d),
                )

    def z_copy(b):
        to = 2 * (2 * b + e) + c
        return pair != b, remote(third.at[b], zr.at[pair], zs_sem.at[b], zr_sem, to, f)

    def along(p):
        for part in range(2):
            b = 2 * p + part
            acc = second[p, part, second_axis[part]].astype(F32)
            for i in range(3):
                landed(r3.at[p, part, i], r3_sem.at[p, part, i])
                acc = acc + r3[p, part, i].astype(F32)
            third[b] = acc.astype(BF)
            away, copy = z_copy(b)

            @pl.when(away)
            def _():
                copy.start()

    take_in(0)
    far(0)
    near(0)
    take_in(1)
    far(1)
    trade(0)
    trade(1)
    own_head = pl.ds(pl.multiple_of(s * HD, HD), HD)
    own_seq = pl.ds(pl.multiple_of(s * TOK, TOK), TOK)
    keep_o = pltpu.make_async_copy(obuf.at[own_seq], out_ref.at[:, own_head], ol_sem)
    keep_o.start()
    for step in range(1, 2 * NZ):
        to = ring(s + step, 2 * NZ)
        theirs_tok = pl.ds(pl.multiple_of(to * TOK, TOK), TOK)
        remote(
            obuf.at[theirs_tok], out_ref.at[:, own_head], os_sem, or_sem, to, f
        ).start()
    hop(0)
    near(1)
    hop(1)
    across(0)

    for b in range(4):
        landed(da.at[:, a_cols(b, 1 - e)], ar_sem.at[b])

    def input_tile(i, carry):
        rows = pl.ds(pl.multiple_of(i * 256, 256), 256)
        gi[:, rows] = lax.dot_general(da[...], wv[rows, :], NT, preferred_element_type=F32)
        return carry

    lax.fori_loop(0, D // 256, input_tile, 0)
    mine_tok = pl.ds(pl.multiple_of(c * TOK, TOK), TOK)
    sib_tok = pl.ds(pl.multiple_of((1 - c) * TOK, TOK), TOK)
    gsend[...] = gi[sib_tok, :].astype(BF)
    give = remote(gsend, grecv, g_sem.at[0], g_sem.at[1], sib, f)
    give.start()
    along(0)
    across(1)
    give.wait()
    gin_ref[...] = (gi[mine_tok, :] + grecv[...].astype(F32)).astype(BF)
    along(1)
    for copy in sent:
        copy.wait_send()
    for b in range(4):
        a_copy(b).wait_send()

    def settle(i, carry):
        swap(i).wait_send()
        mine, _, away = d_copy(i)

        @pl.when(jnp.logical_not(mine))
        def _():
            away.wait_send()

        return carry

    lax.fori_loop(0, SEQLEN // QT, settle, 0)
    keep_o.wait()
    others = obuf.at[pl.ds(0, SEQLEN - TOK)]
    landed(others, os_sem)
    landed(others, or_sem)
    for b in range(4):
        away, copy = z_copy(b)

        @pl.when(away)
        def _():
            copy.wait_send()

    rest = zr.at[pl.ds(1, 3)]
    landed(rest, zr_sem)
    acc = third[pair].astype(F32)
    for step in range(1, 4):
        acc = acc + zr[ring(pair + step, 4)].astype(F32)
    gw_ref[...] = acc


def whole_kernel(
    len_ref, x_ref, q_ref, w_ref, g_ref, cos_ref, sin_ref, out_ref, gin_ref, gw_ref, *scratch
):
    qh, gh, kv, xt, xp, wg = scratch[:6]
    first, second = scratch[:PROJECT_SCRATCH], scratch[PROJECT_SCRATCH:]
    wait_g = project_part(x_ref, q_ref, w_ref, g_ref, cos_ref, sin_ref, *first)
    gradient_part(
        wait_g, len_ref, qh, gh, kv, xt, xp, wg, cos_ref, sin_ref, out_ref, gin_ref, gw_ref, *second
    )


PROJECT_SCRATCH = 22


def layer(lengths, x, q, w, g, cosine, sine):
    dma = pltpu.SemaphoreType.DMA
    return pl.pallas_call(
        whole_kernel,
        out_shape=(
            jax.ShapeDtypeStruct((TOK, 2048), BF),
            jax.ShapeDtypeStruct((TOK, D), BF),
            jax.ShapeDtypeStruct((ROWS, HD), F32),
        ),
        in_specs=[pl.BlockSpec(memory_space=pltpu.SMEM), HBM, HBM, HBM, HBM, VM, VM],
        out_specs=(VM, VM, VM),
        scratch_shapes=[
            pltpu.VMEM((SEQLEN, HD), BF),
            pltpu.VMEM((SEQLEN, HD), BF),
            pltpu.VMEM((2, SEQLEN, HD), BF),
            pltpu.VMEM((D, CTOK), BF),
            pltpu.VMEM((D, CTOK), BF),
            pltpu.VMEM((D, HALF), BF),
            pltpu.VMEM((CTOK, D), BF),
            pltpu.VMEM((CTOK, D), BF),
            pltpu.VMEM((8, CTOK, HD), BF),
            dma((8,)),
            dma(()),
            dma((2,)),
            dma((4,)),
            dma((80,)),
            dma((2, 2, 4, 4, 2)),
            dma((2,)),
            dma((2,)),
            dma((2,)),
            dma((8,)),
            dma((2,)),
            dma((2,)),
            dma((2,)),
            pltpu.VMEM((HD, SEQLEN), BF),
            pltpu.VMEM((HD, SEQLEN), BF),
            pltpu.VMEM((8, 5, KT, QT), F32),
            pltpu.VMEM((8, 5, KT, QT), BF),
            pltpu.VMEM((8, 1, QT), F32),
            pltpu.VMEM((8, 1, QT), F32),
            pltpu.VMEM((SEQLEN, HD), BF),
            pltpu.VMEM((SEQLEN, HD), BF),
            pltpu.VMEM((2, SEQLEN, HD), BF),
            pltpu.VMEM((SEQLEN, HD), BF),
            pltpu.VMEM((SEQLEN, HD), BF),
            pltpu.VMEM((4, 2 * CTOK, HD), BF),
            pltpu.VMEM((4, 2 * CTOK, HD), BF),
            pltpu.VMEM((CTOK, HALF), BF),
            pltpu.VMEM((CTOK, D), F32),
            pltpu.VMEM((TOK, D), BF),
            pltpu.VMEM((TOK, D), BF),
            pltpu.VMEM((2, 2, 4, 4, ROWS, HD), BF),
            pltpu.VMEM((2, 2, 2, 2, ROWS, HD), BF),
            pltpu.VMEM((2, 2, 2, 4, ROWS, HD), BF),
            pltpu.VMEM((2, 2, 4, ROWS, HD), BF),
            pltpu.VMEM((2, 2, 3, ROWS, HD), BF),
            pltpu.VMEM((4, ROWS, HD), BF),
            pltpu.VMEM((4, ROWS, HD), BF),
            dma((8,)),
            dma((8,)),
            dma((8,)),
            dma((2,)),
            dma(()),
            dma(()),
            dma(()),
            dma((4,)),
            dma((4,)),
            dma((2,)),
            dma((2, 2, 2)),
            dma((2, 2, 2)),
            dma((2, 2, 2)),
            dma((2, 2, 2)),
            dma((2, 2, 3)),
            dma((2, 2, 3)),
            dma((4,)),
            dma(()),
        ],
        compiler_params=pltpu.CompilerParams(
            collective_id=0, has_side_effects=True, vmem_limit_bytes=50 << 20
        ),
        name="layer",
    )(lengths, x, q, w, g, cosine, sine)


def tables(lengths):
    pair = lax.axis_index("seq") // 4
    places = pair * (2 * CTOK) + jnp.arange(2 * CTOK, dtype=jnp.int32)
    order = jnp.arange(NDOC)
    doc_ends = jnp.sum(jnp.where(order[:, None] <= order[None, :], lengths[:, None], 0), axis=0)
    ended = doc_ends[None, :] <= places[:, None]
    within = places - jnp.sum(jnp.where(ended, lengths[None, :], 0), axis=1)
    exponent = jnp.arange(HD // 2, dtype=F32) * (2.0 / HD)
    rate = jnp.power(ROPE_BASE, -exponent)
    angles = within.astype(F32)[:, None] * rate[None, :]
    cosine, sine = jnp.cos(angles), jnp.sin(angles)
    return (
        jnp.concatenate([cosine, cosine], axis=1),
        jnp.concatenate([-sine, sine], axis=1),
    )


def on_device(inputs, queries, w_kv, doc_lengths, grad_out):
    cosine, sine = tables(doc_lengths[0])
    held = [
        pltpu.with_memory_space_constraint(a, pltpu.HBM)
        for a in (inputs[0], queries[0], w_kv, grad_out[0])
    ]
    out, gin, gw = layer(doc_lengths[0], *held, cosine, sine)
    return out[None], gin[None], gw


def solution(mesh):
    in_specs = (
        P("fsdp", "seq", None),
        P("fsdp", "seq", None),
        P("fsdp", None),
        P("fsdp", None),
        P("fsdp", "seq", None),
    )
    out_specs = (P("fsdp", "seq", None), P("fsdp", "seq", None), P("fsdp", "seq"))
    return jax.shard_map(
        on_device, mesh=mesh, in_specs=in_specs, out_specs=out_specs, check_vma=False
    )
```

```python
import functools

import jax
import jax.numpy as jnp
from jax import lax
from jax.experimental import pallas as pl
from jax.experimental.pallas import tpu as pltpu
from jax.sharding import PartitionSpec as P

D = 2304
HD = 128
WIN = 1024
SEQLEN = 2048
NDOC = 8
NZ = 8
NX = 4
NY = 4
ROWS = D // (NX * NY)
HALF = 1024
PART = 512
TOK = 128
CTOK = 256
CAP = 50.0
SCALE = 1.0 / 12.0
ROPE_BASE = 10000.0
MESH = pl.DeviceIdType.MESH
HBM = pl.BlockSpec(memory_space=pltpu.HBM)
VM = pl.BlockSpec(memory_space=pltpu.VMEM)
BF = jnp.bfloat16
F32 = jnp.float32


def where_am_i():
    s = lax.axis_index("seq")
    f = lax.axis_index("fsdp")
    z = s // 2
    c = s - 2 * z
    x = f // NY
    y = f - NY * x
    return s, f, z, c, x, y


def ring(v, n):
    return lax.rem(v + n, n)


def remote(src, dst, send, recv, s, f):
    return pltpu.make_async_remote_copy(
        src_ref=src,
        dst_ref=dst,
        send_sem=send,
        recv_sem=recv,
        device_id={"seq": s, "fsdp": f},
        device_id_type=MESH,
    )


def enter(s, f, x, y):
    barrier = pltpu.get_barrier_semaphore()
    for step in range(1, 2 * NZ):
        pl.semaphore_signal(
            barrier,
            inc=1,
            device_id={"seq": ring(s + step, 2 * NZ), "fsdp": f},
            device_id_type=MESH,
        )
    for dx, dy in ((1, 0), (-1, 0), (0, 1), (0, -1)):
        pl.semaphore_signal(
            barrier,
            inc=1,
            device_id={"seq": s, "fsdp": ring(x + dx, NX) * NY + ring(y + dy, NY)},
            device_id_type=MESH,
        )
    pl.semaphore_wait(barrier, 2 * NZ - 1 + 4)


def other_chip(s, z):
    return s + 2 - 4 * lax.rem(z, 2)


def rotated(values, cosine, sine):
    return values * cosine + pltpu.roll(values, HD // 2, 1) * sine


def project_part(
    x_ref,
    q_ref,
    w_ref,
    g_ref,
    cos_ref,
    sin_ref,
    qh_ref,
    gh_ref,
    kv_ref,
    xt,
    xp,
    wg,
    xs,
    xo,
    proj,
    wl_sem,
    xl_sem,
    xr_sem,
    xc_sem,
    ws_sem,
    wr_sem,
    ql_sem,
    qs_sem,
    qr_sem,
    ks_sem,
    kr_sem,
    fs_sem,
    fr_sem,
):
    s, f, z, c, x, y = where_am_i()
    sib = s + 1 - 2 * c
    own_rows = pl.ds(pl.multiple_of(f * ROWS, 16), ROWS)
    load_w = []
    for k in range(8):
        cols = pl.ds(pl.multiple_of((2 * k + c) * HD, HD), HD)
        load_w.append(
            pltpu.make_async_copy(
                w_ref.at[:, cols], wg.at[own_rows, pl.ds(k * HD, HD)], wl_sem.at[k]
            )
        )
    for copy in load_w:
        copy.start()
    own_tok = pl.ds(pl.multiple_of(c * TOK, TOK), TOK)
    load_x = pltpu.make_async_copy(x_ref, xs.at[own_tok], xl_sem)
    load_x.start()
    enter(s, f, x, y)

    wide = PART // 2

    def piece(phase, part, off, half):
        origin = ring(x + off[0], NX) * NY + ring(y + off[1], NY)
        rows = pl.ds(pl.multiple_of(origin * ROWS, 16), ROWS)
        base = phase * PART + part * wide
        if half is None:
            return wg.at[rows, pl.ds(base, wide)]
        return wg.at[rows, pl.ds(base + half * (wide // 2), wide // 2)]

    sends = []

    def pass_on(phase, part, off, step, half=None):
        there = tuple((o - d) % 4 for o, d in zip(off, step))
        there = tuple(-1 if t == 3 else t for t in there)
        ref = piece(phase, part, off, half)
        copy = remote(
            ref,
            ref,
            ws_sem.at[len(sends)],
            wr_sem.at[phase, part, there[0] + 1, there[1] + 1, half or 0],
            s,
            ring(x + step[0], NX) * NY + ring(y + step[1], NY),
        )
        copy.start()
        sends.append(copy)

    def arrived(phase, part, off, half=None):
        ref = piece(phase, part, off, half)
        sem = wr_sem.at[phase, part, off[0] + 1, off[1] + 1, half or 0]
        pltpu.make_async_copy(ref, ref, sem).wait()

    def at(part, a, b):
        return (a, b) if part == 0 else (b, a)

    def begin(p):
        for d in (1, -1):
            for part in range(2):
                pass_on(p, part, (0, 0), at(part, d, 0))
        for d in (1, -1):
            for part in range(2):
                pass_on(p, part, (0, 0), at(part, 0, d))

    def near_first(p):
        for d in (-1, 1):
            for part in range(2):
                arrived(p, part, at(part, d, 0))
                pass_on(p, part, at(part, d, 0), at(part, -d, 0), 0 if d < 0 else 1)
                for e in (1, -1):
                    pass_on(p, part, at(part, d, 0), at(part, 0, e))

    def near_second(p):
        for d in (-1, 1):
            for part in range(2):
                arrived(p, part, at(part, 0, d))
                pass_on(p, part, at(part, 0, d), at(part, 0, -d), 0 if d < 0 else 1)

    def far_first(p):
        for part in range(2):
            arrived(p, part, at(part, 2, 0), 0)
            arrived(p, part, at(part, 2, 0), 1)
            for e in (1, -1):
                pass_on(p, part, at(part, 2, 0), at(part, 0, e))

    def rest_second(p):
        for a in (-1, 1, 2):
            for d in (-1, 1):
                for part in range(2):
                    arrived(p, part, at(part, a, d))
                    pass_on(p, part, at(part, a, d), at(part, 0, -d), 0 if d < 0 else 1)

    def finish(p):
        for a in (0, -1, 1, 2):
            for part in range(2):
                arrived(p, part, at(part, a, 2), 0)
                arrived(p, part, at(part, a, 2), 1)

    def kv_copy(k):
        kind = k // 4
        to = 2 * (2 * (k % 4) + c) + z // 4
        rows = pl.ds(pl.multiple_of(z * CTOK, CTOK), CTOK)
        local = pltpu.make_async_copy(proj.at[k], kv_ref.at[kind, rows], kr_sem.at[kind])
        away = remote(proj.at[k], kv_ref.at[kind, rows], ks_sem.at[k], kr_sem.at[kind], to, f)
        return to == s, local, away

    in_pair = pl.ds(pl.multiple_of(lax.rem(z, 2) * CTOK, CTOK), CTOK)

    def project(p):
        for t in (2 * p, 2 * p + 1):
            res = jnp.dot(xs[...], wg[:, t * 256 : (t + 1) * 256], preferred_element_type=F32)
            for j in range(2):
                k = 2 * t + j
                block = res[:, j * HD : (j + 1) * HD]
                if k < 4:
                    block = rotated(block, cos_ref[in_pair, :], sin_ref[in_pair, :])
                proj[k] = block.astype(BF)
                mine, local, away = kv_copy(k)

                @pl.when(mine)
                def _():
                    local.start()

                @pl.when(jnp.logical_not(mine))
                def _():
                    away.start()

    shares = []

    def share(p):
        half = kv_ref.at[p, pl.ds(pl.multiple_of(c * (SEQLEN // 2), SEQLEN // 2), SEQLEN // 2)]
        pltpu.make_async_copy(half, half, kr_sem.at[p]).wait()
        copy = remote(half, half, fs_sem.at[p], fr_sem.at[p], sib, f)
        copy.start()
        shares.append(copy)

    for copy in load_w:
        copy.wait()
    begin(0)
    load_x.wait()
    give_x = remote(xs.at[own_tok], xs.at[own_tok], xr_sem.at[0], xr_sem.at[1], sib, f)
    give_x.start()

    own_seq = pl.ds(pl.multiple_of(s * TOK, TOK), TOK)
    own_head = pl.ds(pl.multiple_of(s * HD, HD), HD)

    def deal(i, src, dst):
        pltpu.make_async_copy(src.at[:, own_head], dst.at[own_seq], ql_sem.at[i]).start()
        for step in range(1, 2 * NZ):
            to = ring(s + step, 2 * NZ)
            head = pl.ds(pl.multiple_of(to * HD, HD), HD)
            remote(src.at[:, head], dst.at[own_seq], qs_sem.at[i], qr_sem.at[i], to, f).start()

    def dealt(i, src, dst):
        pltpu.make_async_copy(src.at[:, own_head], dst.at[own_seq], ql_sem.at[i]).wait()
        others = dst.at[pl.ds(0, SEQLEN - TOK)]
        pltpu.make_async_copy(others, others, qs_sem.at[i]).wait()
        pltpu.make_async_copy(others, others, qr_sem.at[i]).wait()

    deal(0, q_ref, qh_ref)
    deal(1, g_ref, gh_ref)

    near_first(0)
    begin(1)
    near_second(0)
    far_first(0)
    near_first(1)
    rest_second(0)
    near_second(1)
    far_first(1)
    finish(0)
    give_x.wait_recv()
    project(0)
    rest_second(1)
    finish(1)
    project(1)
    cross = remote(
        xs.at[own_tok], xo.at[own_tok], xc_sem.at[0], xc_sem.at[1], other_chip(s, z), f
    )
    cross.start()
    share(0)
    def turn(i, carry):
        cols = pl.ds(pl.multiple_of(i * 256, 256), 256)
        xt[cols, :] = xs[:, cols].T
        return carry

    def turn_other(i, carry):
        cols = pl.ds(pl.multiple_of(i * 256, 256), 256)
        xp[cols, :] = xo[:, cols].T
        return carry

    lax.fori_loop(0, D // 256, turn, 0)
    for copy in sends:
        copy.wait_send()
    give_x.wait_send()
    dealt(0, q_ref, qh_ref)
    share(1)
    for k in range(8):
        mine, _, away = kv_copy(k)

        @pl.when(jnp.logical_not(mine))
        def _():
            away.wait_send()

    for copy in shares:
        copy.wait()
    spread = remote(xo.at[own_tok], xo.at[own_tok], xc_sem.at[2], xc_sem.at[3], sib, f)

    def pass_tokens():
        cross.wait_recv()
        spread.start()

    def take_tokens():
        spread.wait()
        lax.fori_loop(0, D // 256, turn_other, 0)
        cross.wait_send()

    return lambda: dealt(1, g_ref, gh_ref), pass_tokens, take_tokens


QT = 256
KT = 256
NT = (((1,), (1,)), ((), ()))
LOG2E = 1.4426950408889634


def gradient_part(
    waits,
    len_ref,
    q_ref,
    g_ref,
    kv_ref,
    xt,
    xp,
    wv,
    cos_ref,
    sin_ref,
    out_ref,
    gin_ref,
    gw_ref,
    vt,
    ot,
    wbuf,
    tbuf,
    inv,
    delt,
    gs,
    obuf,
    dkv,
    theirs,
    total,
    got,
    dd,
    da,
    gi,
    gsend,
    grecv,
    part_sum,
    r1,
    r2,
    second,
    r3,
    third,
    zr,
    ws_sem,
    wr_sem,
    ds_sem,
    dr_sem,
    ol_sem,
    os_sem,
    or_sem,
    as_sem,
    ar_sem,
    g_sem,
    s1_sem,
    r1_sem,
    s2_sem,
    r2_sem,
    s3_sem,
    r3_sem,
    zs_sem,
    zr_sem,
):
    s, f, z, c, x, y = where_am_i()
    sib = s + 1 - 2 * c
    e = lax.rem(z, 2)
    pair = z // 2
    partner = other_chip(s, z)
    def landed(ref, sem):
        pltpu.make_async_copy(ref, ref, sem).wait()

    ends = []
    so_far = 0
    for i in range(NDOC):
        so_far = so_far + len_ref[i]
        ends.append(so_far)

    def flip(i, carry):
        rows = pl.ds(pl.multiple_of(i * KT, KT), KT)
        vt[:, rows] = kv_ref[1, rows, :].T
        return carry

    lax.fori_loop(0, SEQLEN // KT, flip, 0)

    def tile_rows(i):
        return pl.ds(pl.multiple_of(i * KT, KT), KT)

    def swap(i):
        rows = tile_rows(i)
        return remote(
            dkv.at[1 - c, rows], theirs.at[rows], ws_sem.at[i], wr_sem.at[i], sib, f
        )

    def forward(i, n):
        base = i * QT
        rows = tile_rows(i)
        pos = base + lax.broadcasted_iota(jnp.int32, (1, QT), 1)
        start = jnp.zeros((1, QT), jnp.int32)
        for end in ends:
            start = jnp.where(pos >= end, end, start)
        low = jnp.maximum(start, pos - (WIN - 1))
        first = i + 1 - n
        qt = q_ref[rows, :]
        acc = jnp.zeros((HD, QT), F32)
        norm = jnp.zeros((1, QT), F32)
        key = lax.broadcasted_iota(jnp.int32, (KT, QT), 0)
        for j in range(n):
            span = tile_rows(first + j)
            st = lax.dot_general(kv_ref[0, span, :], qt, NT, preferred_element_type=F32)
            squashed = jnp.tanh(st * (SCALE / CAP))
            allowed = key >= low - (first + j) * KT
            if j == n - 1:
                allowed = allowed & (key <= pos - (first + j) * KT)
            weight = jnp.where(allowed, jnp.exp2((CAP * LOG2E) * squashed), 0.0)
            short = weight.astype(BF)
            norm = norm + jnp.sum(weight, axis=0, keepdims=True)
            wbuf[first + j, n - 1 - j] = weight * (1.0 - squashed * squashed)
            tbuf[first + j, n - 1 - j] = short
            acc = acc + jnp.dot(vt[:, span], short, preferred_element_type=F32)
        inverse = 1.0 / norm
        out_t = (acc * inverse).astype(BF)
        obuf[rows, :] = out_t.T
        inv[i] = inverse
        ot[:, rows] = out_t

    def prepare(i, carry):
        rows = tile_rows(i)
        gt_t = g_ref[rows, :].astype(F32).T
        delt[i] = jnp.sum(gt_t * ot[:, rows].astype(F32), axis=0, keepdims=True)
        gs[rows, :] = (gt_t * inv[i]).T.astype(BF)
        return carry

    def backward(t, n):
        span = tile_rows(t)
        dk = jnp.zeros((KT, HD), F32)
        dv = jnp.zeros((KT, HD), F32)
        for j in range(n):
            rows = tile_rows(t + j)
            dprob = lax.dot_general(
                kv_ref[1, span, :], g_ref[rows, :], NT, preferred_element_type=F32
            )
            dscore = (wbuf[t, j] * inv[t + j] * (dprob - delt[t + j])).astype(BF)
            dk = dk + jnp.dot(dscore, q_ref[rows, :], preferred_element_type=F32)
            dv = dv + jnp.dot(tbuf[t, j], gs[rows, :], preferred_element_type=F32)
        dkv[0, span, :] = (dk * SCALE).astype(BF)
        dkv[1, span, :] = dv.astype(BF)

    head_dev = lax.rem(z, 4)

    def d_copy(i):
        rows = tile_rows(i)
        to = 4 * (i // 2) + head_dev
        dst = got.at[2 * c + z // 4, pl.ds(pl.multiple_of(lax.rem(i, 2) * CTOK, CTOK), CTOK)]
        local = pltpu.make_async_copy(total.at[rows], dst, dr_sem.at[c])
        away = remote(total.at[rows], dst, ds_sem.at[i], dr_sem.at[c], to, f)
        return to == s, local, away

    def hand_over(i):
        rows = tile_rows(i)
        landed(theirs.at[rows], wr_sem.at[i])
        total[rows, :] = (dkv[c, rows, :].astype(F32) + theirs[rows, :].astype(F32)).astype(BF)
        mine, local, away = d_copy(i)

        @pl.when(mine)
        def _():
            local.start()

        @pl.when(jnp.logical_not(mine))
        def _():
            away.start()

    def long_tile(k, carry):
        forward(k + 4, 5)
        return carry

    for i in range(4):
        forward(jnp.int32(i), i + 1)
    lax.fori_loop(0, 4, long_tile, 0)

    wait_g, pass_tokens, take_tokens = waits
    wait_g()
    lax.fori_loop(0, SEQLEN // QT, prepare, 0)

    tiles = SEQLEN // KT

    def key_tile(k, carry):
        t = ring(z + k, tiles)
        count = jnp.minimum(tiles - t, 5)
        for n in range(1, 6):

            @pl.when(count == n)
            def _():
                backward(t, n)

        swap(t).start()

        @pl.when(k > 0)
        def _():
            hand_over(ring(t - 1, tiles))

        return carry

    lax.fori_loop(0, tiles, key_tile, 0)
    hand_over(ring(z - 1, tiles))
    pass_tokens()
    take_tokens()

    own_tok = pl.ds(pl.multiple_of(e * CTOK, CTOK), CTOK)
    pair_tok = pl.ds(pl.multiple_of((1 - e) * CTOK, CTOK), CTOK)

    def a_cols(b, side):
        return pl.ds(pl.multiple_of((side + 2 * b) * HD, HD), HD)

    def a_copy(b):
        return remote(
            dd.at[b, pair_tok], da.at[:, a_cols(b, e)], as_sem.at[b], ar_sem.at[b], partner, f
        )

    def take_in(kind):
        blocks = got.at[pl.ds(2 * kind, 2)]
        landed(blocks, dr_sem.at[kind])
        for b in range(2 * kind, 2 * kind + 2):
            block = got[b]
            if kind == 0:
                block = rotated(block.astype(F32), cos_ref[...], -sin_ref[...]).astype(BF)
            dd[b] = block

    def trade(kind):
        for b in range(2 * kind, 2 * kind + 2):
            a_copy(b).start()
            da[:, a_cols(b, e)] = dd[b, own_tok, :]

    def chunk(p, part, a):
        for j in range(4):
            cx, cy = (a, j) if part == 0 else (j, a)
            rows = pl.ds(pl.multiple_of((cx * NY + cy) * ROWS, 16), ROWS)
            part_sum[p, part, cx, cy] = (
                jnp.dot(xt[rows, :], dd[2 * p + part, own_tok, :], preferred_element_type=F32)
                + jnp.dot(xp[rows, :], dd[2 * p + part, pair_tok, :], preferred_element_type=F32)
            ).astype(BF)

    def chunk_ref(p, part, a, which):
        if part == 0:
            return part_sum.at[p, part, a, which]
        return part_sum.at[p, part, which, a]

    first_axis = (x, y)
    second_axis = (y, x)

    def neighbour(part, level, d):
        if (part == 0) == (level == 0):
            return ring(x + d, NX) * NY + y
        return x * NY + ring(y + d, NY)

    halves = (pl.ds(0, 2), pl.ds(2, 2))
    full = pl.ds(0, 4)
    dirs = (1, -1)
    sent = []

    def go(src, dst, send, recv, to_f):
        copy = remote(src, dst, send, recv, s, to_f)
        copy.start()
        sent.append(copy)

    def far(p):
        for part in range(2):
            a = ring(first_axis[part] + 2, 4)
            chunk(p, part, a)
            for h, d in enumerate(dirs):
                go(
                    chunk_ref(p, part, a, halves[h]),
                    r1.at[p, part, h],
                    s1_sem.at[p, part, h],
                    r1_sem.at[p, part, h],
                    neighbour(part, 0, d),
                )

    def near(p):
        for part in range(2):
            for d in (1, -1, 0):
                chunk(p, part, ring(first_axis[part] + d, 4))

    def hop(p):
        for h, d in enumerate(dirs):
            for part in range(2):
                a = ring(first_axis[part] + d, 4)
                landed(r1.at[p, part, h], r1_sem.at[p, part, h])
                for k in range(2):
                    j = 2 * h + k
                    idx = (p, part, a, j) if part == 0 else (p, part, j, a)
                    part_sum[idx] = (
                        part_sum[idx].astype(F32) + r1[p, part, h, k].astype(F32)
                    ).astype(BF)
                go(
                    chunk_ref(p, part, a, full),
                    r2.at[p, part, h],
                    s2_sem.at[p, part, h],
                    r2_sem.at[p, part, h],
                    neighbour(part, 0, d),
                )

    def across(p):
        for part in range(2):
            for h in range(2):
                landed(r2.at[p, part, h], r2_sem.at[p, part, h])
            for j in range(4):
                idx = (p, part, x, j) if part == 0 else (p, part, j, y)
                second[p, part, j] = (
                    part_sum[idx].astype(F32)
                    + r2[p, part, 0, j].astype(F32)
                    + r2[p, part, 1, j].astype(F32)
                ).astype(BF)
            for i, d in enumerate((2, 1, -1)):
                go(
                    second.at[p, part, ring(second_axis[part] + d, 4)],
                    r3.at[p, part, i],
                    s3_sem.at[p, part, i],
                    r3_sem.at[p, part, i],
                    neighbour(part, 1, d),
                )

    def z_copy(b):
        to = 2 * (2 * b + e) + c
        return pair != b, remote(third.at[b], zr.at[pair], zs_sem.at[b], zr_sem, to, f)

    def along(p):
        for part in range(2):
            b = 2 * p + part
            acc = second[p, part, second_axis[part]].astype(F32)
            for i in range(3):
                landed(r3.at[p, part, i], r3_sem.at[p, part, i])
                acc = acc + r3[p, part, i].astype(F32)
            third[b] = acc.astype(BF)
            away, copy = z_copy(b)

            @pl.when(away)
            def _():
                copy.start()

    take_in(0)
    far(0)
    near(0)
    take_in(1)
    far(1)
    trade(0)
    trade(1)
    own_head = pl.ds(pl.multiple_of(s * HD, HD), HD)
    own_seq = pl.ds(pl.multiple_of(s * TOK, TOK), TOK)
    keep_o = pltpu.make_async_copy(obuf.at[own_seq], out_ref.at[:, own_head], ol_sem)
    keep_o.start()
    for step in range(1, 2 * NZ):
        to = ring(s + step, 2 * NZ)
        theirs_tok = pl.ds(pl.multiple_of(to * TOK, TOK), TOK)
        remote(
            obuf.at[theirs_tok], out_ref.at[:, own_head], os_sem, or_sem, to, f
        ).start()
    hop(0)
    near(1)
    hop(1)
    across(0)

    for b in range(4):
        landed(da.at[:, a_cols(b, 1 - e)], ar_sem.at[b])

    def input_tile(i, carry):
        rows = pl.ds(pl.multiple_of(i * 256, 256), 256)
        gi[:, rows] = lax.dot_general(da[...], wv[rows, :], NT, preferred_element_type=F32)
        return carry

    lax.fori_loop(0, D // 256, input_tile, 0)
    mine_tok = pl.ds(pl.multiple_of(c * TOK, TOK), TOK)
    sib_tok = pl.ds(pl.multiple_of((1 - c) * TOK, TOK), TOK)
    gsend[...] = gi[sib_tok, :].astype(BF)
    give = remote(gsend, grecv, g_sem.at[0], g_sem.at[1], sib, f)
    give.start()
    along(0)
    across(1)
    give.wait()
    gin_ref[...] = (gi[mine_tok, :] + grecv[...].astype(F32)).astype(BF)
    along(1)
    for copy in sent:
        copy.wait_send()
    for b in range(4):
        a_copy(b).wait_send()

    def settle(i, carry):
        swap(i).wait_send()
        mine, _, away = d_copy(i)

        @pl.when(jnp.logical_not(mine))
        def _():
            away.wait_send()

        return carry

    lax.fori_loop(0, SEQLEN // QT, settle, 0)
    keep_o.wait()
    others = obuf.at[pl.ds(0, SEQLEN - TOK)]
    landed(others, os_sem)
    landed(others, or_sem)
    for b in range(4):
        away, copy = z_copy(b)

        @pl.when(away)
        def _():
            copy.wait_send()

    rest = zr.at[pl.ds(1, 3)]
    landed(rest, zr_sem)
    acc = third[pair].astype(F32)
    for step in range(1, 4):
        acc = acc + zr[ring(pair + step, 4)].astype(F32)
    gw_ref[...] = acc


def whole_kernel(
    len_ref, x_ref, q_ref, w_ref, g_ref, cos_ref, sin_ref, out_ref, gin_ref, gw_ref, *scratch
):
    qh, gh, kv, xt, xp, wg = scratch[:6]
    first, second = scratch[:PROJECT_SCRATCH], scratch[PROJECT_SCRATCH:]
    waits = project_part(x_ref, q_ref, w_ref, g_ref, cos_ref, sin_ref, *first)
    gradient_part(
        waits, len_ref, qh, gh, kv, xt, xp, wg, cos_ref, sin_ref, out_ref, gin_ref, gw_ref, *second
    )


PROJECT_SCRATCH = 22


def layer(lengths, x, q, w, g, cosine, sine):
    dma = pltpu.SemaphoreType.DMA
    return pl.pallas_call(
        whole_kernel,
        out_shape=(
            jax.ShapeDtypeStruct((TOK, 2048), BF),
            jax.ShapeDtypeStruct((TOK, D), BF),
            jax.ShapeDtypeStruct((ROWS, HD), F32),
        ),
        in_specs=[pl.BlockSpec(memory_space=pltpu.SMEM), HBM, HBM, HBM, HBM, VM, VM],
        out_specs=(VM, VM, VM),
        scratch_shapes=[
            pltpu.VMEM((SEQLEN, HD), BF),
            pltpu.VMEM((SEQLEN, HD), BF),
            pltpu.VMEM((2, SEQLEN, HD), BF),
            pltpu.VMEM((D, CTOK), BF),
            pltpu.VMEM((D, CTOK), BF),
            pltpu.VMEM((D, HALF), BF),
            pltpu.VMEM((CTOK, D), BF),
            pltpu.VMEM((CTOK, D), BF),
            pltpu.VMEM((8, CTOK, HD), BF),
            dma((8,)),
            dma(()),
            dma((2,)),
            dma((4,)),
            dma((80,)),
            dma((2, 2, 4, 4, 2)),
            dma((2,)),
            dma((2,)),
            dma((2,)),
            dma((8,)),
            dma((2,)),
            dma((2,)),
            dma((2,)),
            pltpu.VMEM((HD, SEQLEN), BF),
            pltpu.VMEM((HD, SEQLEN), BF),
            pltpu.VMEM((8, 5, KT, QT), F32),
            pltpu.VMEM((8, 5, KT, QT), BF),
            pltpu.VMEM((8, 1, QT), F32),
            pltpu.VMEM((8, 1, QT), F32),
            pltpu.VMEM((SEQLEN, HD), BF),
            pltpu.VMEM((SEQLEN, HD), BF),
            pltpu.VMEM((2, SEQLEN, HD), BF),
            pltpu.VMEM((SEQLEN, HD), BF),
            pltpu.VMEM((SEQLEN, HD), BF),
            pltpu.VMEM((4, 2 * CTOK, HD), BF),
            pltpu.VMEM((4, 2 * CTOK, HD), BF),
            pltpu.VMEM((CTOK, HALF), BF),
            pltpu.VMEM((CTOK, D), F32),
            pltpu.VMEM((TOK, D), BF),
            pltpu.VMEM((TOK, D), BF),
            pltpu.VMEM((2, 2, 4, 4, ROWS, HD), BF),
            pltpu.VMEM((2, 2, 2, 2, ROWS, HD), BF),
            pltpu.VMEM((2, 2, 2, 4, ROWS, HD), BF),
            pltpu.VMEM((2, 2, 4, ROWS, HD), BF),
            pltpu.VMEM((2, 2, 3, ROWS, HD), BF),
            pltpu.VMEM((4, ROWS, HD), BF),
            pltpu.VMEM((4, ROWS, HD), BF),
            dma((8,)),
            dma((8,)),
            dma((8,)),
            dma((2,)),
            dma(()),
            dma(()),
            dma(()),
            dma((4,)),
            dma((4,)),
            dma((2,)),
            dma((2, 2, 2)),
            dma((2, 2, 2)),
            dma((2, 2, 2)),
            dma((2, 2, 2)),
            dma((2, 2, 3)),
            dma((2, 2, 3)),
            dma((4,)),
            dma(()),
        ],
        compiler_params=pltpu.CompilerParams(
            collective_id=0, has_side_effects=True, vmem_limit_bytes=50 << 20
        ),
        name="layer",
    )(lengths, x, q, w, g, cosine, sine)


def tables(lengths):
    pair = lax.axis_index("seq") // 4
    places = pair * (2 * CTOK) + jnp.arange(2 * CTOK, dtype=jnp.int32)
    order = jnp.arange(NDOC)
    doc_ends = jnp.sum(jnp.where(order[:, None] <= order[None, :], lengths[:, None], 0), axis=0)
    ended = doc_ends[None, :] <= places[:, None]
    within = places - jnp.sum(jnp.where(ended, lengths[None, :], 0), axis=1)
    exponent = jnp.arange(HD // 2, dtype=F32) * (2.0 / HD)
    rate = jnp.power(ROPE_BASE, -exponent)
    angles = within.astype(F32)[:, None] * rate[None, :]
    cosine, sine = jnp.cos(angles), jnp.sin(angles)
    return (
        jnp.concatenate([cosine, cosine], axis=1),
        jnp.concatenate([-sine, sine], axis=1),
    )


def on_device(inputs, queries, w_kv, doc_lengths, grad_out):
    cosine, sine = tables(doc_lengths[0])
    held = [
        pltpu.with_memory_space_constraint(a, pltpu.HBM)
        for a in (inputs[0], queries[0], w_kv, grad_out[0])
    ]
    out, gin, gw = layer(doc_lengths[0], *held, cosine, sine)
    return out[None], gin[None], gw


def solution(mesh):
    in_specs = (
        P("fsdp", "seq", None),
        P("fsdp", "seq", None),
        P("fsdp", None),
        P("fsdp", None),
        P("fsdp", "seq", None),
    )
    out_specs = (P("fsdp", "seq", None), P("fsdp", "seq", None), P("fsdp", "seq"))
    return jax.shard_map(
        on_device, mesh=mesh, in_specs=in_specs, out_specs=out_specs, check_vma=False
    )
```

```python
import functools

import jax
import jax.numpy as jnp
from jax import lax
from jax.experimental import pallas as pl
from jax.experimental.pallas import tpu as pltpu
from jax.sharding import PartitionSpec as P

D = 2304
HD = 128
WIN = 1024
SEQLEN = 2048
NDOC = 8
NZ = 8
NX = 4
NY = 4
ROWS = D // (NX * NY)
HALF = 1024
PART = 512
TOK = 128
CTOK = 256
CAP = 50.0
SCALE = 1.0 / 12.0
ROPE_BASE = 10000.0
MESH = pl.DeviceIdType.MESH
HBM = pl.BlockSpec(memory_space=pltpu.HBM)
VM = pl.BlockSpec(memory_space=pltpu.VMEM)
BF = jnp.bfloat16
F32 = jnp.float32


def where_am_i():
    s = lax.axis_index("seq")
    f = lax.axis_index("fsdp")
    z = s // 2
    c = s - 2 * z
    x = f // NY
    y = f - NY * x
    return s, f, z, c, x, y


def ring(v, n):
    return lax.rem(v + n, n)


def remote(src, dst, send, recv, s, f):
    return pltpu.make_async_remote_copy(
        src_ref=src,
        dst_ref=dst,
        send_sem=send,
        recv_sem=recv,
        device_id={"seq": s, "fsdp": f},
        device_id_type=MESH,
    )


def enter(s, f, x, y):
    barrier = pltpu.get_barrier_semaphore()
    for step in range(1, 2 * NZ):
        pl.semaphore_signal(
            barrier,
            inc=1,
            device_id={"seq": ring(s + step, 2 * NZ), "fsdp": f},
            device_id_type=MESH,
        )
    for dx, dy in ((1, 0), (-1, 0), (0, 1), (0, -1)):
        pl.semaphore_signal(
            barrier,
            inc=1,
            device_id={"seq": s, "fsdp": ring(x + dx, NX) * NY + ring(y + dy, NY)},
            device_id_type=MESH,
        )
    pl.semaphore_wait(barrier, 2 * NZ - 1 + 4)


def other_chip(s, z):
    return s + 2 - 4 * lax.rem(z, 2)


def rotated(values, cosine, sine):
    return values * cosine + pltpu.roll(values, HD // 2, 1) * sine


def project_part(
    x_ref,
    q_ref,
    w_ref,
    g_ref,
    cos_ref,
    sin_ref,
    qh_ref,
    gh_ref,
    kv_ref,
    xt,
    xp,
    wg,
    xs,
    xo,
    proj,
    wl_sem,
    xl_sem,
    xr_sem,
    xc_sem,
    ws_sem,
    wr_sem,
    ql_sem,
    qs_sem,
    qr_sem,
    ks_sem,
    kr_sem,
    fs_sem,
    fr_sem,
):
    s, f, z, c, x, y = where_am_i()
    sib = s + 1 - 2 * c
    own_rows = pl.ds(pl.multiple_of(f * ROWS, 16), ROWS)
    load_w = []
    for k in range(8):
        cols = pl.ds(pl.multiple_of((2 * k + c) * HD, HD), HD)
        load_w.append(
            pltpu.make_async_copy(
                w_ref.at[:, cols], wg.at[own_rows, pl.ds(k * HD, HD)], wl_sem.at[k]
            )
        )
    for copy in load_w:
        copy.start()
    own_tok = pl.ds(pl.multiple_of(c * TOK, TOK), TOK)
    load_x = pltpu.make_async_copy(x_ref, xs.at[own_tok], xl_sem)
    load_x.start()
    enter(s, f, x, y)

    wide = PART // 2

    def piece(phase, part, off, half):
        origin = ring(x + off[0], NX) * NY + ring(y + off[1], NY)
        rows = pl.ds(pl.multiple_of(origin * ROWS, 16), ROWS)
        base = phase * PART + part * wide
        if half is None:
            return wg.at[rows, pl.ds(base, wide)]
        return wg.at[rows, pl.ds(base + half * (wide // 2), wide // 2)]

    sends = []

    def pass_on(phase, part, off, step, half=None):
        there = tuple((o - d) % 4 for o, d in zip(off, step))
        there = tuple(-1 if t == 3 else t for t in there)
        ref = piece(phase, part, off, half)
        copy = remote(
            ref,
            ref,
            ws_sem.at[len(sends)],
            wr_sem.at[phase, part, there[0] + 1, there[1] + 1, half or 0],
            s,
            ring(x + step[0], NX) * NY + ring(y + step[1], NY),
        )
        copy.start()
        sends.append(copy)

    def arrived(phase, part, off, half=None):
        ref = piece(phase, part, off, half)
        sem = wr_sem.at[phase, part, off[0] + 1, off[1] + 1, half or 0]
        pltpu.make_async_copy(ref, ref, sem).wait()

    def at(part, a, b):
        return (a, b) if part == 0 else (b, a)

    def begin(p):
        for d in (1, -1):
            for part in range(2):
                pass_on(p, part, (0, 0), at(part, d, 0))
        for d in (1, -1):
            for part in range(2):
                pass_on(p, part, (0, 0), at(part, 0, d))

    def near_first(p):
        for d in (-1, 1):
            for part in range(2):
                arrived(p, part, at(part, d, 0))
                pass_on(p, part, at(part, d, 0), at(part, -d, 0), 0 if d < 0 else 1)
                for e in (1, -1):
                    pass_on(p, part, at(part, d, 0), at(part, 0, e))

    def near_second(p):
        for d in (-1, 1):
            for part in range(2):
                arrived(p, part, at(part, 0, d))
                pass_on(p, part, at(part, 0, d), at(part, 0, -d), 0 if d < 0 else 1)

    def far_first(p):
        for part in range(2):
            arrived(p, part, at(part, 2, 0), 0)
            arrived(p, part, at(part, 2, 0), 1)
            for e in (1, -1):
                pass_on(p, part, at(part, 2, 0), at(part, 0, e))

    def rest_second(p):
        for a in (-1, 1, 2):
            for d in (-1, 1):
                for part in range(2):
                    arrived(p, part, at(part, a, d))
                    pass_on(p, part, at(part, a, d), at(part, 0, -d), 0 if d < 0 else 1)

    def finish(p):
        for a in (0, -1, 1, 2):
            for part in range(2):
                arrived(p, part, at(part, a, 2), 0)
                arrived(p, part, at(part, a, 2), 1)

    def kv_copy(k):
        kind = k // 4
        to = 2 * (2 * (k % 4) + c) + z // 4
        rows = pl.ds(pl.multiple_of(z * CTOK, CTOK), CTOK)
        local = pltpu.make_async_copy(proj.at[k], kv_ref.at[kind, rows], kr_sem.at[kind])
        away = remote(proj.at[k], kv_ref.at[kind, rows], ks_sem.at[k], kr_sem.at[kind], to, f)
        return to == s, local, away

    in_pair = pl.ds(pl.multiple_of(lax.rem(z, 2) * CTOK, CTOK), CTOK)

    def project(p):
        for t in (2 * p, 2 * p + 1):
            res = jnp.dot(xs[...], wg[:, t * 256 : (t + 1) * 256], preferred_element_type=F32)
            for j in range(2):
                k = 2 * t + j
                block = res[:, j * HD : (j + 1) * HD]
                if k < 4:
                    block = rotated(block, cos_ref[in_pair, :], sin_ref[in_pair, :])
                proj[k] = block.astype(BF)
                mine, local, away = kv_copy(k)

                @pl.when(mine)
                def _():
                    local.start()

                @pl.when(jnp.logical_not(mine))
                def _():
                    away.start()

    shares = []

    def share(p):
        half = kv_ref.at[p, pl.ds(pl.multiple_of(c * (SEQLEN // 2), SEQLEN // 2), SEQLEN // 2)]
        pltpu.make_async_copy(half, half, kr_sem.at[p]).wait()
        copy = remote(half, half, fs_sem.at[p], fr_sem.at[p], sib, f)
        copy.start()
        shares.append(copy)

    for copy in load_w:
        copy.wait()
    begin(0)
    load_x.wait()
    give_x = remote(xs.at[own_tok], xs.at[own_tok], xr_sem.at[0], xr_sem.at[1], sib, f)
    give_x.start()

    own_seq = pl.ds(pl.multiple_of(s * TOK, TOK), TOK)
    own_head = pl.ds(pl.multiple_of(s * HD, HD), HD)

    def deal(i, src, dst):
        pltpu.make_async_copy(src.at[:, own_head], dst.at[own_seq], ql_sem.at[i]).start()
        for step in range(1, 2 * NZ):
            to = ring(s + step, 2 * NZ)
            head = pl.ds(pl.multiple_of(to * HD, HD), HD)
            remote(src.at[:, head], dst.at[own_seq], qs_sem.at[i], qr_sem.at[i], to, f).start()

    def dealt(i, src, dst):
        pltpu.make_async_copy(src.at[:, own_head], dst.at[own_seq], ql_sem.at[i]).wait()
        others = dst.at[pl.ds(0, SEQLEN - TOK)]
        pltpu.make_async_copy(others, others, qs_sem.at[i]).wait()
        pltpu.make_async_copy(others, others, qr_sem.at[i]).wait()

    deal(0, q_ref, qh_ref)
    deal(1, g_ref, gh_ref)

    near_first(0)
    begin(1)
    near_second(0)
    far_first(0)
    near_first(1)
    rest_second(0)
    near_second(1)
    far_first(1)
    finish(0)
    give_x.wait_recv()
    project(0)
    rest_second(1)
    finish(1)
    project(1)
    cross = remote(
        xs.at[own_tok], xo.at[own_tok], xc_sem.at[0], xc_sem.at[1], other_chip(s, z), f
    )
    cross.start()
    share(0)
    def turn(i, carry):
        cols = pl.ds(pl.multiple_of(i * 256, 256), 256)
        xt[cols, :] = xs[:, cols].T
        return carry

    def turn_other(i, carry):
        cols = pl.ds(pl.multiple_of(i * 256, 256), 256)
        xp[cols, :] = xo[:, cols].T
        return carry

    lax.fori_loop(0, D // 256, turn, 0)
    for copy in sends:
        copy.wait_send()
    give_x.wait_send()
    dealt(0, q_ref, qh_ref)
    share(1)
    for k in range(8):
        mine, _, away = kv_copy(k)

        @pl.when(jnp.logical_not(mine))
        def _():
            away.wait_send()

    for copy in shares:
        copy.wait()
    spread = remote(xo.at[own_tok], xo.at[own_tok], xc_sem.at[2], xc_sem.at[3], sib, f)

    def pass_tokens():
        cross.wait_recv()
        spread.start()

    def take_tokens():
        spread.wait()
        lax.fori_loop(0, D // 256, turn_other, 0)
        cross.wait_send()

    return lambda: dealt(1, g_ref, gh_ref), pass_tokens, take_tokens


QT = 256
KT = 256
NT = (((1,), (1,)), ((), ()))
LOG2E = 1.4426950408889634


def gradient_part(
    waits,
    len_ref,
    q_ref,
    g_ref,
    kv_ref,
    xt,
    xp,
    wv,
    cos_ref,
    sin_ref,
    out_ref,
    gin_ref,
    gw_ref,
    vt,
    ot,
    wbuf,
    tbuf,
    inv,
    delt,
    gs,
    obuf,
    dkv,
    theirs,
    total,
    got,
    dd,
    da,
    gi,
    gsend,
    grecv,
    part_sum,
    r1,
    r2,
    second,
    r3,
    third,
    zr,
    ws_sem,
    wr_sem,
    ds_sem,
    dr_sem,
    ol_sem,
    os_sem,
    or_sem,
    as_sem,
    ar_sem,
    g_sem,
    s1_sem,
    r1_sem,
    s2_sem,
    r2_sem,
    s3_sem,
    r3_sem,
    zs_sem,
    zr_sem,
):
    s, f, z, c, x, y = where_am_i()
    sib = s + 1 - 2 * c
    e = lax.rem(z, 2)
    pair = z // 2
    partner = other_chip(s, z)
    def landed(ref, sem):
        pltpu.make_async_copy(ref, ref, sem).wait()

    ends = []
    so_far = 0
    for i in range(NDOC):
        so_far = so_far + len_ref[i]
        ends.append(so_far)

    def flip(i, carry):
        rows = pl.ds(pl.multiple_of(i * KT, KT), KT)
        vt[:, rows] = kv_ref[1, rows, :].T
        return carry

    lax.fori_loop(0, SEQLEN // KT, flip, 0)

    def tile_rows(i):
        return pl.ds(pl.multiple_of(i * KT, KT), KT)

    def swap(i):
        rows = tile_rows(i)
        return remote(
            dkv.at[1 - c, rows], theirs.at[rows], ws_sem.at[i], wr_sem.at[i], sib, f
        )

    def forward(i, n):
        base = i * QT
        rows = tile_rows(i)
        pos = base + lax.broadcasted_iota(jnp.int32, (1, QT), 1)
        start = jnp.zeros((1, QT), jnp.int32)
        for end in ends:
            start = jnp.where(pos >= end, end, start)
        low = jnp.maximum(start, pos - (WIN - 1))
        first = i + 1 - n
        qt = q_ref[rows, :]
        acc = jnp.zeros((HD, QT), F32)
        norm = jnp.zeros((1, QT), F32)
        key = lax.broadcasted_iota(jnp.int32, (KT, QT), 0)
        for j in range(n):
            span = tile_rows(first + j)
            st = lax.dot_general(kv_ref[0, span, :], qt, NT, preferred_element_type=F32)
            squashed = jnp.tanh(st * (SCALE / CAP))
            allowed = key >= low - (first + j) * KT
            if j == n - 1:
                allowed = allowed & (key <= pos - (first + j) * KT)
            weight = jnp.where(allowed, jnp.exp2((CAP * LOG2E) * squashed), 0.0)
            short = weight.astype(BF)
            norm = norm + jnp.sum(weight, axis=0, keepdims=True)
            wbuf[first + j, n - 1 - j] = weight * (1.0 - squashed * squashed)
            tbuf[first + j, n - 1 - j] = short
            acc = acc + jnp.dot(vt[:, span], short, preferred_element_type=F32)
        inverse = 1.0 / norm
        out_t = (acc * inverse).astype(BF)
        obuf[rows, :] = out_t.T
        inv[i] = inverse
        ot[:, rows] = out_t

    def prepare(i, carry):
        rows = tile_rows(i)
        gt_t = g_ref[rows, :].astype(F32).T
        delt[i] = jnp.sum(gt_t * ot[:, rows].astype(F32), axis=0, keepdims=True)
        gs[rows, :] = (gt_t * inv[i]).T.astype(BF)
        return carry

    def backward(t, n):
        span = tile_rows(t)
        dk = jnp.zeros((KT, HD), F32)
        dv = jnp.zeros((KT, HD), F32)
        for j in range(n):
            rows = tile_rows(t + j)
            dprob = lax.dot_general(
                kv_ref[1, span, :], g_ref[rows, :], NT, preferred_element_type=F32
            )
            dscore = (wbuf[t, j] * inv[t + j] * (dprob - delt[t + j])).astype(BF)
            dk = dk + jnp.dot(dscore, q_ref[rows, :], preferred_element_type=F32)
            dv = dv + jnp.dot(tbuf[t, j], gs[rows, :], preferred_element_type=F32)
        dkv[0, span, :] = (dk * SCALE).astype(BF)
        dkv[1, span, :] = dv.astype(BF)

    head_dev = lax.rem(z, 4)

    def d_copy(i):
        rows = tile_rows(i)
        to = 4 * (i // 2) + head_dev
        dst = got.at[2 * c + z // 4, pl.ds(pl.multiple_of(lax.rem(i, 2) * CTOK, CTOK), CTOK)]
        local = pltpu.make_async_copy(total.at[rows], dst, dr_sem.at[c])
        away = remote(total.at[rows], dst, ds_sem.at[i], dr_sem.at[c], to, f)
        return to == s, local, away

    def hand_over(i):
        rows = tile_rows(i)
        landed(theirs.at[rows], wr_sem.at[i])
        total[rows, :] = (dkv[c, rows, :].astype(F32) + theirs[rows, :].astype(F32)).astype(BF)
        mine, local, away = d_copy(i)

        @pl.when(mine)
        def _():
            local.start()

        @pl.when(jnp.logical_not(mine))
        def _():
            away.start()

    def long_tile(k, carry):
        forward(k + 4, 5)
        return carry

    for i in range(4):
        forward(jnp.int32(i), i + 1)
    lax.fori_loop(0, 4, long_tile, 0)

    wait_g, pass_tokens, take_tokens = waits
    wait_g()
    lax.fori_loop(0, SEQLEN // QT, prepare, 0)

    tiles = SEQLEN // KT

    def key_tile(k, carry):
        t = ring(z + k, tiles)
        count = jnp.minimum(tiles - t, 5)
        for n in range(1, 6):

            @pl.when(count == n)
            def _():
                backward(t, n)

        swap(t).start()

        @pl.when(k > 0)
        def _():
            hand_over(ring(t - 1, tiles))

        return carry

    lax.fori_loop(0, tiles, key_tile, 0)
    hand_over(ring(z - 1, tiles))
    pass_tokens()

    own_tok = pl.ds(pl.multiple_of(e * CTOK, CTOK), CTOK)
    pair_tok = pl.ds(pl.multiple_of((1 - e) * CTOK, CTOK), CTOK)

    def a_cols(b, side):
        return pl.ds(pl.multiple_of((side + 2 * b) * HD, HD), HD)

    def a_copy(b):
        return remote(
            dd.at[b, pair_tok], da.at[:, a_cols(b, e)], as_sem.at[b], ar_sem.at[b], partner, f
        )

    def take_in(kind):
        blocks = got.at[pl.ds(2 * kind, 2)]
        landed(blocks, dr_sem.at[kind])
        for b in range(2 * kind, 2 * kind + 2):
            block = got[b]
            if kind == 0:
                block = rotated(block.astype(F32), cos_ref[...], -sin_ref[...]).astype(BF)
            dd[b] = block

    def trade(kind):
        for b in range(2 * kind, 2 * kind + 2):
            a_copy(b).start()
            da[:, a_cols(b, e)] = dd[b, own_tok, :]

    def chunk(p, part, a):
        for j in range(4):
            cx, cy = (a, j) if part == 0 else (j, a)
            rows = pl.ds(pl.multiple_of((cx * NY + cy) * ROWS, 16), ROWS)
            part_sum[p, part, cx, cy] = (
                jnp.dot(xt[rows, :], dd[2 * p + part, own_tok, :], preferred_element_type=F32)
                + jnp.dot(xp[rows, :], dd[2 * p + part, pair_tok, :], preferred_element_type=F32)
            ).astype(BF)

    def chunk_ref(p, part, a, which):
        if part == 0:
            return part_sum.at[p, part, a, which]
        return part_sum.at[p, part, which, a]

    first_axis = (x, y)
    second_axis = (y, x)

    def neighbour(part, level, d):
        if (part == 0) == (level == 0):
            return ring(x + d, NX) * NY + y
        return x * NY + ring(y + d, NY)

    halves = (pl.ds(0, 2), pl.ds(2, 2))
    full = pl.ds(0, 4)
    dirs = (1, -1)
    sent = []

    def go(src, dst, send, recv, to_f):
        copy = remote(src, dst, send, recv, s, to_f)
        copy.start()
        sent.append(copy)

    def far(p):
        for part in range(2):
            a = ring(first_axis[part] + 2, 4)
            chunk(p, part, a)
            for h, d in enumerate(dirs):
                go(
                    chunk_ref(p, part, a, halves[h]),
                    r1.at[p, part, h],
                    s1_sem.at[p, part, h],
                    r1_sem.at[p, part, h],
                    neighbour(part, 0, d),
                )

    def near(p):
        for part in range(2):
            for d in (1, -1, 0):
                chunk(p, part, ring(first_axis[part] + d, 4))

    def hop(p):
        for h, d in enumerate(dirs):
            for part in range(2):
                a = ring(first_axis[part] + d, 4)
                landed(r1.at[p, part, h], r1_sem.at[p, part, h])
                for k in range(2):
                    j = 2 * h + k
                    idx = (p, part, a, j) if part == 0 else (p, part, j, a)
                    part_sum[idx] = (
                        part_sum[idx].astype(F32) + r1[p, part, h, k].astype(F32)
                    ).astype(BF)
                go(
                    chunk_ref(p, part, a, full),
                    r2.at[p, part, h],
                    s2_sem.at[p, part, h],
                    r2_sem.at[p, part, h],
                    neighbour(part, 0, d),
                )

    def across(p):
        for part in range(2):
            for h in range(2):
                landed(r2.at[p, part, h], r2_sem.at[p, part, h])
            for j in range(4):
                idx = (p, part, x, j) if part == 0 else (p, part, j, y)
                second[p, part, j] = (
                    part_sum[idx].astype(F32)
                    + r2[p, part, 0, j].astype(F32)
                    + r2[p, part, 1, j].astype(F32)
                ).astype(BF)
            for i, d in enumerate((2, 1, -1)):
                go(
                    second.at[p, part, ring(second_axis[part] + d, 4)],
                    r3.at[p, part, i],
                    s3_sem.at[p, part, i],
                    r3_sem.at[p, part, i],
                    neighbour(part, 1, d),
                )

    def z_copy(b):
        to = 2 * (2 * b + e) + c
        return pair != b, remote(third.at[b], zr.at[pair], zs_sem.at[b], zr_sem, to, f)

    def along(p):
        for part in range(2):
            b = 2 * p + part
            acc = second[p, part, second_axis[part]].astype(F32)
            for i in range(3):
                landed(r3.at[p, part, i], r3_sem.at[p, part, i])
                acc = acc + r3[p, part, i].astype(F32)
            third[b] = acc.astype(BF)
            away, copy = z_copy(b)

            @pl.when(away)
            def _():
                copy.start()

    take_in(0)
    trade(0)
    take_in(1)
    trade(1)
    take_tokens()
    far(0)
    near(0)
    far(1)
    own_head = pl.ds(pl.multiple_of(s * HD, HD), HD)
    own_seq = pl.ds(pl.multiple_of(s * TOK, TOK), TOK)
    keep_o = pltpu.make_async_copy(obuf.at[own_seq], out_ref.at[:, own_head], ol_sem)
    keep_o.start()
    for step in range(1, 2 * NZ):
        to = ring(s + step, 2 * NZ)
        theirs_tok = pl.ds(pl.multiple_of(to * TOK, TOK), TOK)
        remote(
            obuf.at[theirs_tok], out_ref.at[:, own_head], os_sem, or_sem, to, f
        ).start()
    hop(0)
    near(1)
    hop(1)
    across(0)

    for b in range(4):
        landed(da.at[:, a_cols(b, 1 - e)], ar_sem.at[b])

    def input_tile(i, carry):
        rows = pl.ds(pl.multiple_of(i * 256, 256), 256)
        gi[:, rows] = lax.dot_general(da[...], wv[rows, :], NT, preferred_element_type=F32)
        return carry

    lax.fori_loop(0, D // 256, input_tile, 0)
    mine_tok = pl.ds(pl.multiple_of(c * TOK, TOK), TOK)
    sib_tok = pl.ds(pl.multiple_of((1 - c) * TOK, TOK), TOK)
    gsend[...] = gi[sib_tok, :].astype(BF)
    give = remote(gsend, grecv, g_sem.at[0], g_sem.at[1], sib, f)
    give.start()
    along(0)
    across(1)
    give.wait()
    gin_ref[...] = (gi[mine_tok, :] + grecv[...].astype(F32)).astype(BF)
    along(1)
    for copy in sent:
        copy.wait_send()
    for b in range(4):
        a_copy(b).wait_send()

    def settle(i, carry):
        swap(i).wait_send()
        mine, _, away = d_copy(i)

        @pl.when(jnp.logical_not(mine))
        def _():
            away.wait_send()

        return carry

    lax.fori_loop(0, SEQLEN // QT, settle, 0)
    keep_o.wait()
    others = obuf.at[pl.ds(0, SEQLEN - TOK)]
    landed(others, os_sem)
    landed(others, or_sem)
    for b in range(4):
        away, copy = z_copy(b)

        @pl.when(away)
        def _():
            copy.wait_send()

    rest = zr.at[pl.ds(1, 3)]
    landed(rest, zr_sem)
    acc = third[pair].astype(F32)
    for step in range(1, 4):
        acc = acc + zr[ring(pair + step, 4)].astype(F32)
    gw_ref[...] = acc


def whole_kernel(
    len_ref, x_ref, q_ref, w_ref, g_ref, cos_ref, sin_ref, out_ref, gin_ref, gw_ref, *scratch
):
    qh, gh, kv, xt, xp, wg = scratch[:6]
    first, second = scratch[:PROJECT_SCRATCH], scratch[PROJECT_SCRATCH:]
    waits = project_part(x_ref, q_ref, w_ref, g_ref, cos_ref, sin_ref, *first)
    gradient_part(
        waits, len_ref, qh, gh, kv, xt, xp, wg, cos_ref, sin_ref, out_ref, gin_ref, gw_ref, *second
    )


PROJECT_SCRATCH = 22


def layer(lengths, x, q, w, g, cosine, sine):
    dma = pltpu.SemaphoreType.DMA
    return pl.pallas_call(
        whole_kernel,
        out_shape=(
            jax.ShapeDtypeStruct((TOK, 2048), BF),
            jax.ShapeDtypeStruct((TOK, D), BF),
            jax.ShapeDtypeStruct((ROWS, HD), F32),
        ),
        in_specs=[pl.BlockSpec(memory_space=pltpu.SMEM), HBM, HBM, HBM, HBM, VM, VM],
        out_specs=(VM, VM, VM),
        scratch_shapes=[
            pltpu.VMEM((SEQLEN, HD), BF),
            pltpu.VMEM((SEQLEN, HD), BF),
            pltpu.VMEM((2, SEQLEN, HD), BF),
            pltpu.VMEM((D, CTOK), BF),
            pltpu.VMEM((D, CTOK), BF),
            pltpu.VMEM((D, HALF), BF),
            pltpu.VMEM((CTOK, D), BF),
            pltpu.VMEM((CTOK, D), BF),
            pltpu.VMEM((8, CTOK, HD), BF),
            dma((8,)),
            dma(()),
            dma((2,)),
            dma((4,)),
            dma((80,)),
            dma((2, 2, 4, 4, 2)),
            dma((2,)),
            dma((2,)),
            dma((2,)),
            dma((8,)),
            dma((2,)),
            dma((2,)),
            dma((2,)),
            pltpu.VMEM((HD, SEQLEN), BF),
            pltpu.VMEM((HD, SEQLEN), BF),
            pltpu.VMEM((8, 5, KT, QT), F32),
            pltpu.VMEM((8, 5, KT, QT), BF),
            pltpu.VMEM((8, 1, QT), F32),
            pltpu.VMEM((8, 1, QT), F32),
            pltpu.VMEM((SEQLEN, HD), BF),
            pltpu.VMEM((SEQLEN, HD), BF),
            pltpu.VMEM((2, SEQLEN, HD), BF),
            pltpu.VMEM((SEQLEN, HD), BF),
            pltpu.VMEM((SEQLEN, HD), BF),
            pltpu.VMEM((4, 2 * CTOK, HD), BF),
            pltpu.VMEM((4, 2 * CTOK, HD), BF),
            pltpu.VMEM((CTOK, HALF), BF),
            pltpu.VMEM((CTOK, D), F32),
            pltpu.VMEM((TOK, D), BF),
            pltpu.VMEM((TOK, D), BF),
            pltpu.VMEM((2, 2, 4, 4, ROWS, HD), BF),
            pltpu.VMEM((2, 2, 2, 2, ROWS, HD), BF),
            pltpu.VMEM((2, 2, 2, 4, ROWS, HD), BF),
            pltpu.VMEM((2, 2, 4, ROWS, HD), BF),
            pltpu.VMEM((2, 2, 3, ROWS, HD), BF),
            pltpu.VMEM((4, ROWS, HD), BF),
            pltpu.VMEM((4, ROWS, HD), BF),
            dma((8,)),
            dma((8,)),
            dma((8,)),
            dma((2,)),
            dma(()),
            dma(()),
            dma(()),
            dma((4,)),
            dma((4,)),
            dma((2,)),
            dma((2, 2, 2)),
            dma((2, 2, 2)),
            dma((2, 2, 2)),
            dma((2, 2, 2)),
            dma((2, 2, 3)),
            dma((2, 2, 3)),
            dma((4,)),
            dma(()),
        ],
        compiler_params=pltpu.CompilerParams(
            collective_id=0, has_side_effects=True, vmem_limit_bytes=50 << 20
        ),
        name="layer",
    )(lengths, x, q, w, g, cosine, sine)


def tables(lengths):
    pair = lax.axis_index("seq") // 4
    places = pair * (2 * CTOK) + jnp.arange(2 * CTOK, dtype=jnp.int32)
    order = jnp.arange(NDOC)
    doc_ends = jnp.sum(jnp.where(order[:, None] <= order[None, :], lengths[:, None], 0), axis=0)
    ended = doc_ends[None, :] <= places[:, None]
    within = places - jnp.sum(jnp.where(ended, lengths[None, :], 0), axis=1)
    exponent = jnp.arange(HD // 2, dtype=F32) * (2.0 / HD)
    rate = jnp.power(ROPE_BASE, -exponent)
    angles = within.astype(F32)[:, None] * rate[None, :]
    cosine, sine = jnp.cos(angles), jnp.sin(angles)
    return (
        jnp.concatenate([cosine, cosine], axis=1),
        jnp.concatenate([-sine, sine], axis=1),
    )


def on_device(inputs, queries, w_kv, doc_lengths, grad_out):
    cosine, sine = tables(doc_lengths[0])
    held = [
        pltpu.with_memory_space_constraint(a, pltpu.HBM)
        for a in (inputs[0], queries[0], w_kv, grad_out[0])
    ]
    out, gin, gw = layer(doc_lengths[0], *held, cosine, sine)
    return out[None], gin[None], gw


def solution(mesh):
    in_specs = (
        P("fsdp", "seq", None),
        P("fsdp", "seq", None),
        P("fsdp", None),
        P("fsdp", None),
        P("fsdp", "seq", None),
    )
    out_specs = (P("fsdp", "seq", None), P("fsdp", "seq", None), P("fsdp", "seq"))
    return jax.shard_map(
        on_device, mesh=mesh, in_specs=in_specs, out_specs=out_specs, check_vma=False
    )
```

```python
import functools

import jax
import jax.numpy as jnp
from jax import lax
from jax.experimental import pallas as pl
from jax.experimental.pallas import tpu as pltpu
from jax.sharding import PartitionSpec as P

D = 2304
HD = 128
WIN = 1024
SEQLEN = 2048
NDOC = 8
NZ = 8
NX = 4
NY = 4
ROWS = D // (NX * NY)
HALF = 1024
PART = 512
TOK = 128
CTOK = 256
CAP = 50.0
SCALE = 1.0 / 12.0
ROPE_BASE = 10000.0
MESH = pl.DeviceIdType.MESH
HBM = pl.BlockSpec(memory_space=pltpu.HBM)
VM = pl.BlockSpec(memory_space=pltpu.VMEM)
BF = jnp.bfloat16
F32 = jnp.float32


def where_am_i():
    s = lax.axis_index("seq")
    f = lax.axis_index("fsdp")
    z = s // 2
    c = s - 2 * z
    x = f // NY
    y = f - NY * x
    return s, f, z, c, x, y


def ring(v, n):
    return lax.rem(v + n, n)


def remote(src, dst, send, recv, s, f):
    return pltpu.make_async_remote_copy(
        src_ref=src,
        dst_ref=dst,
        send_sem=send,
        recv_sem=recv,
        device_id={"seq": s, "fsdp": f},
        device_id_type=MESH,
    )


def enter(s, f, x, y):
    barrier = pltpu.get_barrier_semaphore()
    for step in range(1, 2 * NZ):
        pl.semaphore_signal(
            barrier,
            inc=1,
            device_id={"seq": ring(s + step, 2 * NZ), "fsdp": f},
            device_id_type=MESH,
        )
    for dx, dy in ((1, 0), (-1, 0), (0, 1), (0, -1)):
        pl.semaphore_signal(
            barrier,
            inc=1,
            device_id={"seq": s, "fsdp": ring(x + dx, NX) * NY + ring(y + dy, NY)},
            device_id_type=MESH,
        )
    pl.semaphore_wait(barrier, 2 * NZ - 1 + 4)


def other_chip(s, z):
    return s + 2 - 4 * lax.rem(z, 2)


def rotated(values, cosine, sine):
    return values * cosine + pltpu.roll(values, HD // 2, 1) * sine


def project_part(
    x_ref,
    q_ref,
    w_ref,
    g_ref,
    cos_ref,
    sin_ref,
    qh_ref,
    gh_ref,
    kv_ref,
    xt,
    xp,
    wg,
    xs,
    xo,
    proj,
    wl_sem,
    xl_sem,
    xr_sem,
    xc_sem,
    ws_sem,
    wr_sem,
    ql_sem,
    qs_sem,
    qr_sem,
    ks_sem,
    kr_sem,
    fs_sem,
    fr_sem,
):
    s, f, z, c, x, y = where_am_i()
    sib = s + 1 - 2 * c
    own_rows = pl.ds(pl.multiple_of(f * ROWS, 16), ROWS)
    load_w = []
    for k in range(8):
        cols = pl.ds(pl.multiple_of((2 * k + c) * HD, HD), HD)
        load_w.append(
            pltpu.make_async_copy(
                w_ref.at[:, cols], wg.at[own_rows, pl.ds(k * HD, HD)], wl_sem.at[k]
            )
        )
    for copy in load_w:
        copy.start()
    own_tok = pl.ds(pl.multiple_of(c * TOK, TOK), TOK)
    load_x = pltpu.make_async_copy(x_ref, xs.at[own_tok], xl_sem)
    load_x.start()
    enter(s, f, x, y)

    wide = PART // 2

    def piece(phase, part, off, half):
        origin = ring(x + off[0], NX) * NY + ring(y + off[1], NY)
        rows = pl.ds(pl.multiple_of(origin * ROWS, 16), ROWS)
        base = phase * PART + part * wide
        if half is None:
            return wg.at[rows, pl.ds(base, wide)]
        return wg.at[rows, pl.ds(base + half * (wide // 2), wide // 2)]

    sends = []

    def pass_on(phase, part, off, step, half=None):
        there = tuple((o - d) % 4 for o, d in zip(off, step))
        there = tuple(-1 if t == 3 else t for t in there)
        ref = piece(phase, part, off, half)
        copy = remote(
            ref,
            ref,
            ws_sem.at[len(sends)],
            wr_sem.at[phase, part, there[0] + 1, there[1] + 1, half or 0],
            s,
            ring(x + step[0], NX) * NY + ring(y + step[1], NY),
        )
        copy.start()
        sends.append(copy)

    def arrived(phase, part, off, half=None):
        ref = piece(phase, part, off, half)
        sem = wr_sem.at[phase, part, off[0] + 1, off[1] + 1, half or 0]
        pltpu.make_async_copy(ref, ref, sem).wait()

    def at(part, a, b):
        return (a, b) if part == 0 else (b, a)

    def begin(p):
        for d in (1, -1):
            for part in range(2):
                pass_on(p, part, (0, 0), at(part, d, 0))
        for d in (1, -1):
            for part in range(2):
                pass_on(p, part, (0, 0), at(part, 0, d))

    def near_first(p):
        for d in (-1, 1):
            for part in range(2):
                arrived(p, part, at(part, d, 0))
                pass_on(p, part, at(part, d, 0), at(part, -d, 0), 0 if d < 0 else 1)
                for e in (1, -1):
                    pass_on(p, part, at(part, d, 0), at(part, 0, e))

    def near_second(p):
        for d in (-1, 1):
            for part in range(2):
                arrived(p, part, at(part, 0, d))
                pass_on(p, part, at(part, 0, d), at(part, 0, -d), 0 if d < 0 else 1)

    def far_first(p):
        for part in range(2):
            arrived(p, part, at(part, 2, 0), 0)
            arrived(p, part, at(part, 2, 0), 1)
            for e in (1, -1):
                pass_on(p, part, at(part, 2, 0), at(part, 0, e))

    def rest_second(p):
        for a in (-1, 1, 2):
            for d in (-1, 1):
                for part in range(2):
                    arrived(p, part, at(part, a, d))
                    pass_on(p, part, at(part, a, d), at(part, 0, -d), 0 if d < 0 else 1)

    def finish(p):
        for a in (0, -1, 1, 2):
            for part in range(2):
                arrived(p, part, at(part, a, 2), 0)
                arrived(p, part, at(part, a, 2), 1)

    def kv_copy(k):
        kind = k // 4
        to = 2 * (2 * (k % 4) + c) + z // 4
        rows = pl.ds(pl.multiple_of(z * CTOK, CTOK), CTOK)
        local = pltpu.make_async_copy(proj.at[k], kv_ref.at[kind, rows], kr_sem.at[kind])
        away = remote(proj.at[k], kv_ref.at[kind, rows], ks_sem.at[k], kr_sem.at[kind], to, f)
        return to == s, local, away

    in_pair = pl.ds(pl.multiple_of(lax.rem(z, 2) * CTOK, CTOK), CTOK)

    def project(p):
        for t in (2 * p, 2 * p + 1):
            res = jnp.dot(xs[...], wg[:, t * 256 : (t + 1) * 256], preferred_element_type=F32)
            for j in range(2):
                k = 2 * t + j
                block = res[:, j * HD : (j + 1) * HD]
                if k < 4:
                    block = rotated(block, cos_ref[in_pair, :], sin_ref[in_pair, :])
                proj[k] = block.astype(BF)
                mine, local, away = kv_copy(k)

                @pl.when(mine)
                def _():
                    local.start()

                @pl.when(jnp.logical_not(mine))
                def _():
                    away.start()

    shares = []

    def share(p):
        half = kv_ref.at[p, pl.ds(pl.multiple_of(c * (SEQLEN // 2), SEQLEN // 2), SEQLEN // 2)]
        pltpu.make_async_copy(half, half, kr_sem.at[p]).wait()
        copy = remote(half, half, fs_sem.at[p], fr_sem.at[p], sib, f)
        copy.start()
        shares.append(copy)

    for copy in load_w:
        copy.wait()
    begin(0)
    load_x.wait()
    give_x = remote(xs.at[own_tok], xs.at[own_tok], xr_sem.at[0], xr_sem.at[1], sib, f)
    give_x.start()

    own_seq = pl.ds(pl.multiple_of(s * TOK, TOK), TOK)
    own_head = pl.ds(pl.multiple_of(s * HD, HD), HD)

    def deal(i, src, dst):
        pltpu.make_async_copy(src.at[:, own_head], dst.at[own_seq], ql_sem.at[i]).start()
        for step in range(1, 2 * NZ):
            to = ring(s + step, 2 * NZ)
            head = pl.ds(pl.multiple_of(to * HD, HD), HD)
            remote(src.at[:, head], dst.at[own_seq], qs_sem.at[i], qr_sem.at[i], to, f).start()

    def dealt(i, src, dst):
        pltpu.make_async_copy(src.at[:, own_head], dst.at[own_seq], ql_sem.at[i]).wait()
        others = dst.at[pl.ds(0, SEQLEN - TOK)]
        pltpu.make_async_copy(others, others, qs_sem.at[i]).wait()
        pltpu.make_async_copy(others, others, qr_sem.at[i]).wait()

    deal(0, q_ref, qh_ref)
    deal(1, g_ref, gh_ref)

    near_first(0)
    begin(1)
    near_second(0)
    far_first(0)
    near_first(1)
    rest_second(0)
    near_second(1)
    far_first(1)
    finish(0)
    give_x.wait_recv()
    project(0)
    rest_second(1)
    finish(1)
    project(1)
    cross = remote(
        xs.at[own_tok], xo.at[own_tok], xc_sem.at[0], xc_sem.at[1], other_chip(s, z), f
    )
    cross.start()
    share(0)
    def turn(i, carry):
        cols = pl.ds(pl.multiple_of(i * 256, 256), 256)
        xt[cols, :] = xs[:, cols].T
        return carry

    def turn_other(i, carry):
        cols = pl.ds(pl.multiple_of(i * 256, 256), 256)
        xp[cols, :] = xo[:, cols].T
        return carry

    lax.fori_loop(0, D // 256, turn, 0)
    for copy in sends:
        copy.wait_send()
    give_x.wait_send()
    dealt(0, q_ref, qh_ref)
    share(1)
    for k in range(8):
        mine, _, away = kv_copy(k)

        @pl.when(jnp.logical_not(mine))
        def _():
            away.wait_send()

    for copy in shares:
        copy.wait()
    spread = remote(xo.at[own_tok], xo.at[own_tok], xc_sem.at[2], xc_sem.at[3], sib, f)

    def pass_tokens():
        cross.wait_recv()
        spread.start()

    def take_tokens():
        spread.wait()
        lax.fori_loop(0, D // 256, turn_other, 0)
        cross.wait_send()

    return lambda: dealt(1, g_ref, gh_ref), pass_tokens, take_tokens


QT = 256
KT = 256
NT = (((1,), (1,)), ((), ()))
LOG2E = 1.4426950408889634


def gradient_part(
    waits,
    len_ref,
    q_ref,
    g_ref,
    kv_ref,
    xt,
    xp,
    wv,
    cos_ref,
    sin_ref,
    out_ref,
    gin_ref,
    gw_ref,
    vt,
    ot,
    wbuf,
    tbuf,
    inv,
    delt,
    gs,
    obuf,
    dkv,
    theirs,
    total,
    got,
    dd,
    da,
    gi,
    gsend,
    grecv,
    part_sum,
    r1,
    r2,
    second,
    r3,
    third,
    zr,
    ws_sem,
    wr_sem,
    ds_sem,
    dr_sem,
    ol_sem,
    os_sem,
    or_sem,
    as_sem,
    ar_sem,
    g_sem,
    s1_sem,
    r1_sem,
    s2_sem,
    r2_sem,
    s3_sem,
    r3_sem,
    zs_sem,
    zr_sem,
):
    s, f, z, c, x, y = where_am_i()
    sib = s + 1 - 2 * c
    e = lax.rem(z, 2)
    pair = z // 2
    partner = other_chip(s, z)
    def landed(ref, sem):
        pltpu.make_async_copy(ref, ref, sem).wait()

    ends = []
    so_far = 0
    for i in range(NDOC):
        so_far = so_far + len_ref[i]
        ends.append(so_far)

    def flip(i, carry):
        rows = pl.ds(pl.multiple_of(i * KT, KT), KT)
        vt[:, rows] = kv_ref[1, rows, :].T
        return carry

    lax.fori_loop(0, SEQLEN // KT, flip, 0)

    def tile_rows(i):
        return pl.ds(pl.multiple_of(i * KT, KT), KT)

    def swap(i):
        rows = tile_rows(i)
        return remote(
            dkv.at[1 - c, rows], theirs.at[rows], ws_sem.at[i], wr_sem.at[i], sib, f
        )

    def forward(i, n):
        base = i * QT
        rows = tile_rows(i)
        pos = base + lax.broadcasted_iota(jnp.int32, (1, QT), 1)
        start = jnp.zeros((1, QT), jnp.int32)
        for end in ends:
            start = jnp.where(pos >= end, end, start)
        low = jnp.maximum(start, pos - (WIN - 1))
        first = i + 1 - n
        qt = q_ref[rows, :]
        acc = jnp.zeros((HD, QT), F32)
        norm = jnp.zeros((1, QT), F32)
        key = lax.broadcasted_iota(jnp.int32, (KT, QT), 0)
        for j in range(n):
            span = tile_rows(first + j)
            st = lax.dot_general(kv_ref[0, span, :], qt, NT, preferred_element_type=F32)
            squashed = jnp.tanh(st * (SCALE / CAP))
            allowed = key >= low - (first + j) * KT
            if j == n - 1:
                allowed = allowed & (key <= pos - (first + j) * KT)
            weight = jnp.where(allowed, jnp.exp2((CAP * LOG2E) * squashed), 0.0)
            short = weight.astype(BF)
            norm = norm + jnp.sum(weight, axis=0, keepdims=True)
            wbuf[first + j, n - 1 - j] = weight * (1.0 - squashed * squashed)
            tbuf[first + j, n - 1 - j] = short
            acc = acc + jnp.dot(vt[:, span], short, preferred_element_type=F32)
        inverse = 1.0 / norm
        out_t = (acc * inverse).astype(BF)
        obuf[rows, :] = out_t.T
        inv[i] = inverse
        ot[:, rows] = out_t

    def prepare(i, carry):
        rows = tile_rows(i)
        gt_t = g_ref[rows, :].astype(F32).T
        delt[i] = jnp.sum(gt_t * ot[:, rows].astype(F32), axis=0, keepdims=True)
        gs[rows, :] = (gt_t * inv[i]).T.astype(BF)
        return carry

    def backward(t, n):
        span = tile_rows(t)
        dk = jnp.zeros((KT, HD), F32)
        dv = jnp.zeros((KT, HD), F32)
        for j in range(n):
            rows = tile_rows(t + j)
            dprob = lax.dot_general(
                kv_ref[1, span, :], g_ref[rows, :], NT, preferred_element_type=F32
            )
            dscore = (wbuf[t, j] * inv[t + j] * (dprob - delt[t + j])).astype(BF)
            dk = dk + jnp.dot(dscore, q_ref[rows, :], preferred_element_type=F32)
            dv = dv + jnp.dot(tbuf[t, j], gs[rows, :], preferred_element_type=F32)
        dkv[0, span, :] = (dk * SCALE).astype(BF)
        dkv[1, span, :] = dv.astype(BF)

    head_dev = lax.rem(z, 4)

    def d_copy(i):
        rows = tile_rows(i)
        to = 4 * (i // 2) + head_dev
        dst = got.at[2 * c + z // 4, pl.ds(pl.multiple_of(lax.rem(i, 2) * CTOK, CTOK), CTOK)]
        local = pltpu.make_async_copy(total.at[rows], dst, dr_sem.at[c])
        away = remote(total.at[rows], dst, ds_sem.at[i], dr_sem.at[c], to, f)
        return to == s, local, away

    def hand_over(i):
        rows = tile_rows(i)
        landed(theirs.at[rows], wr_sem.at[i])
        total[rows, :] = (dkv[c, rows, :].astype(F32) + theirs[rows, :].astype(F32)).astype(BF)
        mine, local, away = d_copy(i)

        @pl.when(mine)
        def _():
            local.start()

        @pl.when(jnp.logical_not(mine))
        def _():
            away.start()

    def long_tile(k, carry):
        forward(k + 4, 5)
        return carry

    for i in range(4):
        forward(jnp.int32(i), i + 1)
    lax.fori_loop(0, 4, long_tile, 0)

    wait_g, pass_tokens, take_tokens = waits
    wait_g()
    lax.fori_loop(0, SEQLEN // QT, prepare, 0)

    tiles = SEQLEN // KT

    def key_tile(k, carry):
        t = ring(z + k, tiles)
        count = jnp.minimum(tiles - t, 5)
        for n in range(1, 6):

            @pl.when(count == n)
            def _():
                backward(t, n)

        swap(t).start()

        @pl.when(k > 0)
        def _():
            hand_over(ring(t - 1, tiles))

        return carry

    lax.fori_loop(0, tiles, key_tile, 0)
    hand_over(ring(z - 1, tiles))
    pass_tokens()

    own_tok = pl.ds(pl.multiple_of(e * CTOK, CTOK), CTOK)
    pair_tok = pl.ds(pl.multiple_of((1 - e) * CTOK, CTOK), CTOK)

    def a_cols(b, side):
        return pl.ds(pl.multiple_of((side + 2 * b) * HD, HD), HD)

    def a_copy(b):
        return remote(
            dd.at[b, pair_tok], da.at[:, a_cols(b, e)], as_sem.at[b], ar_sem.at[b], partner, f
        )

    def take_in(kind):
        blocks = got.at[pl.ds(2 * kind, 2)]
        landed(blocks, dr_sem.at[kind])
        for b in range(2 * kind, 2 * kind + 2):
            block = got[b]
            if kind == 0:
                block = rotated(block.astype(F32), cos_ref[...], -sin_ref[...]).astype(BF)
            dd[b] = block

    def trade(kind):
        for b in range(2 * kind, 2 * kind + 2):
            a_copy(b).start()
            da[:, a_cols(b, e)] = dd[b, own_tok, :]

    def chunk(p, part, a):
        for j in range(4):
            cx, cy = (a, j) if part == 0 else (j, a)
            rows = pl.ds(pl.multiple_of((cx * NY + cy) * ROWS, 16), ROWS)
            part_sum[p, part, cx, cy] = (
                jnp.dot(xt[rows, :], dd[2 * p + part, own_tok, :], preferred_element_type=F32)
                + jnp.dot(xp[rows, :], dd[2 * p + part, pair_tok, :], preferred_element_type=F32)
            ).astype(BF)

    def chunk_ref(p, part, a, which):
        if part == 0:
            return part_sum.at[p, part, a, which]
        return part_sum.at[p, part, which, a]

    first_axis = (x, y)
    second_axis = (y, x)

    def neighbour(part, level, d):
        if (part == 0) == (level == 0):
            return ring(x + d, NX) * NY + y
        return x * NY + ring(y + d, NY)

    halves = (pl.ds(0, 2), pl.ds(2, 2))
    full = pl.ds(0, 4)
    dirs = (1, -1)
    sent = []

    def go(src, dst, send, recv, to_f):
        copy = remote(src, dst, send, recv, s, to_f)
        copy.start()
        sent.append(copy)

    def far(p):
        for part in range(2):
            a = ring(first_axis[part] + 2, 4)
            chunk(p, part, a)
            for h, d in enumerate(dirs):
                go(
                    chunk_ref(p, part, a, halves[h]),
                    r1.at[p, part, h],
                    s1_sem.at[p, part, h],
                    r1_sem.at[p, part, h],
                    neighbour(part, 0, d),
                )

    def near(p):
        for part in range(2):
            for d in (1, -1, 0):
                chunk(p, part, ring(first_axis[part] + d, 4))

    def hop(p):
        for h, d in enumerate(dirs):
            for part in range(2):
                a = ring(first_axis[part] + d, 4)
                landed(r1.at[p, part, h], r1_sem.at[p, part, h])
                for k in range(2):
                    j = 2 * h + k
                    idx = (p, part, a, j) if part == 0 else (p, part, j, a)
                    part_sum[idx] = (
                        part_sum[idx].astype(F32) + r1[p, part, h, k].astype(F32)
                    ).astype(BF)
                go(
                    chunk_ref(p, part, a, full),
                    r2.at[p, part, h],
                    s2_sem.at[p, part, h],
                    r2_sem.at[p, part, h],
                    neighbour(part, 0, d),
                )

    def across(p):
        for part in range(2):
            for h in range(2):
                landed(r2.at[p, part, h], r2_sem.at[p, part, h])
            for j in range(4):
                idx = (p, part, x, j) if part == 0 else (p, part, j, y)
                second[p, part, j] = (
                    part_sum[idx].astype(F32)
                    + r2[p, part, 0, j].astype(F32)
                    + r2[p, part, 1, j].astype(F32)
                ).astype(BF)
            for i, d in enumerate((2, 1, -1)):
                go(
                    second.at[p, part, ring(second_axis[part] + d, 4)],
                    r3.at[p, part, i],
                    s3_sem.at[p, part, i],
                    r3_sem.at[p, part, i],
                    neighbour(part, 1, d),
                )

    def z_copy(b):
        to = 2 * (2 * b + e) + c
        return pair != b, remote(third.at[b], zr.at[pair], zs_sem.at[b], zr_sem, to, f)

    def along(p):
        for part in range(2):
            b = 2 * p + part
            acc = second[p, part, second_axis[part]].astype(F32)
            for i in range(3):
                landed(r3.at[p, part, i], r3_sem.at[p, part, i])
                acc = acc + r3[p, part, i].astype(F32)
            third[b] = acc.astype(BF)
            away, copy = z_copy(b)

            @pl.when(away)
            def _():
                copy.start()

    take_in(0)
    trade(0)
    take_in(1)
    trade(1)
    take_tokens()
    far(0)
    far(1)
    near(0)
    own_head = pl.ds(pl.multiple_of(s * HD, HD), HD)
    own_seq = pl.ds(pl.multiple_of(s * TOK, TOK), TOK)
    keep_o = pltpu.make_async_copy(obuf.at[own_seq], out_ref.at[:, own_head], ol_sem)
    keep_o.start()
    for step in range(1, 2 * NZ):
        to = ring(s + step, 2 * NZ)
        theirs_tok = pl.ds(pl.multiple_of(to * TOK, TOK), TOK)
        remote(
            obuf.at[theirs_tok], out_ref.at[:, own_head], os_sem, or_sem, to, f
        ).start()
    hop(0)
    near(1)
    hop(1)
    across(0)

    for b in range(4):
        landed(da.at[:, a_cols(b, 1 - e)], ar_sem.at[b])

    def input_tile(i, carry):
        rows = pl.ds(pl.multiple_of(i * 256, 256), 256)
        gi[:, rows] = lax.dot_general(da[...], wv[rows, :], NT, preferred_element_type=F32)
        return carry

    lax.fori_loop(0, D // 256, input_tile, 0)
    mine_tok = pl.ds(pl.multiple_of(c * TOK, TOK), TOK)
    sib_tok = pl.ds(pl.multiple_of((1 - c) * TOK, TOK), TOK)
    gsend[...] = gi[sib_tok, :].astype(BF)
    give = remote(gsend, grecv, g_sem.at[0], g_sem.at[1], sib, f)
    give.start()
    along(0)
    across(1)
    give.wait()
    gin_ref[...] = (gi[mine_tok, :] + grecv[...].astype(F32)).astype(BF)
    along(1)
    for copy in sent:
        copy.wait_send()
    for b in range(4):
        a_copy(b).wait_send()

    def settle(i, carry):
        swap(i).wait_send()
        mine, _, away = d_copy(i)

        @pl.when(jnp.logical_not(mine))
        def _():
            away.wait_send()

        return carry

    lax.fori_loop(0, SEQLEN // QT, settle, 0)
    keep_o.wait()
    others = obuf.at[pl.ds(0, SEQLEN - TOK)]
    landed(others, os_sem)
    landed(others, or_sem)
    for b in range(4):
        away, copy = z_copy(b)

        @pl.when(away)
        def _():
            copy.wait_send()

    rest = zr.at[pl.ds(1, 3)]
    landed(rest, zr_sem)
    acc = third[pair].astype(F32)
    for step in range(1, 4):
        acc = acc + zr[ring(pair + step, 4)].astype(F32)
    gw_ref[...] = acc


def whole_kernel(
    len_ref, x_ref, q_ref, w_ref, g_ref, cos_ref, sin_ref, out_ref, gin_ref, gw_ref, *scratch
):
    qh, gh, kv, xt, xp, wg = scratch[:6]
    first, second = scratch[:PROJECT_SCRATCH], scratch[PROJECT_SCRATCH:]
    waits = project_part(x_ref, q_ref, w_ref, g_ref, cos_ref, sin_ref, *first)
    gradient_part(
        waits, len_ref, qh, gh, kv, xt, xp, wg, cos_ref, sin_ref, out_ref, gin_ref, gw_ref, *second
    )


PROJECT_SCRATCH = 22


def layer(lengths, x, q, w, g, cosine, sine):
    dma = pltpu.SemaphoreType.DMA
    return pl.pallas_call(
        whole_kernel,
        out_shape=(
            jax.ShapeDtypeStruct((TOK, 2048), BF),
            jax.ShapeDtypeStruct((TOK, D), BF),
            jax.ShapeDtypeStruct((ROWS, HD), F32),
        ),
        in_specs=[pl.BlockSpec(memory_space=pltpu.SMEM), HBM, HBM, HBM, HBM, VM, VM],
        out_specs=(VM, VM, VM),
        scratch_shapes=[
            pltpu.VMEM((SEQLEN, HD), BF),
            pltpu.VMEM((SEQLEN, HD), BF),
            pltpu.VMEM((2, SEQLEN, HD), BF),
            pltpu.VMEM((D, CTOK), BF),
            pltpu.VMEM((D, CTOK), BF),
            pltpu.VMEM((D, HALF), BF),
            pltpu.VMEM((CTOK, D), BF),
            pltpu.VMEM((CTOK, D), BF),
            pltpu.VMEM((8, CTOK, HD), BF),
            dma((8,)),
            dma(()),
            dma((2,)),
            dma((4,)),
            dma((80,)),
            dma((2, 2, 4, 4, 2)),
            dma((2,)),
            dma((2,)),
            dma((2,)),
            dma((8,)),
            dma((2,)),
            dma((2,)),
            dma((2,)),
            pltpu.VMEM((HD, SEQLEN), BF),
            pltpu.VMEM((HD, SEQLEN), BF),
            pltpu.VMEM((8, 5, KT, QT), F32),
            pltpu.VMEM((8, 5, KT, QT), BF),
            pltpu.VMEM((8, 1, QT), F32),
            pltpu.VMEM((8, 1, QT), F32),
            pltpu.VMEM((SEQLEN, HD), BF),
            pltpu.VMEM((SEQLEN, HD), BF),
            pltpu.VMEM((2, SEQLEN, HD), BF),
            pltpu.VMEM((SEQLEN, HD), BF),
            pltpu.VMEM((SEQLEN, HD), BF),
            pltpu.VMEM((4, 2 * CTOK, HD), BF),
            pltpu.VMEM((4, 2 * CTOK, HD), BF),
            pltpu.VMEM((CTOK, HALF), BF),
            pltpu.VMEM((CTOK, D), F32),
            pltpu.VMEM((TOK, D), BF),
            pltpu.VMEM((TOK, D), BF),
            pltpu.VMEM((2, 2, 4, 4, ROWS, HD), BF),
            pltpu.VMEM((2, 2, 2, 2, ROWS, HD), BF),
            pltpu.VMEM((2, 2, 2, 4, ROWS, HD), BF),
            pltpu.VMEM((2, 2, 4, ROWS, HD), BF),
            pltpu.VMEM((2, 2, 3, ROWS, HD), BF),
            pltpu.VMEM((4, ROWS, HD), BF),
            pltpu.VMEM((4, ROWS, HD), BF),
            dma((8,)),
            dma((8,)),
            dma((8,)),
            dma((2,)),
            dma(()),
            dma(()),
            dma(()),
            dma((4,)),
            dma((4,)),
            dma((2,)),
            dma((2, 2, 2)),
            dma((2, 2, 2)),
            dma((2, 2, 2)),
            dma((2, 2, 2)),
            dma((2, 2, 3)),
            dma((2, 2, 3)),
            dma((4,)),
            dma(()),
        ],
        compiler_params=pltpu.CompilerParams(
            collective_id=0, has_side_effects=True, vmem_limit_bytes=50 << 20
        ),
        name="layer",
    )(lengths, x, q, w, g, cosine, sine)


def tables(lengths):
    pair = lax.axis_index("seq") // 4
    places = pair * (2 * CTOK) + jnp.arange(2 * CTOK, dtype=jnp.int32)
    order = jnp.arange(NDOC)
    doc_ends = jnp.sum(jnp.where(order[:, None] <= order[None, :], lengths[:, None], 0), axis=0)
    ended = doc_ends[None, :] <= places[:, None]
    within = places - jnp.sum(jnp.where(ended, lengths[None, :], 0), axis=1)
    exponent = jnp.arange(HD // 2, dtype=F32) * (2.0 / HD)
    rate = jnp.power(ROPE_BASE, -exponent)
    angles = within.astype(F32)[:, None] * rate[None, :]
    cosine, sine = jnp.cos(angles), jnp.sin(angles)
    return (
        jnp.concatenate([cosine, cosine], axis=1),
        jnp.concatenate([-sine, sine], axis=1),
    )


def on_device(inputs, queries, w_kv, doc_lengths, grad_out):
    cosine, sine = tables(doc_lengths[0])
    held = [
        pltpu.with_memory_space_constraint(a, pltpu.HBM)
        for a in (inputs[0], queries[0], w_kv, grad_out[0])
    ]
    out, gin, gw = layer(doc_lengths[0], *held, cosine, sine)
    return out[None], gin[None], gw


def solution(mesh):
    in_specs = (
        P("fsdp", "seq", None),
        P("fsdp", "seq", None),
        P("fsdp", None),
        P("fsdp", None),
        P("fsdp", "seq", None),
    )
    out_specs = (P("fsdp", "seq", None), P("fsdp", "seq", None), P("fsdp", "seq"))
    return jax.shard_map(
        on_device, mesh=mesh, in_specs=in_specs, out_specs=out_specs, check_vma=False
    )
```
